32 devices in a mesh: grp: 4 (over y, x), tile: 8 (over z, core).
Axes of the slice: x: 2, y: 2, z: 4, core: 2. Of those that a mesh axis runs over, the one named last changes fastest.
Arguments:
- flow_fields: float32 [5, 256, 16, 128], P(None, 'tile', 'grp'), may hold values from -6 to 6
- turbulent_diffusivity: float32 [256, 16, 128], P('tile', 'grp'), may hold values from 0.05 to 0.3
- holder_unit: int32 [4, 256, 1], P('grp', 'tile'), may hold values from 0 to 7, as said below
- spray_volume_position: int32 [8, 1024, 128], P('tile'), may hold values from 0 to 511
- patch_pick_unreduced: int32 [8, 1024], P('tile'), may hold values from 0 to 1048575
- droplet_motion: float32 [8, 1024, 3, 128], P('tile'), may hold values from -6 to 6
- droplet_warmth: float32 [8, 1024, 128], P('tile'), may hold values from -6 to 6
- droplet_weightiness: float32 [8, 1024, 128], P('tile'), may hold values from 0.25 to 2
- droplet_multiplicity: float32 [8, 1024, 128], P('tile'), may hold values from 0.5 to 2
- living_spray_batches: int32 [8], P('tile'), may hold values from 1 to 1024, 4096 in all
Outputs:
- gas_next: float32 [5, 256, 16, 128], P(None, 'tile', 'grp')
The draws below stay inside these ranges and needn't reach their ends.
Inputs may be any that keep to these rules, and one draw needn't show every extreme that they name: `holder_unit`: among the 32 tiles of one gas device (aligned blocks of 32 rows of owner, in order of its first two dimensions) no parcel device owns more than 8, and in every such block one parcel device owns exactly 8. Two parcel devices own no tile at all. Rows with g = 3 are not used. `living_spray_batches`: live blocks of a device are its first ones; the busiest parcel device has exactly 1024, and they sum to 4096.
All inputs are finite; a program needn't handle non-finite values.
Results may differ from the reference program's by a relative error of at most 0.0045.
Values may be sent and summed in bfloat16 or wider, within the bound.
A program may use at most 64 MiB of HBM per device.

```python
import math
import jax
import jax.numpy as jnp
import numpy as np

NF = 5
GROUP_DROPLETS = 128
BY = 4
BZ = 128
BX = 32
UNIT_BATCHES = 1024
SPRAY_UNITS = 8
NX = 256
NY = 16
GAS_Y = 12
SLOTS = 8
N_GRP = 4


def draw_holder_unit(key, part):
    block_count = NY // BY * (NX // BX)
    spare_count = SPRAY_UNITS - 2
    key_order, key_blocks, key_rows = jax.random.split(jax.random.fold_in(key, 7), 3)
    middle = (1 + jax.random.permutation(key_order, SPRAY_UNITS - 2)).astype(jnp.int32)
    allowed = jnp.concatenate([jnp.array([0, SPRAY_UNITS - 1], dtype=jnp.int32), middle[2:]])
    shuffles = jax.vmap(lambda subkey: jax.random.permutation(subkey, spare_count))(jax.random.split(key_blocks, block_count)).astype(jnp.int32)
    first_block = jnp.arange(block_count, dtype=jnp.int32)[:, None] == 0
    shuffles = jnp.where(first_block, jnp.arange(spare_count, dtype=jnp.int32)[None, :], shuffles)
    places = jnp.arange(BX, dtype=jnp.int32)
    column = jnp.where(places < SLOTS, 0, 1 + (places - SLOTS) % (spare_count - 1)).astype(jnp.int32)
    labels = allowed[jnp.take(shuffles, column, axis=1)]
    row_order = jax.vmap(lambda subkey: jax.random.permutation(subkey, BX))(jax.random.split(key_rows, block_count)).astype(jnp.int32)
    labels = jnp.take_along_axis(labels, row_order, axis=1)
    return labels.reshape(NY // BY, NX, 1).astype(jnp.int32)


def with_ends(entries, rng, low, high):
    index_at = [jax.random.randint(jax.random.fold_in(rng, axis), (), 0, length) for axis, length in enumerate(entries.shape)]
    widest = entries.shape.index(max(entries.shape))
    next_to = index_at[:widest] + [(index_at[widest] + 1) % entries.shape[widest]] + index_at[widest + 1:]
    return entries.at[tuple(index_at)].set(low).at[tuple(next_to)].set(high)


def shard_levels(rng, dims, cuts, least, high):
    loudness = 1.0
    for dim, shards_of in cuts:
        draws = jax.random.uniform(jax.random.fold_in(jax.random.fold_in(rng, 6), dim), (shards_of,), jnp.float32, least / len(cuts), high / len(cuts))
        loudness = loudness * jnp.repeat(jnp.exp(draws), dims[dim] // shards_of).reshape((-1,) + (1,) * (len(dims) - 1 - dim))
    return loudness


def split_up(amount, total, limit, skew):
    weights = [(1 << 20) // math.isqrt(rank ** skew) + 1 for rank in range(2, amount + 1)]
    rest, given = total - limit - (amount - 1), [1] * (amount - 1)
    while rest > 0:
        free = [i for i in range(amount - 1) if given[i] < limit]
        mass, budget = sum([weights[i] for i in free]), rest
        for i in free:
            extra = min(limit - given[i], max(1, budget * weights[i] // mass), rest)
            given[i] = given[i] + extra
            rest = rest - extra
    return np.array([limit] + given)


def uneven(stream_key, count, total, reach, skew):
    if count == 2:
        one = jax.random.randint(stream_key, (), max(1, total - reach), min(reach, total - 1) + 1)
        return jnp.stack([one, total - one])
    tallies = jnp.asarray(split_up(count, total, reach, skew), jnp.int32)
    twos = (count - 1) // 2
    source_of, receiver = tallies[1:1 + 2 * twos:2], tallies[2:2 + 2 * twos:2]
    margin = jnp.minimum(source_of - 1, reach - receiver)
    passed = jax.random.randint(jax.random.fold_in(stream_key, 1), (twos,), 0, 1 << 20) % (margin + 1)
    tallies = tallies.at[1:1 + 2 * twos:2].set(source_of - passed).at[2:2 + 2 * twos:2].set(receiver + passed)
    return tallies[jax.random.permutation(jax.random.fold_in(stream_key, 2), count)]


def scatter_about(key, shape, scale, bound, pieces=(), kind=jnp.bfloat16):
    level = shard_levels(key, shape, pieces, -0.22, 0.18) if pieces else 1.0
    drawn = jax.random.normal(key, shape, jnp.float32) * scale * level
    return jnp.minimum(jnp.maximum(drawn, -bound), bound).astype(kind)


def setup_inputs(seed: int = 0) -> dict:
    keys = jax.random.split(jax.random.key(seed), 11)
    flow_fields = scatter_about(keys[0], (NF, NX, NY, BZ), 1.0, 6.0, ((1, 8), (2, 4)), jnp.float32)
    turbulent_diffusivity = jnp.clip(jnp.exp(math.log(0.3) - 1.7917595 * jax.random.uniform(keys[1], (NX, NY, BZ), jnp.float32) ** shard_levels(keys[1], (NX, NY, BZ), ((0, 8), (1, 4)), -0.2, 0.2)), 0.05, 0.3)
    holder_unit = draw_holder_unit(jax.random.fold_in(keys[10], 71), 0)
    spray_volume_position = with_ends(jax.random.randint(keys[3], (SPRAY_UNITS, UNIT_BATCHES, GROUP_DROPLETS), 0, BY * BZ), jax.random.fold_in(keys[3], 1), 0, (BY * BZ) - 1).astype(jnp.int32)
    patch_pick_unreduced = with_ends(jax.random.randint(keys[4], (SPRAY_UNITS, UNIT_BATCHES), 0, 1048576), jax.random.fold_in(keys[4], 1), 0, 1048575).astype(jnp.int32)
    droplet_motion = scatter_about(keys[5], (SPRAY_UNITS, UNIT_BATCHES, 3, GROUP_DROPLETS), 1.0, 6.0, ((0, 8),), jnp.float32)
    droplet_warmth = scatter_about(keys[6], (SPRAY_UNITS, UNIT_BATCHES, GROUP_DROPLETS), 1.0, 6.0, ((0, 8),), jnp.float32)
    droplet_weightiness = jnp.clip(jnp.exp(math.log(2.0) - 2.0794415 * jax.random.uniform(keys[7], (SPRAY_UNITS, UNIT_BATCHES, GROUP_DROPLETS), jnp.float32) ** shard_levels(keys[7], (SPRAY_UNITS, UNIT_BATCHES, GROUP_DROPLETS), ((0, 8),), -0.2, 0.2)), 0.25, 2.0)
    droplet_multiplicity = jnp.clip(jnp.exp(math.log(2.0) - 1.3862944 * jax.random.uniform(keys[8], (SPRAY_UNITS, UNIT_BATCHES, GROUP_DROPLETS), jnp.float32) ** shard_levels(keys[8], (SPRAY_UNITS, UNIT_BATCHES, GROUP_DROPLETS), ((0, 8),), -0.2, 0.2)), 0.5, 2.0)
    living_spray_batches = uneven(keys[9], SPRAY_UNITS, SPRAY_UNITS * UNIT_BATCHES // 2, UNIT_BATCHES, 2).astype(jnp.int32)
    return dict(flow_fields=flow_fields, turbulent_diffusivity=turbulent_diffusivity, holder_unit=holder_unit, spray_volume_position=spray_volume_position, patch_pick_unreduced=patch_pick_unreduced, droplet_motion=droplet_motion, droplet_warmth=droplet_warmth, droplet_weightiness=droplet_weightiness, droplet_multiplicity=droplet_multiplicity, living_spray_batches=living_spray_batches)


def droplet_coupling_feeds(reached_markers, droplet_motion, droplet_warmth, droplet_weightiness, droplet_multiplicity):
    gas_velocity = reached_markers[..., 0:3, :]
    fluid_warming_share = reached_markers[..., 3, :]
    gas_fuel = reached_markers[..., 4, :]
    relative = gas_velocity - droplet_motion
    speed_sq = jnp.sum(relative * relative, axis=-2)
    surface = droplet_weightiness ** (2.0 / 3.0)
    inverse_tau = 0.8 * (1.0 + 0.15 * (1.0 + speed_sq) ** 0.3435) / surface
    relaxation = 1.0 - jnp.exp(-0.5 * inverse_tau)
    new_velocity = droplet_motion + relaxation[..., None, :] * relative
    heating = 1.0 / (1.0 + jnp.exp(-(fluid_warming_share - gas_fuel)))
    leftover_liquid_load = jnp.exp(-0.3 * heating / surface)
    updated_droplet_load = droplet_weightiness * leftover_liquid_load
    warming_speed = 1.0 - jnp.exp(-0.25 * inverse_tau)
    updated_droplet_warmth = droplet_warmth + warming_speed * (fluid_warming_share - droplet_warmth) - 0.5 * (1.0 - leftover_liquid_load)
    momentum = droplet_weightiness[..., None, :] * droplet_motion - updated_droplet_load[..., None, :] * new_velocity
    enthalpy_content = droplet_weightiness * droplet_warmth - updated_droplet_load * updated_droplet_warmth
    stacked = jnp.concatenate([momentum, enthalpy_content[..., None, :], (droplet_weightiness - updated_droplet_load)[..., None, :]], axis=-2)
    return droplet_multiplicity[..., None, :] * stacked


def reference(flow_fields, turbulent_diffusivity, holder_unit, spray_volume_position, patch_pick_unreduced, droplet_motion, droplet_warmth, droplet_weightiness, droplet_multiplicity, living_spray_batches):
    gas_rows = GAS_Y
    groups = N_GRP - 1
    tile_cells = BY * BZ
    gas_field = flow_fields[:, :, :gas_rows, :]
    nu_field = turbulent_diffusivity[:, :gas_rows, :]
    padded = jnp.pad(gas_field, ((0, 0), (1, 1), (1, 1), (1, 1)))
    beside = padded[:, 2:, 1:-1, 1:-1] + padded[:, :-2, 1:-1, 1:-1]
    beside = beside + padded[:, 1:-1, 2:, 1:-1] + padded[:, 1:-1, :-2, 1:-1]
    beside = beside + padded[:, 1:-1, 1:-1, 2:] + padded[:, 1:-1, 1:-1, :-2]
    laplace = beside - 6.0 * gas_field
    tiles = gas_field.astype(jnp.bfloat16).reshape(NF, NX, groups, BY, BZ)
    tiles = tiles.transpose(2, 1, 0, 3, 4).reshape(groups * NX, NF, tile_cells)
    plane_owner = holder_unit[:groups, :, 0].reshape(groups * NX)
    owned = plane_owner[None, :] == jnp.arange(SPRAY_UNITS, dtype=jnp.int32)[:, None]
    owned_count = jnp.sum(owned.astype(jnp.int32), axis=1)
    listing = jnp.argsort(jnp.where(owned, 0, 1).astype(jnp.int32), axis=1, stable=True).astype(jnp.int32)
    picked = (patch_pick_unreduced % jnp.maximum(owned_count, 1)[:, None]).astype(jnp.int32)
    block_tile = jnp.take_along_axis(listing, picked, axis=1)
    alive = (jnp.arange(UNIT_BATCHES, dtype=jnp.int32)[None, :] < living_spray_batches[:, None]) & (owned_count[:, None] > 0)
    reached_markers = tiles[block_tile[:, :, None], :, spray_volume_position].astype(jnp.float32).transpose(0, 1, 3, 2)
    coupling_feeds = droplet_coupling_feeds(reached_markers, droplet_motion, droplet_warmth, droplet_weightiness, droplet_multiplicity)
    coupling_feeds = coupling_feeds * alive[:, :, None, None].astype(jnp.float32)
    deposit = jnp.zeros((groups * NX, NF, tile_cells), jnp.float32)
    deposit = deposit.at[block_tile[:, :, None], :, spray_volume_position].add(coupling_feeds.transpose(0, 1, 3, 2))
    placed = deposit.reshape(groups, NX, NF, BY, BZ).transpose(2, 1, 0, 3, 4).reshape(NF, NX, gas_rows, BZ)
    advanced = gas_field + 0.5 * nu_field * laplace + placed
    return jnp.concatenate([advanced, jnp.zeros((NF, NX, BY, BZ), jnp.float32)], axis=2)
```

```python
import functools

import jax
import jax.numpy as jnp
from jax import lax
from jax.experimental import pallas as pl
from jax.experimental.pallas import tpu as pltpu
from jax.sharding import PartitionSpec as P

MESH = pl.DeviceIdType.MESH
SLOTS = 8
BATCH = 32
HBM = pl.BlockSpec(memory_space=pltpu.MemorySpace.HBM)
VMEM = pl.BlockSpec(memory_space=pltpu.VMEM)
SMEM = pl.BlockSpec(memory_space=pltpu.SMEM)
F32, BF16, I32 = jnp.float32, jnp.bfloat16, jnp.int32


def signal_all(peers):
    barrier = pltpu.get_barrier_semaphore()
    for peer in peers:
        pl.semaphore_signal(barrier, inc=1, device_id=peer, device_id_type=MESH)
    return lambda: pl.semaphore_wait(barrier, len(peers))


def send_to(src, dst, ss, rs, dev):
    c = pltpu.make_async_remote_copy(
        src_ref=src, dst_ref=dst, send_sem=ss, recv_sem=rs, device_id=dev, device_id_type=MESH
    )
    c.start()
    return c


def start_all(pairs, sems):
    loads = [pltpu.make_async_copy(a, b, sems.at[k]) for k, (a, b) in enumerate(pairs)]
    for c in loads:
        c.start()
    return loads


def block_list(ng, nt, owners, pick, live):
    g, p = lax.axis_index("grp"), lax.axis_index("tile")
    prow = pick.shape[0]
    shift = (prow * 128).bit_length() - 1
    slots = nt * SLOTS
    owned = jnp.where(owners == p, 1, 0)
    counts = jnp.sum(owned, axis=1, keepdims=True)
    which = lax.broadcasted_iota(I32, counts.shape, 0)
    counts = jnp.where(lax.rem(which, ng) < ng - 1, counts, 0)
    total = jnp.maximum(jnp.sum(counts, axis=0, keepdims=True), 1)
    total_f = total.astype(F32)
    quotient = jnp.floor(pick.astype(F32) / total_f).astype(I32)
    left = pick - quotient * total
    left = jnp.where(left < 0, left + total, left)
    left = jnp.where(left >= total, left - total, left)
    group = lax.rem(which, ng)
    low = jnp.sum(jnp.where(group < g, counts, 0), axis=0, keepdims=True)
    mine = jnp.sum(jnp.where(group == g, counts, 0), axis=0, keepdims=True)
    inner = left - low
    slot = inner
    passed = jnp.zeros((1, 1), I32)
    for d in range(nt - 1):
        count = jnp.sum(jnp.where(which == d * ng + g, counts, 0), axis=0, keepdims=True)
        passed = passed + count
        slot = slot + jnp.where(inner >= passed, SLOTS - count, 0)
    row = lax.broadcasted_iota(I32, (prow, 128), 0)
    lane = lax.broadcasted_iota(I32, (prow, 128), 1)
    number = row * 128 + lane
    inside = (inner >= 0) & (inner < mine) & (number < live)
    flags = jnp.where(inside, 1, 0)
    square_a = lax.broadcasted_iota(I32, (128, 128), 0)
    square_b = lax.broadcasted_iota(I32, (128, 128), 1)
    before = jnp.where(square_a < square_b, 1.0, 0.0).astype(BF16)
    flags_low = flags.astype(F32).astype(BF16)
    place = jnp.dot(flags_low, before, preferred_element_type=F32).astype(I32)
    sums = jnp.sum(flags, axis=1, keepdims=True)
    start = jnp.zeros((1, 1), I32)
    listed = jnp.zeros((3 * prow, 128), F32)
    lane_f, slot_f = lane[0:1].astype(F32), slot.astype(F32)
    for i in range(prow):
        at = jnp.where(inside[i : i + 1], place[i : i + 1] + start, -1)
        goes = row == (at >> 7)
        parts = [
            jnp.where(goes, v, 0.0) for v in (slot_f[i : i + 1], jnp.full((1, 128), float(i), F32), lane_f)
        ]
        spot = jnp.where(square_a == (at & 127), 1.0, 0.0).astype(BF16)
        listed += lax.dot_general(
            jnp.concatenate(parts, axis=0).astype(BF16), spot, (((1,), (1,)), ((), ())),
            preferred_element_type=F32,
        )
        start = start + sums[i : i + 1]
    listed = listed.astype(I32)
    entry = (listed[0:prow] << shift) + listed[prow : 2 * prow] * 128 + listed[2 * prow :]
    return jnp.where(number < start, entry, slots << shift), start


def gas_kernel(
    ng, nt, nf, live_ref, holder_hbm, flow_hbm, nu_hbm, pick_hbm, pos_hbm, mot_hbm, warm_hbm, mass_hbm, mult_hbm,
    table_ref, ints_ref, part_ref, placer_ref, pos_ref, mot_ref, warm_ref, mass_ref, mult_ref,
    holder_ref, pick_ref, nu_ref, gas_ref, own_ref, twice_ref, all_ref, send_ref, recv_ref,
    edge_ref, ylo_ref, yhi_ref, first_ref, last_ref, xlo_ref, xhi_ref,
    small_sem, gas_sem, nu_sem, bulk_sem, tile_s, tile_r, own_s, own_r, own2_s, own2_r, halo_s, halo_r, local_sem,
):
    g, t = lax.axis_index("grp"), lax.axis_index("tile")
    rows, planes, width = gas_ref.shape
    rows_y = rows // nf
    small = start_all([(holder_hbm, holder_ref), (pick_hbm, pick_ref)], small_sem)
    gas_loads = start_all([(flow_hbm.at[q % nf, :, q // nf, :], gas_ref.at[q]) for q in range(rows)], gas_sem)
    nu_loads = start_all([(nu_hbm.at[:, y, :], nu_ref.at[y]) for y in range(rows_y)], nu_sem)
    grp_peers = [(lax.rem(g + k, ng), t) for k in range(1, ng)]
    tile_peers = [(g, lax.rem(t + k, nt)) for k in range(1, nt)]
    everyone_in = signal_all(grp_peers + tile_peers)
    pairs = [(pos_hbm, pos_ref), (warm_hbm, warm_ref), (mass_hbm, mass_ref), (mult_hbm, mult_ref)]
    pairs += [(mot_hbm.at[f], mot_ref.at[f]) for f in range(3)]
    bulk = start_all(pairs, bulk_sem)

    own_ref[0] = jnp.full((1, 128), -1, I32)
    twice_ref[...] = jnp.full((1, 128), -1, I32)
    for c in small:
        c.wait()
    own_ref[0, :, 0:planes] = holder_ref[...]
    own = own_ref[0]
    twice_ref[:, 0:planes] = holder_ref[...]
    twice_ref[:, planes : 2 * planes] = holder_ref[...]
    both = twice_ref[...]
    row = jnp.broadcast_to(both, (128, 128))
    col = row.T
    s = lax.broadcasted_iota(I32, (128, 128), 0)
    l = lax.broadcasted_iota(I32, (128, 128), 1)
    near = (col == row) & ((s >= planes) == (l >= planes))
    rank = jnp.sum(jnp.where(near & (s < l), 1, 0), axis=0, keepdims=True)
    rank_col = jnp.sum(jnp.where(near & (l < s), 1, 0), axis=1, keepdims=True)
    lanes = lax.broadcasted_iota(I32, (1, 128), 1)
    subs = lax.broadcasted_iota(I32, (128, 1), 0)
    goal = both * (2 * SLOTS) + rank + jnp.where(lanes >= planes, SLOTS, 0)
    goal_col = col[:, 0:1] * (2 * SLOTS) + rank_col + jnp.where(subs >= planes, SLOTS, 0)
    picker = jnp.where(
        goal[:, 0 : 2 * planes] == lax.broadcasted_iota(I32, (nt * 2 * SLOTS, 2 * planes), 0), 1.0, 0.0
    ).astype(BF16)
    placer_ref[...] = jnp.where(
        goal_col[0 : 2 * planes] == lax.broadcasted_iota(I32, (2 * planes, nt * 2 * SLOTS), 1), 1.0, 0.0
    ).astype(BF16)
    gas_side = jnp.where(g < ng - 1, 1.0, 0.0).astype(F32)
    for r in range(0, rows, 2):
        two = []
        for q in (r, r + 1):
            gas_loads[q].wait()
            cells = gas_ref[q] * gas_side
            gas_ref[q] = cells
            two.append(cells)
        low = jnp.concatenate(two, axis=0).astype(BF16)
        got = jnp.dot(picker, low, preferred_element_type=F32).astype(BF16)
        for o in range(nt):
            send_ref[o, r * SLOTS : (r + 2) * SLOTS, :] = got[o * 2 * SLOTS : (o + 1) * 2 * SLOTS]
    edge_ref[0] = gas_ref[rows - nf : rows].astype(BF16)
    edge_ref[1] = gas_ref[0:nf].astype(BF16)
    first_ref[...] = gas_ref[:, 0, :].astype(BF16)
    last_ref[...] = gas_ref[:, planes - 1, :].astype(BF16)

    everyone_in()
    own_copies = [
        send_to(own_ref.at[0], all_ref.at[t, g], own_s.at[k], own_r.at[k], peer)
        for k, peer in enumerate(grp_peers)
    ]
    mine = pltpu.make_async_copy(own_ref.at[0], all_ref.at[t, g], local_sem.at[0])
    mine.start()
    slab = pltpu.make_async_copy(send_ref.at[t], recv_ref.at[t], local_sem.at[1])
    slab.start()
    tiles = [
        send_to(send_ref.at[peer[1]], recv_ref.at[t], tile_s.at[k], tile_r.at[k], peer)
        for k, peer in enumerate(tile_peers)
    ]
    halos = [
        send_to(edge_ref.at[0], ylo_ref, halo_s.at[0], halo_r.at[0], grp_peers[0]),
        send_to(edge_ref.at[1], yhi_ref, halo_s.at[1], halo_r.at[1], grp_peers[-1]),
        send_to(last_ref, xlo_ref, halo_s.at[2], halo_r.at[2], tile_peers[0]),
        send_to(first_ref, xhi_ref, halo_s.at[3], halo_r.at[3], tile_peers[-1]),
    ]
    mine.wait()
    for c in own_copies:
        c.wait()
    own2_copies = [
        send_to(all_ref.at[t], all_ref.at[t], own2_s.at[k], own2_r.at[k], peer)
        for k, peer in enumerate(tile_peers)
    ]
    table_ref[...] = jnp.zeros_like(table_ref)
    for c in nu_loads:
        c.wait()
    for c in halos:
        c.wait()
    sub = lax.broadcasted_iota(I32, (planes, width), 0)
    lane = lax.broadcasted_iota(I32, (planes, width), 1)
    has_low = jnp.where(t > 0, 1.0, 0.0).astype(F32)
    has_high = jnp.where(t < nt - 1, 1.0, 0.0).astype(F32)
    x_low = xlo_ref[...].astype(F32) * has_low
    x_high = xhi_ref[...].astype(F32) * has_high
    for r in range(rows):
        mid = gas_ref[r]
        below = gas_ref[r - nf] if r >= nf else ylo_ref[r].astype(F32)
        above = gas_ref[r + nf] if r < rows - nf else yhi_ref[r - (rows - nf)].astype(F32)
        total = below + above
        total += jnp.where(sub == 0, x_low[r : r + 1], pltpu.roll(mid, 1, 0))
        total += jnp.where(sub == planes - 1, x_high[r : r + 1], pltpu.roll(mid, planes - 1, 0))
        total += jnp.where(lane == 0, 0.0, pltpu.roll(mid, 1, 1))
        total += jnp.where(lane == width - 1, 0.0, pltpu.roll(mid, width - 1, 1))
        part_ref[r] = (mid + 0.5 * nu_ref[r // nf] * (total - 6.0 * mid)) * gas_side

    for c in own2_copies:
        c.wait()
    owners = jnp.concatenate([all_ref[d].reshape(ng, 128) for d in range(nt)], axis=0)
    entries, number = block_list(ng, nt, owners, pick_ref[...], live_ref[0])
    prow = entries.shape[0]
    ints_ref[0:prow, :] = entries
    ints_ref[prow : prow + 8, :] = jnp.broadcast_to(number, (8, 128))

    def unpack(d):
        for r in range(0, rows, 2):
            both = recv_ref[d, r * SLOTS : (r + 2) * SLOTS, :].astype(F32)
            for h in range(2):
                at = (r + h) // nf * 8 + (r + h) % nf
                table_ref[pl.ds(d * SLOTS * 32 + at, SLOTS, stride=32), :] = both[h * SLOTS : (h + 1) * SLOTS]

    slab.wait()
    unpack(t)
    for k, peer in enumerate(tile_peers):
        tiles[k].wait()
        unpack(lax.rem(t + nt - 1 - k, nt))
    for c in bulk:
        c.wait()


def parcel_kernel(
    nt, nf, ints_ref, table, pos_ref, mot_ref, warm_ref, mass_ref, mult_ref,
    dep_ref, acc, seen, par, src, smem, sem,
):
    to_smem = pltpu.make_async_copy(ints_ref, smem, sem)
    to_smem.start()
    blocks = pos_ref.shape[0]
    shift = blocks.bit_length() - 1
    prow = blocks // 128
    rows = dep_ref.shape[1] // SLOTS
    acc[...] = jnp.zeros_like(acc)
    src[...] = jnp.zeros_like(src)
    to_smem.wait()

    n = smem[prow, 0]
    sub = lax.broadcasted_iota(I32, (128, 128), 0).astype(F32).astype(BF16)
    yes, no = jnp.ones((128, 128), BF16), jnp.zeros((128, 128), BF16)
    half = lax.broadcasted_iota(I32, (16, 128), 0) >> 3
    half = [(half + 2 * k).astype(F32).astype(BF16) for k in range(2)]
    zero = jnp.zeros((32, 128), BF16)

    @pl.loop(0, (n + BATCH - 1) // BATCH)
    def _(step):
        where_at, which = [], []
        for j in range(BATCH):
            v = smem[step // (128 // BATCH), lax.rem(step, 128 // BATCH) * BATCH + j]
            b = v & (blocks - 1)
            base = pl.multiple_of((v >> shift) * 32, 32)
            cell = jnp.broadcast_to(pos_ref[pl.ds(b, 1), :], (8, 128))
            z = cell & 127
            got = [
                jnp.take_along_axis(table[pl.ds(base + k * 8, 8), :], z, axis=1) for k in range(4)
            ]
            upper = jnp.where(cell < 128, got[0], got[1])
            lower = jnp.where(cell < 384, got[2], got[3])
            seen[pl.ds(j, 8, stride=BATCH), :] = jnp.where(cell < 256, upper, lower)
            for f in range(3):
                par[f : f + 1, j, :] = mot_ref[f, pl.ds(b, 1), :]
            par[3:4, j, :] = warm_ref[pl.ds(b, 1), :]
            par[4:5, j, :] = mass_ref[pl.ds(b, 1), :]
            par[5:6, j, :] = mult_ref[pl.ds(b, 1), :]
            where_at.append(base)
            which.append(b)
        field = [seen[f * BATCH : (f + 1) * BATCH, :] for f in range(5)]
        v0, v1, v2, warm, mass, mult = [par[f] for f in range(6)]
        r0, r1, r2 = field[0] - v0, field[1] - v1, field[2] - v2
        speed_sq = r0 * r0 + r1 * r1 + r2 * r2
        inv_surface = jnp.exp(jnp.log(mass) * (-2.0 / 3.0))
        inverse_tau = 0.8 * (1.0 + 0.15 * jnp.exp(0.3435 * jnp.log(1.0 + speed_sq))) * inv_surface
        relax = 1.0 - jnp.exp(-0.5 * inverse_tau)
        heating = 1.0 / (1.0 + jnp.exp(field[4] - field[3]))
        remain = jnp.exp(-0.3 * heating * inv_surface)
        new_mass = mass * remain
        warming = 1.0 - jnp.exp(-0.25 * inverse_tau)
        new_warm = warm + warming * (field[3] - warm) - 0.5 * (1.0 - remain)
        outs = [mass * v - new_mass * (v + relax * r) for v, r in ((v0, r0), (v1, r1), (v2, r2))]
        outs += [mass * warm - new_mass * new_warm, mass - new_mass]
        for f, o in enumerate(outs):
            src[pl.ds(f, BATCH, stride=8), :] = mult * o
        for j in range(0, BATCH, 2):
            left, hot = [], []
            for i in (j, j + 1):
                cell = jnp.broadcast_to(pos_ref[pl.ds(which[i], 1), :], (16, 128))
                z = (cell & 127).astype(F32).astype(BF16)
                y = (cell >> 7).astype(F32).astype(BF16)
                s8 = src[pl.ds(i * 8, 8), :]
                s16 = jnp.concatenate([s8, s8], axis=0).astype(BF16)
                s32 = jnp.concatenate([jnp.where(y == h, s16, no[0:16]) for h in half], axis=0)
                left.append(jnp.concatenate([s32, zero] if i == j else [zero, s32], axis=1))
                hot.append(jnp.where(sub == jnp.concatenate([z] * 8, axis=0), yes, no))
            added = lax.dot_general(
                jnp.concatenate(left, axis=0), jnp.concatenate(hot, axis=1), (((1,), (1,)), ((), ())),
                preferred_element_type=F32,
            )
            for i in (j, j + 1):
                at = pl.ds(where_at[i], 32)
                acc[at, :] = acc[at, :] + added[(i - j) * 32 : (i - j + 1) * 32]

    for d in range(nt):
        for r in range(0, rows, 2):
            pair = [
                acc[pl.ds(d * SLOTS * 32 + q // nf * 8 + q % nf, SLOTS, stride=32), :] for q in (r, r + 1)
            ]
            dep_ref[d, r * SLOTS : (r + 2) * SLOTS, :] = jnp.concatenate(pair, axis=0).astype(BF16)


def return_kernel(ng, nt, dep_ref, recv_ref, tile_s, tile_r, local_sem):
    g, t = lax.axis_index("grp"), lax.axis_index("tile")
    peers = [(g, lax.rem(t + k, nt)) for k in range(1, nt)]
    everyone_in = signal_all(peers)
    slab = pltpu.make_async_copy(dep_ref.at[t], recv_ref.at[t], local_sem)
    slab.start()
    everyone_in()
    copies = [
        send_to(dep_ref.at[peer[1]], recv_ref.at[t], tile_s.at[k], tile_r.at[k], peer)
        for k, peer in enumerate(peers)
    ]
    slab.wait()
    for c in copies:
        c.wait()


def place_kernel(ng, nt, nf, recv_ref, placer_ref, part_ref, out_hbm, buf, sem):
    rows, planes, width = part_ref.shape
    gas_side = jnp.where(lax.axis_index("grp") < ng - 1, 1.0, 0.0).astype(F32)
    placer = placer_ref[...]
    copies = []
    for r in range(0, rows, 2):
        inc = jnp.concatenate([recv_ref[d, r * SLOTS : (r + 2) * SLOTS, :] for d in range(nt)], axis=0)
        placed = jnp.dot(placer, inc, preferred_element_type=F32)
        for h in range(2):
            q = r + h
            buf[q] = part_ref[q] + placed[h * planes : (h + 1) * planes] * gas_side
            c = pltpu.make_async_copy(buf.at[q], out_hbm.at[q % nf, :, q // nf, :], sem.at[q])
            c.start()
            copies.append(c)
    for c in copies:
        c.wait()


def local(
    flow_fields, turbulent_diffusivity, holder_unit, spray_volume_position, patch_pick_unreduced,
    droplet_motion, droplet_warmth, droplet_weightiness, droplet_multiplicity, living_spray_batches,
):
    ng, nt = lax.axis_size("grp"), lax.axis_size("tile")
    nf, planes, rows_y, width = flow_fields.shape
    rows = nf * rows_y
    dma = pltpu.SemaphoreType.DMA
    shape = jax.ShapeDtypeStruct
    blocks = spray_volume_position.shape[1]
    slots = nt * SLOTS
    prow = blocks // 128
    slab = (nt, rows * SLOTS, width)
    gas = (rows, planes, width)
    bulk = (shape((blocks, 128), I32), shape((3, blocks, 128), F32)) + (shape((blocks, 128), F32),) * 3
    table, ints, part, placer, *loaded = pl.pallas_call(
        functools.partial(gas_kernel, ng, nt, nf),
        out_shape=(
            shape(((slots + 1) * 32, width), F32), shape((prow + 8, 128), I32), shape(gas, F32),
            shape((2 * planes, nt * 2 * SLOTS), BF16),
        ) + bulk,
        in_specs=[SMEM] + [HBM] * 9, out_specs=(VMEM,) * 9,
        scratch_shapes=[
            pltpu.VMEM((1, planes), I32), pltpu.VMEM((prow, 128), I32),
            pltpu.VMEM((rows_y, planes, width), F32), pltpu.VMEM(gas, F32),
            pltpu.VMEM((1, 1, 128), I32), pltpu.VMEM((1, 128), I32), pltpu.VMEM((nt, ng, 1, 128), I32),
            pltpu.VMEM(slab, BF16), pltpu.VMEM(slab, BF16),
            pltpu.VMEM((2, nf, planes, width), BF16),
            pltpu.VMEM((nf, planes, width), BF16), pltpu.VMEM((nf, planes, width), BF16),
            pltpu.VMEM((rows, width), BF16), pltpu.VMEM((rows, width), BF16),
            pltpu.VMEM((rows, width), BF16), pltpu.VMEM((rows, width), BF16),
            dma((2,)), dma((rows,)), dma((rows_y,)), dma((7,)),
            dma((nt - 1,)), dma((nt - 1,)), dma((ng - 1,)), dma((ng - 1,)),
            dma((nt - 1,)), dma((nt - 1,)), dma((4,)), dma((4,)), dma((2,)),
        ],
        compiler_params=pltpu.CompilerParams(
            collective_id=0, has_side_effects=True, vmem_limit_bytes=24 << 20
        ),
        name="gas",
    )(living_spray_batches, *(pltpu.with_memory_space_constraint(a, pltpu.MemorySpace.HBM) for a in (
        holder_unit.reshape(1, planes), flow_fields, turbulent_diffusivity,
        patch_pick_unreduced.reshape(prow, 128), spray_volume_position[0],
        droplet_motion[0].transpose(1, 0, 2), droplet_warmth[0], droplet_weightiness[0],
        droplet_multiplicity[0],
    )))
    dep = pl.pallas_call(
        functools.partial(parcel_kernel, nt, nf),
        out_shape=shape(slab, BF16),
        in_specs=[VMEM] * 7, out_specs=VMEM,
        scratch_shapes=[
            pltpu.VMEM(((slots + 1) * 32, width), F32),
            pltpu.VMEM((BATCH * 8, width), F32),
            pltpu.VMEM((6, BATCH, width), F32),
            pltpu.VMEM((BATCH * 8, width), F32),
            pltpu.SMEM((prow + 8, 128), I32),
            dma,
        ],
        compiler_params=pltpu.CompilerParams(vmem_limit_bytes=24 << 20),
        name="parcels",
    )(ints, table, *loaded)
    recv = pl.pallas_call(
        functools.partial(return_kernel, ng, nt),
        out_shape=shape(slab, BF16),
        in_specs=[VMEM], out_specs=VMEM,
        scratch_shapes=[dma((nt - 1,)), dma((nt - 1,)), dma],
        compiler_params=pltpu.CompilerParams(
            collective_id=1, has_side_effects=True, vmem_limit_bytes=12 << 20
        ),
        name="return",
    )(dep)
    return pl.pallas_call(
        functools.partial(place_kernel, ng, nt, nf),
        out_shape=shape((nf, planes, rows_y, width), F32),
        in_specs=[VMEM] * 3, out_specs=HBM,
        scratch_shapes=[pltpu.VMEM(gas, F32), dma((rows,))],
        compiler_params=pltpu.CompilerParams(vmem_limit_bytes=12 << 20),
        name="place",
    )(recv, placer, part)


def solution(mesh):
    in_specs = (
        P(None, "tile", "grp", None),
        P("tile", "grp", None),
        P("grp", "tile", None),
        P("tile", None, None),
        P("tile", None),
        P("tile", None, None, None),
        P("tile", None, None),
        P("tile", None, None),
        P("tile", None, None),
        P("tile"),
    )
    out_specs = P(None, "tile", "grp", None)
    return jax.shard_map(local, mesh=mesh, in_specs=in_specs, out_specs=out_specs, check_vma=False)
```

```python
import functools

import jax
import jax.numpy as jnp
from jax import lax
from jax.experimental import pallas as pl
from jax.experimental.pallas import tpu as pltpu
from jax.sharding import PartitionSpec as P

MESH = pl.DeviceIdType.MESH
SLOTS = 8
BATCH = 64
HBM = pl.BlockSpec(memory_space=pltpu.MemorySpace.HBM)
VMEM = pl.BlockSpec(memory_space=pltpu.VMEM)
SMEM = pl.BlockSpec(memory_space=pltpu.SMEM)
F32, BF16, I32 = jnp.float32, jnp.bfloat16, jnp.int32


ROW = 8
PITCH = 33
SHARE = 4


def greet_all(ng, nt):
    me = lax.axis_index("grp") * nt + lax.axis_index("tile")
    barrier = pltpu.get_barrier_semaphore()

    def one(k, carry):
        other = lax.rem(me + k, ng * nt)
        pl.semaphore_signal(
            barrier, inc=1, device_id=(other // nt, lax.rem(other, nt)), device_id_type=MESH
        )
        return carry

    lax.fori_loop(1, ng * nt, one, 0)
    return lambda: pl.semaphore_wait(barrier, ng * nt - 1)


def source(ng, nt, s):
    g = lax.axis_index("grp")
    spare = g == ng - 1
    d = jnp.where(spare, s // (ng - 1) * SHARE + SHARE - 1, s + s // (SHARE - 1))
    return jnp.where(spare, lax.rem(s, ng - 1), g), d


def home(ng, nt):
    g, t = lax.axis_index("grp"), lax.axis_index("tile")
    shared = lax.rem(t, SHARE) == SHARE - 1
    return jnp.where(shared, ng - 1, g), jnp.where(shared, t // SHARE * (ng - 1) + g, t - t // SHARE)


def send_to(src, dst, ss, rs, dev):
    c = pltpu.make_async_remote_copy(
        src_ref=src, dst_ref=dst, send_sem=ss, recv_sem=rs, device_id=dev, device_id_type=MESH
    )
    c.start()
    return c


def start_all(pairs, sems):
    loads = [pltpu.make_async_copy(a, b, sems.at[k]) for k, (a, b) in enumerate(pairs)]
    for c in loads:
        c.start()
    return loads


def block_list(ng, nt, owners, pick, live):
    p = lax.axis_index("tile")
    prow = pick.shape[0]
    shift = (prow * 128).bit_length() - 1
    sources = nt * (SHARE - 1) // SHARE
    slots = sources * SLOTS
    owned = jnp.where(owners == p, 1, 0)
    counts = jnp.sum(owned, axis=1, keepdims=True)
    which = lax.broadcasted_iota(I32, counts.shape, 0)
    counts = jnp.where(which < (ng - 1) * nt, counts, 0)
    total = jnp.maximum(jnp.sum(counts, axis=0, keepdims=True), 1)
    total_f = total.astype(F32)
    quotient = jnp.floor(pick.astype(F32) / total_f).astype(I32)
    left = pick - quotient * total
    left = jnp.where(left < 0, left + total, left)
    left = jnp.where(left >= total, left - total, left)
    slot = jnp.full(pick.shape, -1, I32)
    for k in range(sources):
        from_g, from_d = source(ng, nt, k)
        number = from_g * nt + from_d
        low = jnp.sum(jnp.where(which < number, counts, 0), axis=0, keepdims=True)
        size = jnp.sum(jnp.where(which == number, counts, 0), axis=0, keepdims=True)
        rank = left - low
        slot = jnp.where((rank >= 0) & (rank < size), rank + k * SLOTS, slot)
    row = lax.broadcasted_iota(I32, (prow, 128), 0)
    lane = lax.broadcasted_iota(I32, (prow, 128), 1)
    number = row * 128 + lane
    inside = (slot >= 0) & (number < live)
    flags = jnp.where(inside, 1, 0)
    square_a = lax.broadcasted_iota(I32, (128, 128), 0)
    square_b = lax.broadcasted_iota(I32, (128, 128), 1)
    before = jnp.where(square_a < square_b, 1.0, 0.0).astype(BF16)
    flags_low = flags.astype(F32).astype(BF16)
    place = jnp.dot(flags_low, before, preferred_element_type=F32).astype(I32)
    sums = jnp.sum(flags, axis=1, keepdims=True)
    start = jnp.zeros((1, 1), I32)
    listed = jnp.zeros((3 * prow, 128), F32)
    lane_f, slot_f = lane[0:1].astype(F32), slot.astype(F32)
    for i in range(prow):
        at = jnp.where(inside[i : i + 1], place[i : i + 1] + start, -1)
        goes = row == (at >> 7)
        parts = [
            jnp.where(goes, v, 0.0) for v in (slot_f[i : i + 1], jnp.full((1, 128), float(i), F32), lane_f)
        ]
        spot = jnp.where(square_a == (at & 127), 1.0, 0.0).astype(BF16)
        listed += lax.dot_general(
            jnp.concatenate(parts, axis=0).astype(BF16), spot, (((1,), (1,)), ((), ())),
            preferred_element_type=F32,
        )
        start = start + sums[i : i + 1]
    listed = listed.astype(I32)
    entry = (listed[0:prow] << shift) + listed[prow : 2 * prow] * 128 + listed[2 * prow :]
    return jnp.where(number < start, entry, slots << shift), start


def gas_kernel(
    ng, nt, nf, live_ref, holder_hbm, flow_hbm, nu_hbm, pick_hbm, pos_hbm, mot_hbm, warm_hbm, mass_hbm, mult_hbm,
    table_ref, ints_ref, part_ref, placer_ref, parcel_ref,
    pos_ref, mot_ref, warm_ref, mass_ref, mult_ref, holder_ref, pick_ref, nu_ref, gas_ref, own_ref, twice_ref, all_ref, send_ref, recv_ref,
    edge_ref, ylo_ref, yhi_ref, first_ref, last_ref, xlo_ref, xhi_ref,
    small_sem, gas_sem, nu_sem, bulk_sem, tile_s, tile_r, own_s, own_r, own2_s, own2_r, halo_s, halo_r, local_sem,
):
    g, t = lax.axis_index("grp"), lax.axis_index("tile")
    rows, planes, width = gas_ref.shape
    rows_y = rows // nf
    sources = recv_ref.shape[0]
    small = start_all([(holder_hbm, holder_ref), (pick_hbm, pick_ref)], small_sem)
    gas_loads = start_all([(flow_hbm.at[q % nf, :, q // nf, :], gas_ref.at[q]) for q in range(rows)], gas_sem)
    nu_loads = start_all([(nu_hbm.at[:, y, :], nu_ref.at[y]) for y in range(rows_y)], nu_sem)
    grp_peers = [(lax.rem(g + k, ng), t) for k in range(1, ng)]
    tile_peers = [(g, lax.rem(t + k, nt)) for k in range(1, nt)]
    everyone_in = greet_all(ng, nt)
    pairs = [(pos_hbm, pos_ref), (warm_hbm, warm_ref), (mass_hbm, mass_ref), (mult_hbm, mult_ref)]
    pairs += [(mot_hbm.at[f], mot_ref.at[f]) for f in range(3)]
    bulk = start_all(pairs, bulk_sem)

    own_ref[0] = jnp.full((1, 128), -1, I32)
    twice_ref[...] = jnp.full((1, 128), -1, I32)
    for c in small:
        c.wait()
    own_ref[0, :, 0:planes] = holder_ref[...]
    own = own_ref[0]
    twice_ref[:, 0:planes] = holder_ref[...]
    twice_ref[:, planes : 2 * planes] = holder_ref[...]
    both = twice_ref[...]
    row = jnp.broadcast_to(both, (128, 128))
    col = row.T
    s = lax.broadcasted_iota(I32, (128, 128), 0)
    l = lax.broadcasted_iota(I32, (128, 128), 1)
    near = (col == row) & ((s >= planes) == (l >= planes))
    rank = jnp.sum(jnp.where(near & (s < l), 1, 0), axis=0, keepdims=True)
    rank_col = jnp.sum(jnp.where(near & (l < s), 1, 0), axis=1, keepdims=True)
    lanes = lax.broadcasted_iota(I32, (1, 128), 1)
    subs = lax.broadcasted_iota(I32, (128, 1), 0)
    goal = both * (2 * SLOTS) + rank + jnp.where(lanes >= planes, SLOTS, 0)
    goal_col = col[:, 0:1] * (2 * SLOTS) + rank_col + jnp.where(subs >= planes, SLOTS, 0)
    picker = jnp.where(
        goal[:, 0 : 2 * planes] == lax.broadcasted_iota(I32, (nt * 2 * SLOTS, 2 * planes), 0), 1.0, 0.0
    ).astype(BF16)
    placer_ref[...] = jnp.where(
        goal_col[0 : 2 * planes] == lax.broadcasted_iota(I32, (2 * planes, nt * 2 * SLOTS), 1), 1.0, 0.0
    ).astype(BF16)
    gas_side = jnp.where(g < ng - 1, 1.0, 0.0).astype(F32)
    for r in range(0, rows, 2):
        two = []
        for q in (r, r + 1):
            gas_loads[q].wait()
            cells = gas_ref[q] * gas_side
            gas_ref[q] = cells
            two.append(cells)
        low = jnp.concatenate(two, axis=0).astype(BF16)
        got = jnp.dot(picker, low, preferred_element_type=F32).astype(BF16)
        for o in range(nt):
            send_ref[o, r * SLOTS : (r + 2) * SLOTS, :] = got[o * 2 * SLOTS : (o + 1) * 2 * SLOTS]
    edge_ref[0] = gas_ref[rows - nf : rows].astype(BF16)
    edge_ref[1] = gas_ref[0:nf].astype(BF16)
    first_ref[...] = gas_ref[:, 0, :].astype(BF16)
    last_ref[...] = gas_ref[:, planes - 1, :].astype(BF16)

    everyone_in()
    own_copies = [
        send_to(own_ref.at[0], all_ref.at[g, t], own_s.at[k], own_r.at[k], peer)
        for k, peer in enumerate(tile_peers)
    ]
    mine = pltpu.make_async_copy(own_ref.at[0], all_ref.at[g, t], local_sem.at[0])
    mine.start()
    home_g, home_s = home(ng, nt)
    gives = g < ng - 1
    stays = gives & (home_g == g)

    def slab(k):
        p = lax.rem(t + k, nt)
        return pltpu.make_async_remote_copy(
            src_ref=send_ref.at[p], dst_ref=recv_ref.at[home_s], send_sem=tile_s.at[k],
            recv_sem=tile_r.at[home_s], device_id=(home_g, p), device_id_type=MESH,
        )

    kept = pltpu.make_async_copy(send_ref.at[t], recv_ref.at[home_s], local_sem.at[1])

    @pl.when(stays)
    def _():
        kept.start()

    for k in range(1, nt):

        @pl.when(gives)
        def _():
            slab(k).start()

    @pl.when(gives & (home_g != g))
    def _():
        slab(0).start()

    halos = [
        send_to(edge_ref.at[0], ylo_ref, halo_s.at[0], halo_r.at[0], grp_peers[0]),
        send_to(edge_ref.at[1], yhi_ref, halo_s.at[1], halo_r.at[1], grp_peers[-1]),
        send_to(last_ref, xlo_ref, halo_s.at[2], halo_r.at[2], tile_peers[0]),
        send_to(first_ref, xhi_ref, halo_s.at[3], halo_r.at[3], tile_peers[-1]),
    ]
    mine.wait()
    for c in own_copies:
        c.wait()
    own2_copies = [
        send_to(all_ref.at[g], all_ref.at[g], own2_s.at[k], own2_r.at[k], peer)
        for k, peer in enumerate(grp_peers)
    ]
    table_ref[...] = jnp.zeros_like(table_ref)
    for c in bulk:
        c.wait()

    @pl.loop(0, pos_ref.shape[0] // 8)
    def _(k):
        at = pl.ds(pl.multiple_of(k * 8, 8), 8)
        cell = pos_ref[at, :]
        values = [mot_ref[f, at, :] for f in range(3)] + [warm_ref[at, :], mass_ref[at, :], mult_ref[at, :]]
        values += [(cell & 127).astype(F32), (cell >> 7).astype(F32)]
        for f, v in enumerate(values):
            parcel_ref[pl.ds(k * 8 * (ROW + 1) + f, 8, stride=ROW + 1), :] = v

    for c in nu_loads:
        c.wait()
    for c in halos:
        c.wait()
    sub = lax.broadcasted_iota(I32, (planes, width), 0)
    lane = lax.broadcasted_iota(I32, (planes, width), 1)
    has_low = jnp.where(t > 0, 1.0, 0.0).astype(F32)
    has_high = jnp.where(t < nt - 1, 1.0, 0.0).astype(F32)
    x_low = xlo_ref[...].astype(F32) * has_low
    x_high = xhi_ref[...].astype(F32) * has_high
    for r in range(rows):
        mid = gas_ref[r]
        below = gas_ref[r - nf] if r >= nf else ylo_ref[r].astype(F32)
        above = gas_ref[r + nf] if r < rows - nf else yhi_ref[r - (rows - nf)].astype(F32)
        total = below + above
        total += jnp.where(sub == 0, x_low[r : r + 1], pltpu.roll(mid, 1, 0))
        total += jnp.where(sub == planes - 1, x_high[r : r + 1], pltpu.roll(mid, planes - 1, 0))
        total += jnp.where(lane == 0, 0.0, pltpu.roll(mid, 1, 1))
        total += jnp.where(lane == width - 1, 0.0, pltpu.roll(mid, width - 1, 1))
        part_ref[r] = (mid + 0.5 * nu_ref[r // nf] * (total - 6.0 * mid)) * gas_side

    for c in own2_copies:
        c.wait()
    owners = jnp.concatenate([all_ref[k].reshape(nt, 128) for k in range(ng)], axis=0)
    entries, number = block_list(ng, nt, owners, pick_ref[...], live_ref[0])
    prow = entries.shape[0]
    ints_ref[0:prow, :] = entries
    ints_ref[prow : prow + 8, :] = jnp.broadcast_to(number, (8, 128))

    def unpack(d):
        for r in range(0, rows, 2):
            both = recv_ref[d, r * SLOTS : (r + 2) * SLOTS, :].astype(F32)
            for h in range(2):
                at = (r + h) // nf * 8 + (r + h) % nf
                table_ref[pl.ds(d * SLOTS * PITCH + at, SLOTS, stride=PITCH), :] = both[h * SLOTS : (h + 1) * SLOTS]

    @pl.when(stays)
    def _():
        kept.wait()

    for k in range(sources):
        from_g, from_d = source(ng, nt, k)

        @pl.when((from_g != g) | (from_d != t))
        def _():
            pltpu.make_async_remote_copy(
                src_ref=send_ref.at[0], dst_ref=recv_ref.at[k], send_sem=tile_s.at[0],
                recv_sem=tile_r.at[k], device_id=(from_g, from_d), device_id_type=MESH,
            ).wait_recv()

        unpack(k)
    for k in range(1, nt):

        @pl.when(gives)
        def _():
            slab(k).wait_send()

    @pl.when(gives & (home_g != g))
    def _():
        slab(0).wait_send()


def parcel_kernel(
    ints_ref, table, parcels, acc, seen, par, src, add, smem, sem,
):
    to_smem = pltpu.make_async_copy(ints_ref, smem, sem)
    to_smem.start()
    blocks = parcels.shape[0] // (ROW + 1)
    shift = blocks.bit_length() - 1
    prow = blocks // 128
    span = BATCH + 1
    acc[...] = jnp.zeros_like(acc)
    src[...] = jnp.zeros_like(src)
    par[...] = jnp.zeros_like(par)
    to_smem.wait()

    n = smem[prow, 0]
    sub = lax.broadcasted_iota(I32, (128, 128), 0).astype(F32).astype(BF16)
    yes, no = jnp.ones((128, 128), BF16), jnp.zeros((128, 128), BF16)
    half = lax.broadcasted_iota(I32, (16, 128), 0) >> 3
    half = [(half + 2 * k).astype(F32).astype(BF16) for k in range(2)]
    zero = jnp.zeros((32, 128), BF16)

    @pl.loop(0, (n + BATCH - 1) // BATCH + 1)
    def _(step):
        last = jnp.maximum(step - 1, 0)
        rows = [(k // (128 // BATCH), lax.rem(k, 128 // BATCH) * BATCH) for k in (step, last)]
        for j in range(0, BATCH, 2):
            left, hot = [], []
            for i in (j, j + 1):
                z = jnp.broadcast_to(par[6 * span + i : 6 * span + i + 1, :], (16, 128)).astype(BF16)
                y = jnp.broadcast_to(par[7 * span + i : 7 * span + i + 1, :], (16, 128)).astype(BF16)
                s8 = src[pl.ds(i * 9, 8), :]
                s16 = jnp.concatenate([s8, s8], axis=0).astype(BF16)
                s32 = jnp.concatenate([jnp.where(y == h, s16, no[0:16]) for h in half], axis=0)
                left.append(jnp.concatenate([s32, zero] if i == j else [zero, s32], axis=1))
                hot.append(jnp.where(sub == jnp.concatenate([z] * 8, axis=0), yes, no))
            add[j * 32 : (j + 2) * 32, :] = lax.dot_general(
                jnp.concatenate(left, axis=0), jnp.concatenate(hot, axis=1), (((1,), (1,)), ((), ())),
                preferred_element_type=F32,
            )
            for i in (j, j + 1):
                v = smem[rows[0][0], rows[0][1] + i]
                b = (v & (blocks - 1)) * (ROW + 1)
                base = (v >> shift) * PITCH
                values = parcels[pl.ds(b, 8), :]
                z = jnp.broadcast_to(parcels[pl.ds(b + 6, 1), :], (8, 128)).astype(I32)
                y = jnp.broadcast_to(parcels[pl.ds(b + 7, 1), :], (8, 128))
                got = [
                    jnp.take_along_axis(table[pl.ds(base + k * 8, 8), :], z, axis=1) for k in range(4)
                ]
                upper = jnp.where(y < 1, got[0], got[1])
                lower = jnp.where(y < 3, got[2], got[3])
                seen[pl.ds(i, 8, stride=span), :] = jnp.where(y < 2, upper, lower)
                par[pl.ds(i, 8, stride=span), :] = values
        for i in range(BATCH):
            at = pl.ds((smem[rows[1][0], rows[1][1] + i] >> shift) * PITCH, 32)
            acc[at, :] = acc[at, :] + add[i * 32 : (i + 1) * 32, :]
        field = [seen[f * span : f * span + BATCH, :] for f in range(5)]
        v0, v1, v2, warm, mass, mult = [par[f * span : f * span + BATCH, :] for f in range(6)]
        r0, r1, r2 = field[0] - v0, field[1] - v1, field[2] - v2
        speed_sq = r0 * r0 + r1 * r1 + r2 * r2
        inv_surface = jnp.exp(jnp.log(mass) * (-2.0 / 3.0))
        inverse_tau = 0.8 * (1.0 + 0.15 * jnp.exp(0.3435 * jnp.log(1.0 + speed_sq))) * inv_surface
        relax = 1.0 - jnp.exp(-0.5 * inverse_tau)
        heating = 1.0 / (1.0 + jnp.exp(field[4] - field[3]))
        remain = jnp.exp(-0.3 * heating * inv_surface)
        new_mass = mass * remain
        warming = 1.0 - jnp.exp(-0.25 * inverse_tau)
        new_warm = warm + warming * (field[3] - warm) - 0.5 * (1.0 - remain)
        outs = [mass * v - new_mass * (v + relax * r) for v, r in ((v0, r0), (v1, r1), (v2, r2))]
        outs += [mass * warm - new_mass * new_warm, mass - new_mass]
        for f, o in enumerate(outs):
            src[pl.ds(f, BATCH, stride=9), :] = mult * o


def return_kernel(ng, nt, nf, acc_ref, recv_ref, send_ref, tile_s, tile_r, local_sem):
    g, t = lax.axis_index("grp"), lax.axis_index("tile")
    everyone_in = greet_all(ng, nt)
    sources, rows, _ = send_ref.shape
    for d in range(sources):
        for r in range(0, rows // SLOTS, 2):
            pair = [
                acc_ref[pl.ds(d * SLOTS * PITCH + q // nf * 8 + q % nf, SLOTS, stride=PITCH), :]
                for q in (r, r + 1)
            ]
            send_ref[d, r * SLOTS : (r + 2) * SLOTS, :] = jnp.concatenate(pair, axis=0).astype(BF16)
    home_g, home_s = home(ng, nt)
    takes = g < ng - 1
    stays = takes & (home_g == g)

    def slab(k):
        return pltpu.make_async_remote_copy(
            src_ref=send_ref.at[k], dst_ref=recv_ref.at[t], send_sem=tile_s.at[k],
            recv_sem=tile_r.at[t], device_id=source(ng, nt, k), device_id_type=MESH,
        )

    def remote(k):
        to_g, to_d = source(ng, nt, k)
        return (to_g != g) | (to_d != t)

    everyone_in()
    for k in range(sources):

        @pl.when(remote(k))
        def _():
            slab(k).start()

    kept = pltpu.make_async_copy(send_ref.at[jnp.where(takes, home_s, 0)], recv_ref.at[t], local_sem)

    @pl.when(stays)
    def _():
        kept.start()
        kept.wait()

    @pl.when(jnp.logical_not(takes))
    def _():
        recv_ref[...] = jnp.zeros_like(recv_ref)

    for p in range(nt):

        @pl.when(takes & ((home_g != g) | (t != p)))
        def _():
            pltpu.make_async_remote_copy(
                src_ref=send_ref.at[0], dst_ref=recv_ref.at[p], send_sem=tile_s.at[0],
                recv_sem=tile_r.at[p], device_id=(home_g, p), device_id_type=MESH,
            ).wait_recv()

    for k in range(sources):

        @pl.when(remote(k))
        def _():
            slab(k).wait_send()


def place_kernel(ng, nt, nf, recv_ref, placer_ref, part_ref, out_hbm, buf, sem):
    rows, planes, width = part_ref.shape
    gas_side = lax.axis_index("grp") < ng - 1
    placer = placer_ref[...]
    copies = []
    for r in range(0, rows, 2):
        inc = jnp.concatenate([recv_ref[d, r * SLOTS : (r + 2) * SLOTS, :] for d in range(nt)], axis=0)
        placed = jnp.dot(placer, inc, preferred_element_type=F32)
        for h in range(2):
            q = r + h
            buf[q] = part_ref[q] + jnp.where(gas_side, placed[h * planes : (h + 1) * planes], 0.0)
            c = pltpu.make_async_copy(buf.at[q], out_hbm.at[q % nf, :, q // nf, :], sem.at[q])
            c.start()
            copies.append(c)
    for c in copies:
        c.wait()


def local(
    flow_fields, turbulent_diffusivity, holder_unit, spray_volume_position, patch_pick_unreduced,
    droplet_motion, droplet_warmth, droplet_weightiness, droplet_multiplicity, living_spray_batches,
):
    ng, nt = lax.axis_size("grp"), lax.axis_size("tile")
    nf, planes, rows_y, width = flow_fields.shape
    rows = nf * rows_y
    dma = pltpu.SemaphoreType.DMA
    shape = jax.ShapeDtypeStruct
    blocks = spray_volume_position.shape[1]
    sources = nt * (SHARE - 1) // SHARE
    slots = sources * SLOTS
    prow = blocks // 128
    slab = (nt, rows * SLOTS, width)
    gas = (rows, planes, width)
    table, ints, part, placer, parcels = pl.pallas_call(
        functools.partial(gas_kernel, ng, nt, nf),
        out_shape=(
            shape(((slots + 1) * PITCH + 7, width), F32), shape((prow + 8, 128), I32), shape(gas, F32),
            shape((2 * planes, nt * 2 * SLOTS), BF16), shape((blocks * (ROW + 1), 128), F32),
        ),
        in_specs=[SMEM] + [HBM] * 9, out_specs=(VMEM,) * 5,
        scratch_shapes=[
            pltpu.VMEM((blocks, 128), I32), pltpu.VMEM((3, blocks, 128), F32),
            pltpu.VMEM((blocks, 128), F32), pltpu.VMEM((blocks, 128), F32), pltpu.VMEM((blocks, 128), F32),
            pltpu.VMEM((1, planes), I32), pltpu.VMEM((prow, 128), I32),
            pltpu.VMEM((rows_y, planes, width), F32), pltpu.VMEM(gas, F32),
            pltpu.VMEM((1, 1, 128), I32), pltpu.VMEM((1, 128), I32), pltpu.VMEM((ng, nt, 1, 128), I32),
            pltpu.VMEM(slab, BF16), pltpu.VMEM((sources,) + slab[1:], BF16),
            pltpu.VMEM((2, nf, planes, width), BF16),
            pltpu.VMEM((nf, planes, width), BF16), pltpu.VMEM((nf, planes, width), BF16),
            pltpu.VMEM((rows, width), BF16), pltpu.VMEM((rows, width), BF16),
            pltpu.VMEM((rows, width), BF16), pltpu.VMEM((rows, width), BF16),
            dma((2,)), dma((rows,)), dma((rows_y,)), dma((7,)),
            dma((nt,)), dma((sources,)), dma((nt - 1,)), dma((nt - 1,)),
            dma((ng - 1,)), dma((ng - 1,)), dma((4,)), dma((4,)), dma((2,)),
        ],
        compiler_params=pltpu.CompilerParams(
            collective_id=0, has_side_effects=True, vmem_limit_bytes=24 << 20
        ),
        name="gas",
    )(living_spray_batches, *(pltpu.with_memory_space_constraint(a, pltpu.MemorySpace.HBM) for a in (
        holder_unit.reshape(1, planes), flow_fields, turbulent_diffusivity,
        patch_pick_unreduced.reshape(prow, 128), spray_volume_position[0],
        droplet_motion[0].transpose(1, 0, 2), droplet_warmth[0], droplet_weightiness[0],
        droplet_multiplicity[0],
    )))
    acc = pl.pallas_call(
        parcel_kernel,
        out_shape=shape(((slots + 1) * PITCH + 7, width), F32),
        in_specs=[VMEM] * 3, out_specs=VMEM,
        scratch_shapes=[
            pltpu.VMEM((8 * (BATCH + 1), width), F32),
            pltpu.VMEM((8 * (BATCH + 1), width), F32),
            pltpu.VMEM((BATCH * 9, width), F32),
            pltpu.VMEM((BATCH * 32, width), F32),
            pltpu.SMEM((prow + 8, 128), I32),
            dma,
        ],
        compiler_params=pltpu.CompilerParams(vmem_limit_bytes=24 << 20),
        name="parcels",
    )(ints, table, parcels)
    recv = pl.pallas_call(
        functools.partial(return_kernel, ng, nt, nf),
        out_shape=shape(slab, BF16),
        in_specs=[VMEM], out_specs=VMEM,
        scratch_shapes=[
            pltpu.VMEM((sources,) + slab[1:], BF16), dma((sources,)), dma((nt,)), dma,
        ],
        compiler_params=pltpu.CompilerParams(
            collective_id=1, has_side_effects=True, vmem_limit_bytes=16 << 20
        ),
        name="return",
    )(acc)
    return pl.pallas_call(
        functools.partial(place_kernel, ng, nt, nf),
        out_shape=shape((nf, planes, rows_y, width), F32),
        in_specs=[VMEM] * 3, out_specs=HBM,
        scratch_shapes=[pltpu.VMEM(gas, F32), dma((rows,))],
        compiler_params=pltpu.CompilerParams(vmem_limit_bytes=12 << 20),
        name="place",
    )(recv, placer, part)


def solution(mesh):
    in_specs = (
        P(None, "tile", "grp", None),
        P("tile", "grp", None),
        P("grp", "tile", None),
        P("tile", None, None),
        P("tile", None),
        P("tile", None, None, None),
        P("tile", None, None),
        P("tile", None, None),
        P("tile", None, None),
        P("tile"),
    )
    out_specs = P(None, "tile", "grp", None)
    return jax.shard_map(local, mesh=mesh, in_specs=in_specs, out_specs=out_specs, check_vma=False)
```

```python
import functools

import jax
import jax.numpy as jnp
from jax import lax
from jax.experimental import pallas as pl
from jax.experimental.pallas import tpu as pltpu
from jax.sharding import PartitionSpec as P

MESH = pl.DeviceIdType.MESH
SLOTS = 8
BATCH = 64
HBM = pl.BlockSpec(memory_space=pltpu.MemorySpace.HBM)
VMEM = pl.BlockSpec(memory_space=pltpu.VMEM)
SMEM = pl.BlockSpec(memory_space=pltpu.SMEM)
F32, BF16, I32 = jnp.float32, jnp.bfloat16, jnp.int32


ROW = 8
PITCH = 33
SHARE = 4


def greet_all(ng, nt):
    me = lax.axis_index("grp") * nt + lax.axis_index("tile")
    barrier = pltpu.get_barrier_semaphore()

    def one(k, carry):
        other = lax.rem(me + k, ng * nt)
        pl.semaphore_signal(
            barrier, inc=1, device_id=(other // nt, lax.rem(other, nt)), device_id_type=MESH
        )
        return carry

    lax.fori_loop(1, ng * nt, one, 0)
    return lambda: pl.semaphore_wait(barrier, ng * nt - 1)


def source(ng, nt, s):
    g, p = lax.axis_index("grp"), lax.axis_index("tile")
    spare = g == ng - 1
    e = jnp.where(spare, s // (ng - 1) * SHARE + SHARE - 1, s + s // (SHARE - 1))
    return jnp.where(spare, lax.rem(s, ng - 1), g), lax.rem(e - p + nt, nt)


def home(ng, nt, p):
    g = lax.axis_index("grp")
    e = lax.rem(lax.axis_index("tile") + p, nt)
    shared = lax.rem(e, SHARE) == SHARE - 1
    return jnp.where(shared, ng - 1, g), jnp.where(shared, e // SHARE * (ng - 1) + g, e - e // SHARE)


def send_to(src, dst, ss, rs, dev):
    c = pltpu.make_async_remote_copy(
        src_ref=src, dst_ref=dst, send_sem=ss, recv_sem=rs, device_id=dev, device_id_type=MESH
    )
    c.start()
    return c


def start_all(pairs, sems):
    loads = [pltpu.make_async_copy(a, b, sems.at[k]) for k, (a, b) in enumerate(pairs)]
    for c in loads:
        c.start()
    return loads


def block_list(ng, nt, owners, pick, live):
    p = lax.axis_index("tile")
    prow = pick.shape[0]
    shift = (prow * 128).bit_length() - 1
    sources = nt * (SHARE - 1) // SHARE
    slots = sources * SLOTS
    owned = jnp.where(owners == p, 1, 0)
    counts = jnp.sum(owned, axis=1, keepdims=True)
    which = lax.broadcasted_iota(I32, counts.shape, 0)
    counts = jnp.where(which < (ng - 1) * nt, counts, 0)
    total = jnp.maximum(jnp.sum(counts, axis=0, keepdims=True), 1)
    total_f = total.astype(F32)
    quotient = jnp.floor(pick.astype(F32) / total_f).astype(I32)
    left = pick - quotient * total
    left = jnp.where(left < 0, left + total, left)
    left = jnp.where(left >= total, left - total, left)
    slot = jnp.full(pick.shape, -1, I32)
    for k in range(sources):
        from_g, from_d = source(ng, nt, k)
        number = from_g * nt + from_d
        low = jnp.sum(jnp.where(which < number, counts, 0), axis=0, keepdims=True)
        size = jnp.sum(jnp.where(which == number, counts, 0), axis=0, keepdims=True)
        rank = left - low
        slot = jnp.where((rank >= 0) & (rank < size), rank + k * SLOTS, slot)
    row = lax.broadcasted_iota(I32, (prow, 128), 0)
    lane = lax.broadcasted_iota(I32, (prow, 128), 1)
    number = row * 128 + lane
    inside = (slot >= 0) & (number < live)
    flags = jnp.where(inside, 1, 0)
    square_a = lax.broadcasted_iota(I32, (128, 128), 0)
    square_b = lax.broadcasted_iota(I32, (128, 128), 1)
    before = jnp.where(square_a < square_b, 1.0, 0.0).astype(BF16)
    flags_low = flags.astype(F32).astype(BF16)
    place = jnp.dot(flags_low, before, preferred_element_type=F32).astype(I32)
    sums = jnp.sum(flags, axis=1, keepdims=True)
    start = jnp.zeros((1, 1), I32)
    listed = jnp.zeros((3 * prow, 128), F32)
    lane_f, slot_f = lane[0:1].astype(F32), slot.astype(F32)
    for i in range(prow):
        at = jnp.where(inside[i : i + 1], place[i : i + 1] + start, -1)
        goes = row == (at >> 7)
        parts = [
            jnp.where(goes, v, 0.0) for v in (slot_f[i : i + 1], jnp.full((1, 128), float(i), F32), lane_f)
        ]
        spot = jnp.where(square_a == (at & 127), 1.0, 0.0).astype(BF16)
        listed += lax.dot_general(
            jnp.concatenate(parts, axis=0).astype(BF16), spot, (((1,), (1,)), ((), ())),
            preferred_element_type=F32,
        )
        start = start + sums[i : i + 1]
    listed = listed.astype(I32)
    entry = (listed[0:prow] << shift) + listed[prow : 2 * prow] * 128 + listed[2 * prow :]
    return jnp.where(number < start, entry, slots << shift), start


def gas_kernel(
    ng, nt, nf, live_ref, holder_hbm, flow_hbm, nu_hbm, pick_hbm, pos_hbm, mot_hbm, warm_hbm, mass_hbm, mult_hbm,
    table_ref, ints_ref, part_ref, placer_ref, parcel_ref,
    pos_ref, mot_ref, warm_ref, mass_ref, mult_ref, holder_ref, pick_ref, nu_ref, gas_ref, own_ref, twice_ref, all_ref, send_ref, recv_ref,
    edge_ref, ylo_ref, yhi_ref, first_ref, last_ref, xlo_ref, xhi_ref,
    small_sem, gas_sem, nu_sem, bulk_sem, tile_s, tile_r, own_s, own_r, own2_s, own2_r, halo_s, halo_r, local_sem,
):
    g, t = lax.axis_index("grp"), lax.axis_index("tile")
    rows, planes, width = gas_ref.shape
    rows_y = rows // nf
    sources = recv_ref.shape[0]
    small = start_all([(holder_hbm, holder_ref), (pick_hbm, pick_ref)], small_sem)
    gas_loads = start_all([(flow_hbm.at[q % nf, :, q // nf, :], gas_ref.at[q]) for q in range(rows)], gas_sem)
    nu_loads = start_all([(nu_hbm.at[:, y, :], nu_ref.at[y]) for y in range(rows_y)], nu_sem)
    grp_peers = [(lax.rem(g + k, ng), t) for k in range(1, ng)]
    tile_peers = [(g, lax.rem(t + k, nt)) for k in range(1, nt)]
    everyone_in = greet_all(ng, nt)
    pairs = [(pos_hbm, pos_ref), (warm_hbm, warm_ref), (mass_hbm, mass_ref), (mult_hbm, mult_ref)]
    pairs += [(mot_hbm.at[f], mot_ref.at[f]) for f in range(3)]
    bulk = start_all(pairs, bulk_sem)

    own_ref[0] = jnp.full((1, 128), -1, I32)
    twice_ref[...] = jnp.full((1, 128), -1, I32)
    for c in small:
        c.wait()
    own_ref[0, :, 0:planes] = holder_ref[...]
    own = own_ref[0]
    twice_ref[:, 0:planes] = holder_ref[...]
    twice_ref[:, planes : 2 * planes] = holder_ref[...]
    both = twice_ref[...]
    row = jnp.broadcast_to(both, (128, 128))
    col = row.T
    s = lax.broadcasted_iota(I32, (128, 128), 0)
    l = lax.broadcasted_iota(I32, (128, 128), 1)
    near = (col == row) & ((s >= planes) == (l >= planes))
    rank = jnp.sum(jnp.where(near & (s < l), 1, 0), axis=0, keepdims=True)
    rank_col = jnp.sum(jnp.where(near & (l < s), 1, 0), axis=1, keepdims=True)
    lanes = lax.broadcasted_iota(I32, (1, 128), 1)
    subs = lax.broadcasted_iota(I32, (128, 1), 0)
    goal = both * (2 * SLOTS) + rank + jnp.where(lanes >= planes, SLOTS, 0)
    goal_col = col[:, 0:1] * (2 * SLOTS) + rank_col + jnp.where(subs >= planes, SLOTS, 0)
    picker = jnp.where(
        goal[:, 0 : 2 * planes] == lax.broadcasted_iota(I32, (nt * 2 * SLOTS, 2 * planes), 0), 1.0, 0.0
    ).astype(BF16)
    placer_ref[...] = jnp.where(
        goal_col[0 : 2 * planes] == lax.broadcasted_iota(I32, (2 * planes, nt * 2 * SLOTS), 1), 1.0, 0.0
    ).astype(BF16)
    gas_side = jnp.where(g < ng - 1, 1.0, 0.0).astype(F32)
    for r in range(0, rows, 2):
        two = []
        for q in (r, r + 1):
            gas_loads[q].wait()
            cells = gas_ref[q] * gas_side
            gas_ref[q] = cells
            two.append(cells)
        low = jnp.concatenate(two, axis=0).astype(BF16)
        got = jnp.dot(picker, low, preferred_element_type=F32).astype(BF16)
        for o in range(nt):
            send_ref[o, r * SLOTS : (r + 2) * SLOTS, :] = got[o * 2 * SLOTS : (o + 1) * 2 * SLOTS]
    edge_ref[0] = gas_ref[rows - nf : rows].astype(BF16)
    edge_ref[1] = gas_ref[0:nf].astype(BF16)
    first_ref[...] = gas_ref[:, 0, :].astype(BF16)
    last_ref[...] = gas_ref[:, planes - 1, :].astype(BF16)

    everyone_in()
    own_copies = [
        send_to(own_ref.at[0], all_ref.at[g, t], own_s.at[k], own_r.at[k], peer)
        for k, peer in enumerate(tile_peers)
    ]
    mine = pltpu.make_async_copy(own_ref.at[0], all_ref.at[g, t], local_sem.at[0])
    mine.start()
    gives = g < ng - 1

    def slab(k):
        p = lax.rem(t + k, nt)
        to_g, at = home(ng, nt, p)
        return pltpu.make_async_remote_copy(
            src_ref=send_ref.at[p], dst_ref=recv_ref.at[at], send_sem=tile_s.at[k],
            recv_sem=tile_r.at[at], device_id=(to_g, p), device_id_type=MESH,
        )

    kept = pltpu.make_async_copy(send_ref.at[t], recv_ref.at[home(ng, nt, t)[1]], local_sem.at[1])

    @pl.when(gives)
    def _():
        for k in range(1, nt):
            slab(k).start()
        kept.start()

    halos = [
        send_to(edge_ref.at[0], ylo_ref, halo_s.at[0], halo_r.at[0], grp_peers[0]),
        send_to(edge_ref.at[1], yhi_ref, halo_s.at[1], halo_r.at[1], grp_peers[-1]),
        send_to(last_ref, xlo_ref, halo_s.at[2], halo_r.at[2], tile_peers[0]),
        send_to(first_ref, xhi_ref, halo_s.at[3], halo_r.at[3], tile_peers[-1]),
    ]
    mine.wait()
    for c in own_copies:
        c.wait()
    own2_copies = [
        send_to(all_ref.at[g], all_ref.at[g], own2_s.at[k], own2_r.at[k], peer)
        for k, peer in enumerate(grp_peers)
    ]
    table_ref[...] = jnp.zeros_like(table_ref)
    for c in bulk:
        c.wait()

    @pl.loop(0, pos_ref.shape[0] // 8)
    def _(k):
        at = pl.ds(pl.multiple_of(k * 8, 8), 8)
        cell = pos_ref[at, :]
        values = [mot_ref[f, at, :] for f in range(3)] + [warm_ref[at, :], mass_ref[at, :], mult_ref[at, :]]
        values += [(cell & 127).astype(F32), (cell >> 7).astype(F32)]
        for f, v in enumerate(values):
            parcel_ref[pl.ds(k * 8 * (ROW + 1) + f, 8, stride=ROW + 1), :] = v

    for c in nu_loads:
        c.wait()
    for c in halos:
        c.wait()
    sub = lax.broadcasted_iota(I32, (planes, width), 0)
    lane = lax.broadcasted_iota(I32, (planes, width), 1)
    has_low = jnp.where(t > 0, 1.0, 0.0).astype(F32)
    has_high = jnp.where(t < nt - 1, 1.0, 0.0).astype(F32)
    x_low = xlo_ref[...].astype(F32) * has_low
    x_high = xhi_ref[...].astype(F32) * has_high
    for r in range(rows):
        mid = gas_ref[r]
        below = gas_ref[r - nf] if r >= nf else ylo_ref[r].astype(F32)
        above = gas_ref[r + nf] if r < rows - nf else yhi_ref[r - (rows - nf)].astype(F32)
        total = below + above
        total += jnp.where(sub == 0, x_low[r : r + 1], pltpu.roll(mid, 1, 0))
        total += jnp.where(sub == planes - 1, x_high[r : r + 1], pltpu.roll(mid, planes - 1, 0))
        total += jnp.where(lane == 0, 0.0, pltpu.roll(mid, 1, 1))
        total += jnp.where(lane == width - 1, 0.0, pltpu.roll(mid, width - 1, 1))
        part_ref[r] = (mid + 0.5 * nu_ref[r // nf] * (total - 6.0 * mid)) * gas_side

    for c in own2_copies:
        c.wait()
    owners = jnp.concatenate([all_ref[k].reshape(nt, 128) for k in range(ng)], axis=0)
    entries, number = block_list(ng, nt, owners, pick_ref[...], live_ref[0])
    prow = entries.shape[0]
    ints_ref[0:prow, :] = entries
    ints_ref[prow : prow + 8, :] = jnp.broadcast_to(number, (8, 128))

    def unpack(d):
        for r in range(0, rows, 2):
            both = recv_ref[d, r * SLOTS : (r + 2) * SLOTS, :].astype(F32)
            for h in range(2):
                at = (r + h) // nf * 8 + (r + h) % nf
                table_ref[pl.ds(d * SLOTS * PITCH + at, SLOTS, stride=PITCH), :] = both[h * SLOTS : (h + 1) * SLOTS]

    @pl.when(gives)
    def _():
        kept.wait()

    for k in range(sources):
        from_g, from_d = source(ng, nt, k)

        @pl.when((from_g != g) | (from_d != t))
        def _():
            pltpu.make_async_remote_copy(
                src_ref=send_ref.at[0], dst_ref=recv_ref.at[k], send_sem=tile_s.at[0],
                recv_sem=tile_r.at[k], device_id=(from_g, from_d), device_id_type=MESH,
            ).wait_recv()

        unpack(k)

    @pl.when(gives)
    def _():
        for k in range(1, nt):
            slab(k).wait_send()


def parcel_kernel(
    ints_ref, table, parcels, acc, seen, par, src, add, smem, sem,
):
    to_smem = pltpu.make_async_copy(ints_ref, smem, sem)
    to_smem.start()
    blocks = parcels.shape[0] // (ROW + 1)
    shift = blocks.bit_length() - 1
    prow = blocks // 128
    span = BATCH + 1
    acc[...] = jnp.zeros_like(acc)
    src[...] = jnp.zeros_like(src)
    par[...] = jnp.zeros_like(par)
    to_smem.wait()

    n = smem[prow, 0]
    sub = lax.broadcasted_iota(I32, (128, 128), 0).astype(F32).astype(BF16)
    yes, no = jnp.ones((128, 128), BF16), jnp.zeros((128, 128), BF16)
    half = lax.broadcasted_iota(I32, (16, 128), 0) >> 3
    half = [(half + 2 * k).astype(F32).astype(BF16) for k in range(2)]
    zero = jnp.zeros((32, 128), BF16)

    @pl.loop(0, (n + BATCH - 1) // BATCH + 1)
    def _(step):
        last = jnp.maximum(step - 1, 0)
        rows = [(k // (128 // BATCH), lax.rem(k, 128 // BATCH) * BATCH) for k in (step, last)]
        for j in range(0, BATCH, 2):
            left, hot = [], []
            for i in (j, j + 1):
                z = jnp.broadcast_to(par[6 * span + i : 6 * span + i + 1, :], (16, 128)).astype(BF16)
                y = jnp.broadcast_to(par[7 * span + i : 7 * span + i + 1, :], (16, 128)).astype(BF16)
                s8 = src[pl.ds(i * 9, 8), :]
                s16 = jnp.concatenate([s8, s8], axis=0).astype(BF16)
                s32 = jnp.concatenate([jnp.where(y == h, s16, no[0:16]) for h in half], axis=0)
                left.append(jnp.concatenate([s32, zero] if i == j else [zero, s32], axis=1))
                hot.append(jnp.where(sub == jnp.concatenate([z] * 8, axis=0), yes, no))
            add[j * 32 : (j + 2) * 32, :] = lax.dot_general(
                jnp.concatenate(left, axis=0), jnp.concatenate(hot, axis=1), (((1,), (1,)), ((), ())),
                preferred_element_type=F32,
            )
            for i in (j, j + 1):
                v = smem[rows[0][0], rows[0][1] + i]
                b = (v & (blocks - 1)) * (ROW + 1)
                base = (v >> shift) * PITCH
                values = parcels[pl.ds(b, 8), :]
                z = jnp.broadcast_to(parcels[pl.ds(b + 6, 1), :], (8, 128)).astype(I32)
                y = jnp.broadcast_to(parcels[pl.ds(b + 7, 1), :], (8, 128))
                got = [
                    jnp.take_along_axis(table[pl.ds(base + k * 8, 8), :], z, axis=1) for k in range(4)
                ]
                upper = jnp.where(y < 1, got[0], got[1])
                lower = jnp.where(y < 3, got[2], got[3])
                seen[pl.ds(i, 8, stride=span), :] = jnp.where(y < 2, upper, lower)
                par[pl.ds(i, 8, stride=span), :] = values
        for i in range(BATCH):
            at = pl.ds((smem[rows[1][0], rows[1][1] + i] >> shift) * PITCH, 32)
            acc[at, :] = acc[at, :] + add[i * 32 : (i + 1) * 32, :]
        field = [seen[f * span : f * span + BATCH, :] for f in range(5)]
        v0, v1, v2, warm, mass, mult = [par[f * span : f * span + BATCH, :] for f in range(6)]
        r0, r1, r2 = field[0] - v0, field[1] - v1, field[2] - v2
        speed_sq = r0 * r0 + r1 * r1 + r2 * r2
        inv_surface = jnp.exp(jnp.log(mass) * (-2.0 / 3.0))
        inverse_tau = 0.8 * (1.0 + 0.15 * jnp.exp(0.3435 * jnp.log(1.0 + speed_sq))) * inv_surface
        relax = 1.0 - jnp.exp(-0.5 * inverse_tau)
        heating = 1.0 / (1.0 + jnp.exp(field[4] - field[3]))
        remain = jnp.exp(-0.3 * heating * inv_surface)
        new_mass = mass * remain
        warming = 1.0 - jnp.exp(-0.25 * inverse_tau)
        new_warm = warm + warming * (field[3] - warm) - 0.5 * (1.0 - remain)
        outs = [mass * v - new_mass * (v + relax * r) for v, r in ((v0, r0), (v1, r1), (v2, r2))]
        outs += [mass * warm - new_mass * new_warm, mass - new_mass]
        for f, o in enumerate(outs):
            src[pl.ds(f, BATCH, stride=9), :] = mult * o


def return_kernel(ng, nt, nf, acc_ref, recv_ref, send_ref, tile_s, tile_r, local_sem):
    g, t = lax.axis_index("grp"), lax.axis_index("tile")
    everyone_in = greet_all(ng, nt)
    sources, rows, _ = send_ref.shape
    for d in range(sources):
        for r in range(0, rows // SLOTS, 2):
            pair = [
                acc_ref[pl.ds(d * SLOTS * PITCH + q // nf * 8 + q % nf, SLOTS, stride=PITCH), :]
                for q in (r, r + 1)
            ]
            send_ref[d, r * SLOTS : (r + 2) * SLOTS, :] = jnp.concatenate(pair, axis=0).astype(BF16)
    takes = g < ng - 1

    def slab(k):
        return pltpu.make_async_remote_copy(
            src_ref=send_ref.at[k], dst_ref=recv_ref.at[t], send_sem=tile_s.at[k],
            recv_sem=tile_r.at[t], device_id=source(ng, nt, k), device_id_type=MESH,
        )

    def remote(k):
        to_g, to_d = source(ng, nt, k)
        return (to_g != g) | (to_d != t)

    everyone_in()
    for k in range(sources):

        @pl.when(remote(k))
        def _():
            slab(k).start()

    kept = pltpu.make_async_copy(send_ref.at[home(ng, nt, t)[1]], recv_ref.at[t], local_sem)

    @pl.when(takes)
    def _():
        kept.start()
        kept.wait()
        for k in range(1, nt):
            p = lax.rem(t + k, nt)
            pltpu.make_async_remote_copy(
                src_ref=send_ref.at[0], dst_ref=recv_ref.at[p], send_sem=tile_s.at[0],
                recv_sem=tile_r.at[p], device_id=(home(ng, nt, p)[0], p), device_id_type=MESH,
            ).wait_recv()

    @pl.when(jnp.logical_not(takes))
    def _():
        recv_ref[...] = jnp.zeros_like(recv_ref)

    for k in range(sources):

        @pl.when(remote(k))
        def _():
            slab(k).wait_send()


def place_kernel(ng, nt, nf, recv_ref, placer_ref, part_ref, out_hbm, buf, sem):
    rows, planes, width = part_ref.shape
    gas_side = lax.axis_index("grp") < ng - 1
    placer = placer_ref[...]
    copies = []
    for r in range(0, rows, 2):
        inc = jnp.concatenate([recv_ref[d, r * SLOTS : (r + 2) * SLOTS, :] for d in range(nt)], axis=0)
        placed = jnp.dot(placer, inc, preferred_element_type=F32)
        for h in range(2):
            q = r + h
            buf[q] = part_ref[q] + jnp.where(gas_side, placed[h * planes : (h + 1) * planes], 0.0)
            c = pltpu.make_async_copy(buf.at[q], out_hbm.at[q % nf, :, q // nf, :], sem.at[q])
            c.start()
            copies.append(c)
    for c in copies:
        c.wait()


def local(
    flow_fields, turbulent_diffusivity, holder_unit, spray_volume_position, patch_pick_unreduced,
    droplet_motion, droplet_warmth, droplet_weightiness, droplet_multiplicity, living_spray_batches,
):
    ng, nt = lax.axis_size("grp"), lax.axis_size("tile")
    nf, planes, rows_y, width = flow_fields.shape
    rows = nf * rows_y
    dma = pltpu.SemaphoreType.DMA
    shape = jax.ShapeDtypeStruct
    blocks = spray_volume_position.shape[1]
    sources = nt * (SHARE - 1) // SHARE
    slots = sources * SLOTS
    prow = blocks // 128
    slab = (nt, rows * SLOTS, width)
    gas = (rows, planes, width)
    table, ints, part, placer, parcels = pl.pallas_call(
        functools.partial(gas_kernel, ng, nt, nf),
        out_shape=(
            shape(((slots + 1) * PITCH + 7, width), F32), shape((prow + 8, 128), I32), shape(gas, F32),
            shape((2 * planes, nt * 2 * SLOTS), BF16), shape((blocks * (ROW + 1), 128), F32),
        ),
        in_specs=[SMEM] + [HBM] * 9, out_specs=(VMEM,) * 5,
        scratch_shapes=[
            pltpu.VMEM((blocks, 128), I32), pltpu.VMEM((3, blocks, 128), F32),
            pltpu.VMEM((blocks, 128), F32), pltpu.VMEM((blocks, 128), F32), pltpu.VMEM((blocks, 128), F32),
            pltpu.VMEM((1, planes), I32), pltpu.VMEM((prow, 128), I32),
            pltpu.VMEM((rows_y, planes, width), F32), pltpu.VMEM(gas, F32),
            pltpu.VMEM((1, 1, 128), I32), pltpu.VMEM((1, 128), I32), pltpu.VMEM((ng, nt, 1, 128), I32),
            pltpu.VMEM(slab, BF16), pltpu.VMEM((sources,) + slab[1:], BF16),
            pltpu.VMEM((2, nf, planes, width), BF16),
            pltpu.VMEM((nf, planes, width), BF16), pltpu.VMEM((nf, planes, width), BF16),
            pltpu.VMEM((rows, width), BF16), pltpu.VMEM((rows, width), BF16),
            pltpu.VMEM((rows, width), BF16), pltpu.VMEM((rows, width), BF16),
            dma((2,)), dma((rows,)), dma((rows_y,)), dma((7,)),
            dma((nt,)), dma((sources,)), dma((nt - 1,)), dma((nt - 1,)),
            dma((ng - 1,)), dma((ng - 1,)), dma((4,)), dma((4,)), dma((2,)),
        ],
        compiler_params=pltpu.CompilerParams(
            collective_id=0, has_side_effects=True, vmem_limit_bytes=24 << 20
        ),
        name="gas",
    )(living_spray_batches, *(pltpu.with_memory_space_constraint(a, pltpu.MemorySpace.HBM) for a in (
        holder_unit.reshape(1, planes), flow_fields, turbulent_diffusivity,
        patch_pick_unreduced.reshape(prow, 128), spray_volume_position[0],
        droplet_motion[0].transpose(1, 0, 2), droplet_warmth[0], droplet_weightiness[0],
        droplet_multiplicity[0],
    )))
    acc = pl.pallas_call(
        parcel_kernel,
        out_shape=shape(((slots + 1) * PITCH + 7, width), F32),
        in_specs=[VMEM] * 3, out_specs=VMEM,
        scratch_shapes=[
            pltpu.VMEM((8 * (BATCH + 1), width), F32),
            pltpu.VMEM((8 * (BATCH + 1), width), F32),
            pltpu.VMEM((BATCH * 9, width), F32),
            pltpu.VMEM((BATCH * 32, width), F32),
            pltpu.SMEM((prow + 8, 128), I32),
            dma,
        ],
        compiler_params=pltpu.CompilerParams(vmem_limit_bytes=24 << 20),
        name="parcels",
    )(ints, table, parcels)
    recv = pl.pallas_call(
        functools.partial(return_kernel, ng, nt, nf),
        out_shape=shape(slab, BF16),
        in_specs=[VMEM], out_specs=VMEM,
        scratch_shapes=[
            pltpu.VMEM((sources,) + slab[1:], BF16), dma((sources,)), dma((nt,)), dma,
        ],
        compiler_params=pltpu.CompilerParams(
            collective_id=1, has_side_effects=True, vmem_limit_bytes=16 << 20
        ),
        name="return",
    )(acc)
    return pl.pallas_call(
        functools.partial(place_kernel, ng, nt, nf),
        out_shape=shape((nf, planes, rows_y, width), F32),
        in_specs=[VMEM] * 3, out_specs=HBM,
        scratch_shapes=[pltpu.VMEM(gas, F32), dma((rows,))],
        compiler_params=pltpu.CompilerParams(vmem_limit_bytes=12 << 20),
        name="place",
    )(recv, placer, part)


def solution(mesh):
    in_specs = (
        P(None, "tile", "grp", None),
        P("tile", "grp", None),
        P("grp", "tile", None),
        P("tile", None, None),
        P("tile", None),
        P("tile", None, None, None),
        P("tile", None, None),
        P("tile", None, None),
        P("tile", None, None),
        P("tile"),
    )
    out_specs = P(None, "tile", "grp", None)
    return jax.shard_map(local, mesh=mesh, in_specs=in_specs, out_specs=out_specs, check_vma=False)
```

```python
import functools

import jax
import jax.numpy as jnp
from jax import lax
from jax.experimental import pallas as pl
from jax.experimental.pallas import tpu as pltpu
from jax.sharding import PartitionSpec as P

MESH = pl.DeviceIdType.MESH
SLOTS = 8
BATCH = 64
HBM = pl.BlockSpec(memory_space=pltpu.MemorySpace.HBM)
VMEM = pl.BlockSpec(memory_space=pltpu.VMEM)
SMEM = pl.BlockSpec(memory_space=pltpu.SMEM)
F32, BF16, I32 = jnp.float32, jnp.bfloat16, jnp.int32


ROW = 8
PITCH = 33
SHARE = 4


def say_in(peer):
    pl.semaphore_signal(pltpu.get_barrier_semaphore(), inc=1, device_id=peer, device_id_type=MESH)


def source(ng, nt, s):
    g, p = lax.axis_index("grp"), lax.axis_index("tile")
    spare = g == ng - 1
    e = jnp.where(spare, s // (ng - 1) * SHARE + SHARE - 1, s + s // (SHARE - 1))
    return jnp.where(spare, lax.rem(s, ng - 1), g), lax.rem(e - p + nt, nt)


def home(ng, nt, p):
    g = lax.axis_index("grp")
    e = lax.rem(lax.axis_index("tile") + p, nt)
    shared = lax.rem(e, SHARE) == SHARE - 1
    return jnp.where(shared, ng - 1, g), jnp.where(shared, e // SHARE * (ng - 1) + g, e - e // SHARE)


def send_to(src, dst, ss, rs, dev):
    c = pltpu.make_async_remote_copy(
        src_ref=src, dst_ref=dst, send_sem=ss, recv_sem=rs, device_id=dev, device_id_type=MESH
    )
    c.start()
    return c


def start_all(pairs, sems):
    loads = [pltpu.make_async_copy(a, b, sems.at[k]) for k, (a, b) in enumerate(pairs)]
    for c in loads:
        c.start()
    return loads


def block_list(ng, nt, owners, pick, live):
    p = lax.axis_index("tile")
    prow = pick.shape[0]
    shift = (prow * 128).bit_length() - 1
    sources = nt * (SHARE - 1) // SHARE
    slots = sources * SLOTS
    owned = jnp.where(owners == p, 1, 0)
    counts = jnp.sum(owned, axis=1, keepdims=True)
    which = lax.broadcasted_iota(I32, counts.shape, 0)
    counts = jnp.where(which < (ng - 1) * nt, counts, 0)
    total = jnp.maximum(jnp.sum(counts, axis=0, keepdims=True), 1)
    total_f = total.astype(F32)
    quotient = jnp.floor(pick.astype(F32) / total_f).astype(I32)
    left = pick - quotient * total
    left = jnp.where(left < 0, left + total, left)
    left = jnp.where(left >= total, left - total, left)
    slot = jnp.full(pick.shape, -1, I32)
    for k in range(sources):
        from_g, from_d = source(ng, nt, k)
        number = from_g * nt + from_d
        low = jnp.sum(jnp.where(which < number, counts, 0), axis=0, keepdims=True)
        size = jnp.sum(jnp.where(which == number, counts, 0), axis=0, keepdims=True)
        rank = left - low
        slot = jnp.where((rank >= 0) & (rank < size), rank + k * SLOTS, slot)
    row = lax.broadcasted_iota(I32, (prow, 128), 0)
    lane = lax.broadcasted_iota(I32, (prow, 128), 1)
    number = row * 128 + lane
    inside = (slot >= 0) & (number < live)
    flags = jnp.where(inside, 1, 0)
    square_a = lax.broadcasted_iota(I32, (128, 128), 0)
    square_b = lax.broadcasted_iota(I32, (128, 128), 1)
    before = jnp.where(square_a < square_b, 1.0, 0.0).astype(BF16)
    flags_low = flags.astype(F32).astype(BF16)
    place = jnp.dot(flags_low, before, preferred_element_type=F32).astype(I32)
    sums = jnp.sum(flags, axis=1, keepdims=True)
    start = jnp.zeros((1, 1), I32)
    listed = jnp.zeros((3 * prow, 128), F32)
    lane_f, slot_f = lane[0:1].astype(F32), slot.astype(F32)
    for i in range(prow):
        at = jnp.where(inside[i : i + 1], place[i : i + 1] + start, -1)
        goes = row == (at >> 7)
        parts = [
            jnp.where(goes, v, 0.0) for v in (slot_f[i : i + 1], jnp.full((1, 128), float(i), F32), lane_f)
        ]
        spot = jnp.where(square_a == (at & 127), 1.0, 0.0).astype(BF16)
        listed += lax.dot_general(
            jnp.concatenate(parts, axis=0).astype(BF16), spot, (((1,), (1,)), ((), ())),
            preferred_element_type=F32,
        )
        start = start + sums[i : i + 1]
    listed = listed.astype(I32)
    entry = (listed[0:prow] << shift) + listed[prow : 2 * prow] * 128 + listed[2 * prow :]
    return jnp.where(number < start, entry, slots << shift), start


def gas_kernel(
    ng, nt, nf, live_ref, holder_hbm, flow_hbm, nu_hbm, pick_hbm, pos_hbm, mot_hbm, warm_hbm, mass_hbm, mult_hbm,
    table_ref, ints_ref, part_ref, placer_ref, parcel_ref,
    pos_ref, mot_ref, warm_ref, mass_ref, mult_ref, holder_ref, pick_ref, nu_ref, gas_ref, own_ref, twice_ref, all_ref, send_ref, recv_ref,
    edge_ref, ylo_ref, yhi_ref, first_ref, last_ref, xlo_ref, xhi_ref,
    small_sem, gas_sem, nu_sem, bulk_sem, tile_s, tile_r, own_s, own_r, own2_s, own2_r, halo_s, halo_r, local_sem,
):
    g, t = lax.axis_index("grp"), lax.axis_index("tile")
    rows, planes, width = gas_ref.shape
    rows_y = rows // nf
    sources = recv_ref.shape[0]
    small = start_all([(holder_hbm, holder_ref), (pick_hbm, pick_ref)], small_sem)
    gas_loads = start_all([(flow_hbm.at[q % nf, :, q // nf, :], gas_ref.at[q]) for q in range(rows)], gas_sem)
    nu_loads = start_all([(nu_hbm.at[:, y, :], nu_ref.at[y]) for y in range(rows_y)], nu_sem)
    grp_peers = [(lax.rem(g + k, ng), t) for k in range(1, ng)]
    tile_peers = [(g, lax.rem(t + k, nt)) for k in range(1, nt)]
    for peer in grp_peers + tile_peers:
        say_in(peer)

    @pl.when(g == ng - 1)
    def _():
        for k in range(sources):
            say_in(source(ng, nt, k))

    targets = ng + nt - 2 + jnp.where(g < ng - 1, nt // SHARE, 0)
    pairs = [(pos_hbm, pos_ref), (warm_hbm, warm_ref), (mass_hbm, mass_ref), (mult_hbm, mult_ref)]
    pairs += [(mot_hbm.at[f], mot_ref.at[f]) for f in range(3)]
    bulk = start_all(pairs, bulk_sem)

    own_ref[0] = jnp.full((1, 128), -1, I32)
    twice_ref[...] = jnp.full((1, 128), -1, I32)
    for c in small:
        c.wait()
    own_ref[0, :, 0:planes] = holder_ref[...]
    own = own_ref[0]
    twice_ref[:, 0:planes] = holder_ref[...]
    twice_ref[:, planes : 2 * planes] = holder_ref[...]
    both = twice_ref[...]
    row = jnp.broadcast_to(both, (128, 128))
    col = row.T
    s = lax.broadcasted_iota(I32, (128, 128), 0)
    l = lax.broadcasted_iota(I32, (128, 128), 1)
    near = (col == row) & ((s >= planes) == (l >= planes))
    rank = jnp.sum(jnp.where(near & (s < l), 1, 0), axis=0, keepdims=True)
    rank_col = jnp.sum(jnp.where(near & (l < s), 1, 0), axis=1, keepdims=True)
    lanes = lax.broadcasted_iota(I32, (1, 128), 1)
    subs = lax.broadcasted_iota(I32, (128, 1), 0)
    goal = both * (2 * SLOTS) + rank + jnp.where(lanes >= planes, SLOTS, 0)
    goal_col = col[:, 0:1] * (2 * SLOTS) + rank_col + jnp.where(subs >= planes, SLOTS, 0)
    picker = jnp.where(
        goal[:, 0 : 2 * planes] == lax.broadcasted_iota(I32, (nt * 2 * SLOTS, 2 * planes), 0), 1.0, 0.0
    ).astype(BF16)
    placer_ref[...] = jnp.where(
        goal_col[0 : 2 * planes] == lax.broadcasted_iota(I32, (2 * planes, nt * 2 * SLOTS), 1), 1.0, 0.0
    ).astype(BF16)
    gas_side = jnp.where(g < ng - 1, 1.0, 0.0).astype(F32)
    for r in range(0, rows, 2):
        two = []
        for q in (r, r + 1):
            gas_loads[q].wait()
            cells = gas_ref[q] * gas_side
            gas_ref[q] = cells
            two.append(cells)
        low = jnp.concatenate(two, axis=0).astype(BF16)
        got = jnp.dot(picker, low, preferred_element_type=F32).astype(BF16)
        for o in range(nt):
            send_ref[o, r * SLOTS : (r + 2) * SLOTS, :] = got[o * 2 * SLOTS : (o + 1) * 2 * SLOTS]
    edge_ref[0] = gas_ref[rows - nf : rows].astype(BF16)
    edge_ref[1] = gas_ref[0:nf].astype(BF16)
    first_ref[...] = gas_ref[:, 0, :].astype(BF16)
    last_ref[...] = gas_ref[:, planes - 1, :].astype(BF16)

    pl.semaphore_wait(pltpu.get_barrier_semaphore(), targets)
    own_copies = [
        send_to(own_ref.at[0], all_ref.at[g, t], own_s.at[k], own_r.at[k], peer)
        for k, peer in enumerate(tile_peers)
    ]
    mine = pltpu.make_async_copy(own_ref.at[0], all_ref.at[g, t], local_sem.at[0])
    mine.start()
    gives = g < ng - 1

    def slab(k):
        p = lax.rem(t + k, nt)
        to_g, at = home(ng, nt, p)
        return pltpu.make_async_remote_copy(
            src_ref=send_ref.at[p], dst_ref=recv_ref.at[at], send_sem=tile_s.at[k],
            recv_sem=tile_r.at[at], device_id=(to_g, p), device_id_type=MESH,
        )

    kept = pltpu.make_async_copy(send_ref.at[t], recv_ref.at[home(ng, nt, t)[1]], local_sem.at[1])

    @pl.when(gives)
    def _():
        for k in range(1, nt):
            slab(k).start()
        kept.start()

    halos = [
        send_to(edge_ref.at[0], ylo_ref, halo_s.at[0], halo_r.at[0], grp_peers[0]),
        send_to(edge_ref.at[1], yhi_ref, halo_s.at[1], halo_r.at[1], grp_peers[-1]),
        send_to(last_ref, xlo_ref, halo_s.at[2], halo_r.at[2], tile_peers[0]),
        send_to(first_ref, xhi_ref, halo_s.at[3], halo_r.at[3], tile_peers[-1]),
    ]
    mine.wait()
    for c in own_copies:
        c.wait_recv()
    own2_copies = [
        send_to(all_ref.at[g], all_ref.at[g], own2_s.at[k], own2_r.at[k], peer)
        for k, peer in enumerate(grp_peers)
    ]
    table_ref[...] = jnp.zeros_like(table_ref)
    for c in bulk:
        c.wait()

    @pl.loop(0, pos_ref.shape[0] // 8)
    def _(k):
        at = pl.ds(pl.multiple_of(k * 8, 8), 8)
        cell = pos_ref[at, :]
        values = [mot_ref[f, at, :] for f in range(3)] + [warm_ref[at, :], mass_ref[at, :], mult_ref[at, :]]
        values += [(cell & 127).astype(F32), (cell >> 7).astype(F32)]
        for f, v in enumerate(values):
            parcel_ref[pl.ds(k * 8 * (ROW + 1) + f, 8, stride=ROW + 1), :] = v

    for c in nu_loads:
        c.wait()
    for c in halos:
        c.wait_recv()
    sub = lax.broadcasted_iota(I32, (planes, width), 0)
    lane = lax.broadcasted_iota(I32, (planes, width), 1)
    has_low = jnp.where(t > 0, 1.0, 0.0).astype(F32)
    has_high = jnp.where(t < nt - 1, 1.0, 0.0).astype(F32)
    x_low = xlo_ref[...].astype(F32) * has_low
    x_high = xhi_ref[...].astype(F32) * has_high
    for r in range(rows):
        mid = gas_ref[r]
        below = gas_ref[r - nf] if r >= nf else ylo_ref[r].astype(F32)
        above = gas_ref[r + nf] if r < rows - nf else yhi_ref[r - (rows - nf)].astype(F32)
        total = below + above
        total += jnp.where(sub == 0, x_low[r : r + 1], pltpu.roll(mid, 1, 0))
        total += jnp.where(sub == planes - 1, x_high[r : r + 1], pltpu.roll(mid, planes - 1, 0))
        total += jnp.where(lane == 0, 0.0, pltpu.roll(mid, 1, 1))
        total += jnp.where(lane == width - 1, 0.0, pltpu.roll(mid, width - 1, 1))
        part_ref[r] = (mid + 0.5 * nu_ref[r // nf] * (total - 6.0 * mid)) * gas_side

    for c in own2_copies:
        c.wait_recv()
    owners = jnp.concatenate([all_ref[k].reshape(nt, 128) for k in range(ng)], axis=0)
    entries, number = block_list(ng, nt, owners, pick_ref[...], live_ref[0])
    prow = entries.shape[0]
    ints_ref[0:prow, :] = entries
    ints_ref[prow : prow + 8, :] = jnp.broadcast_to(number, (8, 128))

    def unpack(d):
        for r in range(0, rows, 2):
            both = recv_ref[d, r * SLOTS : (r + 2) * SLOTS, :].astype(F32)
            for h in range(2):
                at = (r + h) // nf * 8 + (r + h) % nf
                table_ref[pl.ds(d * SLOTS * PITCH + at, SLOTS, stride=PITCH), :] = both[h * SLOTS : (h + 1) * SLOTS]

    @pl.when(gives)
    def _():
        kept.wait()

    for k in range(sources):
        from_g, from_d = source(ng, nt, k)

        @pl.when((from_g != g) | (from_d != t))
        def _():
            pltpu.make_async_remote_copy(
                src_ref=send_ref.at[0], dst_ref=recv_ref.at[k], send_sem=tile_s.at[0],
                recv_sem=tile_r.at[k], device_id=(from_g, from_d), device_id_type=MESH,
            ).wait_recv()

        unpack(k)

    @pl.when(gives)
    def _():
        for k in range(1, nt):
            slab(k).wait_send()
    for c in own_copies + own2_copies + halos:
        c.wait_send()


def parcel_kernel(
    ints_ref, table, parcels, acc, seen, par, src, add, smem, sem,
):
    to_smem = pltpu.make_async_copy(ints_ref, smem, sem)
    to_smem.start()
    blocks = parcels.shape[0] // (ROW + 1)
    shift = blocks.bit_length() - 1
    prow = blocks // 128
    span = BATCH + 1
    acc[...] = jnp.zeros_like(acc)
    src[...] = jnp.zeros_like(src)
    par[...] = jnp.zeros_like(par)
    to_smem.wait()

    n = smem[prow, 0]
    sub = lax.broadcasted_iota(I32, (128, 128), 0).astype(F32).astype(BF16)
    yes, no = jnp.ones((128, 128), BF16), jnp.zeros((128, 128), BF16)
    half = lax.broadcasted_iota(I32, (16, 128), 0) >> 3
    half = [(half + 2 * k).astype(F32).astype(BF16) for k in range(2)]
    zero = jnp.zeros((32, 128), BF16)

    @pl.loop(0, (n + BATCH - 1) // BATCH + 1)
    def _(step):
        last = jnp.maximum(step - 1, 0)
        rows = [(k // (128 // BATCH), lax.rem(k, 128 // BATCH) * BATCH) for k in (step, last)]
        for j in range(0, BATCH, 2):
            left, hot = [], []
            for i in (j, j + 1):
                z = jnp.broadcast_to(par[6 * span + i : 6 * span + i + 1, :], (16, 128)).astype(BF16)
                y = jnp.broadcast_to(par[7 * span + i : 7 * span + i + 1, :], (16, 128)).astype(BF16)
                s8 = src[pl.ds(i * 9, 8), :]
                s16 = jnp.concatenate([s8, s8], axis=0).astype(BF16)
                s32 = jnp.concatenate([jnp.where(y == h, s16, no[0:16]) for h in half], axis=0)
                left.append(jnp.concatenate([s32, zero] if i == j else [zero, s32], axis=1))
                hot.append(jnp.where(sub == jnp.concatenate([z] * 8, axis=0), yes, no))
            add[j * 32 : (j + 2) * 32, :] = lax.dot_general(
                jnp.concatenate(left, axis=0), jnp.concatenate(hot, axis=1), (((1,), (1,)), ((), ())),
                preferred_element_type=F32,
            )
            for i in (j, j + 1):
                v = smem[rows[0][0], rows[0][1] + i]
                b = (v & (blocks - 1)) * (ROW + 1)
                base = (v >> shift) * PITCH
                values = parcels[pl.ds(b, 8), :]
                z = jnp.broadcast_to(parcels[pl.ds(b + 6, 1), :], (8, 128)).astype(I32)
                y = jnp.broadcast_to(parcels[pl.ds(b + 7, 1), :], (8, 128))
                got = [
                    jnp.take_along_axis(table[pl.ds(base + k * 8, 8), :], z, axis=1) for k in range(4)
                ]
                upper = jnp.where(y < 1, got[0], got[1])
                lower = jnp.where(y < 3, got[2], got[3])
                seen[pl.ds(i, 8, stride=span), :] = jnp.where(y < 2, upper, lower)
                par[pl.ds(i, 8, stride=span), :] = values
        for i in range(BATCH):
            at = pl.ds((smem[rows[1][0], rows[1][1] + i] >> shift) * PITCH, 32)
            acc[at, :] = acc[at, :] + add[i * 32 : (i + 1) * 32, :]
        field = [seen[f * span : f * span + BATCH, :] for f in range(5)]
        v0, v1, v2, warm, mass, mult = [par[f * span : f * span + BATCH, :] for f in range(6)]
        r0, r1, r2 = field[0] - v0, field[1] - v1, field[2] - v2
        speed_sq = r0 * r0 + r1 * r1 + r2 * r2
        inv_surface = jnp.exp(jnp.log(mass) * (-2.0 / 3.0))
        inverse_tau = 0.8 * (1.0 + 0.15 * jnp.exp(0.3435 * jnp.log(1.0 + speed_sq))) * inv_surface
        relax = 1.0 - jnp.exp(-0.5 * inverse_tau)
        heating = 1.0 / (1.0 + jnp.exp(field[4] - field[3]))
        remain = jnp.exp(-0.3 * heating * inv_surface)
        new_mass = mass * remain
        warming = 1.0 - jnp.exp(-0.25 * inverse_tau)
        new_warm = warm + warming * (field[3] - warm) - 0.5 * (1.0 - remain)
        outs = [mass * v - new_mass * (v + relax * r) for v, r in ((v0, r0), (v1, r1), (v2, r2))]
        outs += [mass * warm - new_mass * new_warm, mass - new_mass]
        for f, o in enumerate(outs):
            src[pl.ds(f, BATCH, stride=9), :] = mult * o


def return_kernel(ng, nt, nf, acc_ref, recv_ref, send_ref, tile_s, tile_r, local_sem):
    g, t = lax.axis_index("grp"), lax.axis_index("tile")
    sources, rows, _ = send_ref.shape
    takes = g < ng - 1

    @pl.when(takes)
    def _():
        for k in range(1, nt):
            p = lax.rem(t + k, nt)
            say_in((home(ng, nt, p)[0], p))

    for d in range(sources):
        for r in range(0, rows // SLOTS, 2):
            pair = [
                acc_ref[pl.ds(d * SLOTS * PITCH + q // nf * 8 + q % nf, SLOTS, stride=PITCH), :]
                for q in (r, r + 1)
            ]
            send_ref[d, r * SLOTS : (r + 2) * SLOTS, :] = jnp.concatenate(pair, axis=0).astype(BF16)
    def slab(k):
        return pltpu.make_async_remote_copy(
            src_ref=send_ref.at[k], dst_ref=recv_ref.at[t], send_sem=tile_s.at[k],
            recv_sem=tile_r.at[t], device_id=source(ng, nt, k), device_id_type=MESH,
        )

    def remote(k):
        to_g, to_d = source(ng, nt, k)
        return (to_g != g) | (to_d != t)

    pl.semaphore_wait(pltpu.get_barrier_semaphore(), sources - jnp.where(takes, 1, 0))
    for k in range(sources):

        @pl.when(remote(k))
        def _():
            slab(k).start()

    kept = pltpu.make_async_copy(send_ref.at[home(ng, nt, t)[1]], recv_ref.at[t], local_sem)

    @pl.when(takes)
    def _():
        kept.start()
        kept.wait()
        for k in range(1, nt):
            p = lax.rem(t + k, nt)
            pltpu.make_async_remote_copy(
                src_ref=send_ref.at[0], dst_ref=recv_ref.at[p], send_sem=tile_s.at[0],
                recv_sem=tile_r.at[p], device_id=(home(ng, nt, p)[0], p), device_id_type=MESH,
            ).wait_recv()

    @pl.when(jnp.logical_not(takes))
    def _():
        recv_ref[...] = jnp.zeros_like(recv_ref)

    for k in range(sources):

        @pl.when(remote(k))
        def _():
            slab(k).wait_send()


def place_kernel(ng, nt, nf, recv_ref, placer_ref, part_ref, out_hbm, buf, sem):
    rows, planes, width = part_ref.shape
    gas_side = lax.axis_index("grp") < ng - 1
    placer = placer_ref[...]
    copies = []
    for r in range(0, rows, 2):
        inc = jnp.concatenate([recv_ref[d, r * SLOTS : (r + 2) * SLOTS, :] for d in range(nt)], axis=0)
        placed = jnp.dot(placer, inc, preferred_element_type=F32)
        for h in range(2):
            q = r + h
            buf[q] = part_ref[q] + jnp.where(gas_side, placed[h * planes : (h + 1) * planes], 0.0)
            c = pltpu.make_async_copy(buf.at[q], out_hbm.at[q % nf, :, q // nf, :], sem.at[q])
            c.start()
            copies.append(c)
    for c in copies:
        c.wait()


def local(
    flow_fields, turbulent_diffusivity, holder_unit, spray_volume_position, patch_pick_unreduced,
    droplet_motion, droplet_warmth, droplet_weightiness, droplet_multiplicity, living_spray_batches,
):
    ng, nt = lax.axis_size("grp"), lax.axis_size("tile")
    nf, planes, rows_y, width = flow_fields.shape
    rows = nf * rows_y
    dma = pltpu.SemaphoreType.DMA
    shape = jax.ShapeDtypeStruct
    blocks = spray_volume_position.shape[1]
    sources = nt * (SHARE - 1) // SHARE
    slots = sources * SLOTS
    prow = blocks // 128
    slab = (nt, rows * SLOTS, width)
    gas = (rows, planes, width)
    table, ints, part, placer, parcels = pl.pallas_call(
        functools.partial(gas_kernel, ng, nt, nf),
        out_shape=(
            shape(((slots + 1) * PITCH + 7, width), F32), shape((prow + 8, 128), I32), shape(gas, F32),
            shape((2 * planes, nt * 2 * SLOTS), BF16), shape((blocks * (ROW + 1), 128), F32),
        ),
        in_specs=[SMEM] + [HBM] * 9, out_specs=(VMEM,) * 5,
        scratch_shapes=[
            pltpu.VMEM((blocks, 128), I32), pltpu.VMEM((3, blocks, 128), F32),
            pltpu.VMEM((blocks, 128), F32), pltpu.VMEM((blocks, 128), F32), pltpu.VMEM((blocks, 128), F32),
            pltpu.VMEM((1, planes), I32), pltpu.VMEM((prow, 128), I32),
            pltpu.VMEM((rows_y, planes, width), F32), pltpu.VMEM(gas, F32),
            pltpu.VMEM((1, 1, 128), I32), pltpu.VMEM((1, 128), I32), pltpu.VMEM((ng, nt, 1, 128), I32),
            pltpu.VMEM(slab, BF16), pltpu.VMEM((sources,) + slab[1:], BF16),
            pltpu.VMEM((2, nf, planes, width), BF16),
            pltpu.VMEM((nf, planes, width), BF16), pltpu.VMEM((nf, planes, width), BF16),
            pltpu.VMEM((rows, width), BF16), pltpu.VMEM((rows, width), BF16),
            pltpu.VMEM((rows, width), BF16), pltpu.VMEM((rows, width), BF16),
            dma((2,)), dma((rows,)), dma((rows_y,)), dma((7,)),
            dma((nt,)), dma((sources,)), dma((nt - 1,)), dma((nt - 1,)),
            dma((ng - 1,)), dma((ng - 1,)), dma((4,)), dma((4,)), dma((2,)),
        ],
        compiler_params=pltpu.CompilerParams(
            collective_id=0, has_side_effects=True, vmem_limit_bytes=24 << 20
        ),
        name="gas",
    )(living_spray_batches, *(pltpu.with_memory_space_constraint(a, pltpu.MemorySpace.HBM) for a in (
        holder_unit.reshape(1, planes), flow_fields, turbulent_diffusivity,
        patch_pick_unreduced.reshape(prow, 128), spray_volume_position[0],
        droplet_motion[0].transpose(1, 0, 2), droplet_warmth[0], droplet_weightiness[0],
        droplet_multiplicity[0],
    )))
    acc = pl.pallas_call(
        parcel_kernel,
        out_shape=shape(((slots + 1) * PITCH + 7, width), F32),
        in_specs=[VMEM] * 3, out_specs=VMEM,
        scratch_shapes=[
            pltpu.VMEM((8 * (BATCH + 1), width), F32),
            pltpu.VMEM((8 * (BATCH + 1), width), F32),
            pltpu.VMEM((BATCH * 9, width), F32),
            pltpu.VMEM((BATCH * 32, width), F32),
            pltpu.SMEM((prow + 8, 128), I32),
            dma,
        ],
        compiler_params=pltpu.CompilerParams(vmem_limit_bytes=24 << 20),
        name="parcels",
    )(ints, table, parcels)
    recv = pl.pallas_call(
        functools.partial(return_kernel, ng, nt, nf),
        out_shape=shape(slab, BF16),
        in_specs=[VMEM], out_specs=VMEM,
        scratch_shapes=[
            pltpu.VMEM((sources,) + slab[1:], BF16), dma((sources,)), dma((nt,)), dma,
        ],
        compiler_params=pltpu.CompilerParams(
            collective_id=1, has_side_effects=True, vmem_limit_bytes=16 << 20
        ),
        name="return",
    )(acc)
    return pl.pallas_call(
        functools.partial(place_kernel, ng, nt, nf),
        out_shape=shape((nf, planes, rows_y, width), F32),
        in_specs=[VMEM] * 3, out_specs=HBM,
        scratch_shapes=[pltpu.VMEM(gas, F32), dma((rows,))],
        compiler_params=pltpu.CompilerParams(vmem_limit_bytes=12 << 20),
        name="place",
    )(recv, placer, part)


def solution(mesh):
    in_specs = (
        P(None, "tile", "grp", None),
        P("tile", "grp", None),
        P("grp", "tile", None),
        P("tile", None, None),
        P("tile", None),
        P("tile", None, None, None),
        P("tile", None, None),
        P("tile", None, None),
        P("tile", None, None),
        P("tile"),
    )
    out_specs = P(None, "tile", "grp", None)
    return jax.shard_map(local, mesh=mesh, in_specs=in_specs, out_specs=out_specs, check_vma=False)
```

```python
import functools

import jax
import jax.numpy as jnp
from jax import lax
from jax.experimental import pallas as pl
from jax.experimental.pallas import tpu as pltpu
from jax.sharding import PartitionSpec as P

MESH = pl.DeviceIdType.MESH
SLOTS = 8
BATCH = 64
HBM = pl.BlockSpec(memory_space=pltpu.MemorySpace.HBM)
VMEM = pl.BlockSpec(memory_space=pltpu.VMEM)
SMEM = pl.BlockSpec(memory_space=pltpu.SMEM)
F32, BF16, I32 = jnp.float32, jnp.bfloat16, jnp.int32


ROW = 8
PITCH = 33
SHARE = 4


def say_in(peer):
    pl.semaphore_signal(pltpu.get_barrier_semaphore(), inc=1, device_id=peer, device_id_type=MESH)


def source(ng, nt, s):
    g, p = lax.axis_index("grp"), lax.axis_index("tile")
    spare = g == ng - 1
    e = jnp.where(spare, s // (ng - 1) * SHARE + SHARE - 1, s + s // (SHARE - 1))
    return jnp.where(spare, lax.rem(s, ng - 1), g), lax.rem(e - p + nt, nt)


def home(ng, nt, p):
    g = lax.axis_index("grp")
    e = lax.rem(lax.axis_index("tile") + p, nt)
    shared = lax.rem(e, SHARE) == SHARE - 1
    return jnp.where(shared, ng - 1, g), jnp.where(shared, e // SHARE * (ng - 1) + g, e - e // SHARE)


def send_to(src, dst, ss, rs, dev):
    c = pltpu.make_async_remote_copy(
        src_ref=src, dst_ref=dst, send_sem=ss, recv_sem=rs, device_id=dev, device_id_type=MESH
    )
    c.start()
    return c


def start_all(pairs, sems):
    loads = [pltpu.make_async_copy(a, b, sems.at[k]) for k, (a, b) in enumerate(pairs)]
    for c in loads:
        c.start()
    return loads


def block_list(ng, nt, owners, pick, live):
    p = lax.axis_index("tile")
    prow = pick.shape[0]
    shift = (prow * 128).bit_length() - 1
    sources = nt * (SHARE - 1) // SHARE
    slots = sources * SLOTS
    owned = jnp.where(owners == p, 1, 0)
    counts = jnp.sum(owned, axis=1, keepdims=True)
    which = lax.broadcasted_iota(I32, counts.shape, 0)
    counts = jnp.where(which < (ng - 1) * nt, counts, 0)
    total = jnp.maximum(jnp.sum(counts, axis=0, keepdims=True), 1)
    total_f = total.astype(F32)
    quotient = jnp.floor(pick.astype(F32) / total_f).astype(I32)
    left = pick - quotient * total
    left = jnp.where(left < 0, left + total, left)
    left = jnp.where(left >= total, left - total, left)
    slot = jnp.full(pick.shape, -1, I32)
    for k in range(sources):
        from_g, from_d = source(ng, nt, k)
        number = from_g * nt + from_d
        low = jnp.sum(jnp.where(which < number, counts, 0), axis=0, keepdims=True)
        size = jnp.sum(jnp.where(which == number, counts, 0), axis=0, keepdims=True)
        rank = left - low
        slot = jnp.where((rank >= 0) & (rank < size), rank + k * SLOTS, slot)
    row = lax.broadcasted_iota(I32, (prow, 128), 0)
    lane = lax.broadcasted_iota(I32, (prow, 128), 1)
    number = row * 128 + lane
    inside = (slot >= 0) & (number < live)
    flags = jnp.where(inside, 1, 0)
    square_a = lax.broadcasted_iota(I32, (128, 128), 0)
    square_b = lax.broadcasted_iota(I32, (128, 128), 1)
    before = jnp.where(square_a < square_b, 1.0, 0.0).astype(BF16)
    flags_low = flags.astype(F32).astype(BF16)
    place = jnp.dot(flags_low, before, preferred_element_type=F32).astype(I32)
    sums = jnp.sum(flags, axis=1, keepdims=True)
    start = jnp.zeros((1, 1), I32)
    listed = jnp.zeros((3 * prow, 128), F32)
    lane_f, slot_f = lane[0:1].astype(F32), slot.astype(F32)
    for i in range(prow):
        at = jnp.where(inside[i : i + 1], place[i : i + 1] + start, -1)
        goes = row == (at >> 7)
        parts = [
            jnp.where(goes, v, 0.0) for v in (slot_f[i : i + 1], jnp.full((1, 128), float(i), F32), lane_f)
        ]
        spot = jnp.where(square_a == (at & 127), 1.0, 0.0).astype(BF16)
        listed += lax.dot_general(
            jnp.concatenate(parts, axis=0).astype(BF16), spot, (((1,), (1,)), ((), ())),
            preferred_element_type=F32,
        )
        start = start + sums[i : i + 1]
    listed = listed.astype(I32)
    entry = (listed[0:prow] << shift) + listed[prow : 2 * prow] * 128 + listed[2 * prow :]
    return jnp.where(number < start, entry, slots << shift), start


def gas_kernel(
    ng, nt, nf, live_ref, holder_hbm, flow_hbm, nu_hbm, pick_hbm, pos_hbm, mot_hbm, warm_hbm, mass_hbm, mult_hbm,
    table_ref, ints_ref, part_ref, placer_ref, parcel_ref,
    pos_ref, mot_ref, warm_ref, mass_ref, mult_ref, holder_ref, pick_ref, nu_ref, gas_ref, own_ref, twice_ref, all_ref, send_ref, recv_ref,
    edge_ref, ylo_ref, yhi_ref, first_ref, last_ref, xlo_ref, xhi_ref,
    small_sem, gas_sem, nu_sem, bulk_sem, tile_s, tile_r, own_s, own_r, own2_s, own2_r, halo_s, halo_r, local_sem,
):
    g, t = lax.axis_index("grp"), lax.axis_index("tile")
    rows, planes, width = gas_ref.shape
    rows_y = rows // nf
    sources = recv_ref.shape[0]
    small = start_all([(holder_hbm, holder_ref), (pick_hbm, pick_ref)], small_sem)
    gas_loads = start_all(
        [(flow_hbm.at[:, :, y, :], gas_ref.at[pl.ds(y * nf, nf)]) for y in range(rows_y)], gas_sem
    )
    grp_peers = [(lax.rem(g + k, ng), t) for k in range(1, ng)]
    tile_peers = [(g, lax.rem(t + k, nt)) for k in range(1, nt)]
    for peer in grp_peers + tile_peers:
        say_in(peer)

    @pl.when(g == ng - 1)
    def _():
        for k in range(sources):
            say_in(source(ng, nt, k))

    targets = ng + nt - 2 + jnp.where(g < ng - 1, nt // SHARE, 0)
    pairs = [(pos_hbm, pos_ref), (warm_hbm, warm_ref), (mass_hbm, mass_ref), (mult_hbm, mult_ref)]
    pairs += [(mot_hbm, mot_ref)]
    bulk = start_all(pairs, bulk_sem)
    nu_loads = start_all([(nu_hbm.at[:, y, :], nu_ref.at[y]) for y in range(rows_y)], nu_sem)
    partners = [lax.rem(t + k, nt) for k in range(nt)]
    homes = [home(ng, nt, p) for p in partners]

    own_ref[0] = jnp.full((1, 128), -1, I32)
    twice_ref[...] = jnp.full((1, 128), -1, I32)
    for c in small:
        c.wait()
    own_ref[0, :, 0:planes] = holder_ref[...]
    own = own_ref[0]
    twice_ref[:, 0:planes] = holder_ref[...]
    twice_ref[:, planes : 2 * planes] = holder_ref[...]
    both = twice_ref[...]
    row = jnp.broadcast_to(both, (128, 128))
    col = row.T
    s = lax.broadcasted_iota(I32, (128, 128), 0)
    l = lax.broadcasted_iota(I32, (128, 128), 1)
    near = (col == row) & ((s >= planes) == (l >= planes))
    rank = jnp.sum(jnp.where(near & (s < l), 1, 0), axis=0, keepdims=True)
    rank_col = jnp.sum(jnp.where(near & (l < s), 1, 0), axis=1, keepdims=True)
    lanes = lax.broadcasted_iota(I32, (1, 128), 1)
    subs = lax.broadcasted_iota(I32, (128, 1), 0)
    goal = both * (2 * SLOTS) + rank + jnp.where(lanes >= planes, SLOTS, 0)
    goal_col = col[:, 0:1] * (2 * SLOTS) + rank_col + jnp.where(subs >= planes, SLOTS, 0)
    picker = jnp.where(
        goal[:, 0 : 2 * planes] == lax.broadcasted_iota(I32, (nt * 2 * SLOTS, 2 * planes), 0), 1.0, 0.0
    ).astype(BF16)
    placer_ref[...] = jnp.where(
        goal_col[0 : 2 * planes] == lax.broadcasted_iota(I32, (2 * planes, nt * 2 * SLOTS), 1), 1.0, 0.0
    ).astype(BF16)
    for c in gas_loads:
        c.wait()
    for r in range(0, rows, 2):
        low = jnp.concatenate([gas_ref[r], gas_ref[r + 1]], axis=0).astype(BF16)
        got = jnp.dot(picker, low, preferred_element_type=F32).astype(BF16)
        for o in range(nt):
            send_ref[o, r * SLOTS : (r + 2) * SLOTS, :] = got[o * 2 * SLOTS : (o + 1) * 2 * SLOTS]

    pl.semaphore_wait(pltpu.get_barrier_semaphore(), targets)
    own_copies = [
        send_to(own_ref.at[0], all_ref.at[g, t], own_s.at[k], own_r.at[k], peer)
        for k, peer in enumerate(tile_peers)
    ]
    mine = pltpu.make_async_copy(own_ref.at[0], all_ref.at[g, t], local_sem.at[0])
    mine.start()
    gives = g < ng - 1

    def slab(k):
        p, (to_g, at) = partners[k], homes[k]
        return pltpu.make_async_remote_copy(
            src_ref=send_ref.at[p], dst_ref=recv_ref.at[at], send_sem=tile_s.at[k],
            recv_sem=tile_r.at[at], device_id=(to_g, p), device_id_type=MESH,
        )

    kept = pltpu.make_async_copy(send_ref.at[t], recv_ref.at[homes[0][1]], local_sem.at[1])

    @pl.when(gives)
    def _():
        for k in range(1, nt):
            slab(k).start()
        kept.start()

    mine.wait()
    for c in own_copies:
        c.wait_recv()
    own2_copies = [
        send_to(all_ref.at[g], all_ref.at[g], own2_s.at[k], own2_r.at[k], peer)
        for k, peer in enumerate(grp_peers)
    ]
    gas_side = jnp.where(g < ng - 1, 1.0, 0.0).astype(F32)
    edge_ref[0] = (gas_ref[rows - nf : rows] * gas_side).astype(BF16)
    edge_ref[1] = (gas_ref[0:nf] * gas_side).astype(BF16)
    first_ref[...] = gas_ref[:, 0, :].astype(BF16)
    last_ref[...] = gas_ref[:, planes - 1, :].astype(BF16)
    halos = [
        send_to(edge_ref.at[0], ylo_ref, halo_s.at[0], halo_r.at[0], grp_peers[0]),
        send_to(edge_ref.at[1], yhi_ref, halo_s.at[1], halo_r.at[1], grp_peers[-1]),
        send_to(last_ref, xlo_ref, halo_s.at[2], halo_r.at[2], tile_peers[0]),
        send_to(first_ref, xhi_ref, halo_s.at[3], halo_r.at[3], tile_peers[-1]),
    ]
    table_ref[...] = jnp.zeros_like(table_ref)
    for c in bulk:
        c.wait()

    @pl.loop(0, pos_ref.shape[0] // 8)
    def _(k):
        at = pl.ds(pl.multiple_of(k * 8, 8), 8)
        cell = pos_ref[at, :]
        values = [mot_ref[f, at, :] for f in range(3)] + [warm_ref[at, :], mass_ref[at, :], mult_ref[at, :]]
        values += [(cell & 127).astype(F32), (cell >> 7).astype(F32)]
        for f, v in enumerate(values):
            parcel_ref[pl.ds(k * 8 * (ROW + 1) + f, 8, stride=ROW + 1), :] = v

    for c in own2_copies:
        c.wait_recv()
    owners = jnp.concatenate([all_ref[k].reshape(nt, 128) for k in range(ng)], axis=0)
    entries, number = block_list(ng, nt, owners, pick_ref[...], live_ref[0])
    prow = entries.shape[0]
    ints_ref[0:prow, :] = entries
    ints_ref[prow : prow + 8, :] = jnp.broadcast_to(number, (8, 128))

    for c in nu_loads:
        c.wait()
    for c in halos:
        c.wait_recv()
    sub = lax.broadcasted_iota(I32, (planes, width), 0)
    lane = lax.broadcasted_iota(I32, (planes, width), 1)
    has_low = jnp.where(t > 0, 1.0, 0.0).astype(F32)
    has_high = jnp.where(t < nt - 1, 1.0, 0.0).astype(F32)
    x_low = xlo_ref[...].astype(F32) * has_low
    x_high = xhi_ref[...].astype(F32) * has_high
    for r in range(rows):
        mid = gas_ref[r]
        below = gas_ref[r - nf] if r >= nf else ylo_ref[r].astype(F32)
        above = gas_ref[r + nf] if r < rows - nf else yhi_ref[r - (rows - nf)].astype(F32)
        total = below + above
        total += jnp.where(sub == 0, x_low[r : r + 1], pltpu.roll(mid, 1, 0))
        total += jnp.where(sub == planes - 1, x_high[r : r + 1], pltpu.roll(mid, planes - 1, 0))
        total += jnp.where(lane == 0, 0.0, pltpu.roll(mid, 1, 1))
        total += jnp.where(lane == width - 1, 0.0, pltpu.roll(mid, width - 1, 1))
        part_ref[r] = (mid + 0.5 * nu_ref[r // nf] * (total - 6.0 * mid)) * gas_side

    def unpack(d):
        for r in range(0, rows, 2):
            both = recv_ref[d, r * SLOTS : (r + 2) * SLOTS, :].astype(F32)
            for h in range(2):
                at = (r + h) // nf * 8 + (r + h) % nf
                table_ref[pl.ds(d * SLOTS * PITCH + at, SLOTS, stride=PITCH), :] = both[h * SLOTS : (h + 1) * SLOTS]

    @pl.when(gives)
    def _():
        kept.wait()

    for k in range(sources):
        from_g, from_d = source(ng, nt, k)

        @pl.when((from_g != g) | (from_d != t))
        def _():
            pltpu.make_async_remote_copy(
                src_ref=send_ref.at[0], dst_ref=recv_ref.at[k], send_sem=tile_s.at[0],
                recv_sem=tile_r.at[k], device_id=(from_g, from_d), device_id_type=MESH,
            ).wait_recv()

        unpack(k)

    @pl.when(gives)
    def _():
        for k in range(1, nt):
            slab(k).wait_send()
    for c in own_copies + own2_copies + halos:
        c.wait_send()


def parcel_kernel(
    ints_ref, table, parcels, acc, seen, par, src, add, smem, sem,
):
    to_smem = pltpu.make_async_copy(ints_ref, smem, sem)
    to_smem.start()
    blocks = parcels.shape[0] // (ROW + 1)
    shift = blocks.bit_length() - 1
    prow = blocks // 128
    span = BATCH + 1
    acc[...] = jnp.zeros_like(acc)
    src[...] = jnp.zeros_like(src)
    par[...] = jnp.zeros_like(par)
    to_smem.wait()

    n = smem[prow, 0]
    sub = lax.broadcasted_iota(I32, (128, 128), 0).astype(F32).astype(BF16)
    yes, no = jnp.ones((128, 128), BF16), jnp.zeros((128, 128), BF16)
    half = lax.broadcasted_iota(I32, (16, 128), 0) >> 3
    half = [(half + 2 * k).astype(F32).astype(BF16) for k in range(2)]
    zero = jnp.zeros((32, 128), BF16)

    @pl.loop(0, (n + BATCH - 1) // BATCH + 1)
    def _(step):
        last = jnp.maximum(step - 1, 0)
        rows = [(k // (128 // BATCH), lax.rem(k, 128 // BATCH) * BATCH) for k in (step, last)]
        for j in range(0, BATCH, 2):
            left, hot = [], []
            for i in (j, j + 1):
                z = jnp.broadcast_to(par[6 * span + i : 6 * span + i + 1, :], (16, 128)).astype(BF16)
                y = jnp.broadcast_to(par[7 * span + i : 7 * span + i + 1, :], (16, 128)).astype(BF16)
                s8 = src[pl.ds(i * 9, 8), :]
                s16 = jnp.concatenate([s8, s8], axis=0).astype(BF16)
                s32 = jnp.concatenate([jnp.where(y == h, s16, no[0:16]) for h in half], axis=0)
                left.append(jnp.concatenate([s32, zero] if i == j else [zero, s32], axis=1))
                hot.append(jnp.where(sub == jnp.concatenate([z] * 8, axis=0), yes, no))
            add[j * 32 : (j + 2) * 32, :] = lax.dot_general(
                jnp.concatenate(left, axis=0), jnp.concatenate(hot, axis=1), (((1,), (1,)), ((), ())),
                preferred_element_type=F32,
            )
            for i in (j, j + 1):
                v = smem[rows[0][0], rows[0][1] + i]
                b = (v & (blocks - 1)) * (ROW + 1)
                base = (v >> shift) * PITCH
                values = parcels[pl.ds(b, 8), :]
                z = jnp.broadcast_to(parcels[pl.ds(b + 6, 1), :], (8, 128)).astype(I32)
                y = jnp.broadcast_to(parcels[pl.ds(b + 7, 1), :], (8, 128))
                got = [
                    jnp.take_along_axis(table[pl.ds(base + k * 8, 8), :], z, axis=1) for k in range(4)
                ]
                upper = jnp.where(y < 1, got[0], got[1])
                lower = jnp.where(y < 3, got[2], got[3])
                seen[pl.ds(i, 8, stride=span), :] = jnp.where(y < 2, upper, lower)
                par[pl.ds(i, 8, stride=span), :] = values
        for i in range(BATCH):
            at = pl.ds((smem[rows[1][0], rows[1][1] + i] >> shift) * PITCH, 32)
            acc[at, :] = acc[at, :] + add[i * 32 : (i + 1) * 32, :]
        field = [seen[f * span : f * span + BATCH, :] for f in range(5)]
        v0, v1, v2, warm, mass, mult = [par[f * span : f * span + BATCH, :] for f in range(6)]
        r0, r1, r2 = field[0] - v0, field[1] - v1, field[2] - v2
        speed_sq = r0 * r0 + r1 * r1 + r2 * r2
        inv_surface = jnp.exp(jnp.log(mass) * (-2.0 / 3.0))
        inverse_tau = 0.8 * (1.0 + 0.15 * jnp.exp(0.3435 * jnp.log(1.0 + speed_sq))) * inv_surface
        relax = 1.0 - jnp.exp(-0.5 * inverse_tau)
        heating = 1.0 / (1.0 + jnp.exp(field[4] - field[3]))
        remain = jnp.exp(-0.3 * heating * inv_surface)
        new_mass = mass * remain
        warming = 1.0 - jnp.exp(-0.25 * inverse_tau)
        new_warm = warm + warming * (field[3] - warm) - 0.5 * (1.0 - remain)
        outs = [mass * v - new_mass * (v + relax * r) for v, r in ((v0, r0), (v1, r1), (v2, r2))]
        outs += [mass * warm - new_mass * new_warm, mass - new_mass]
        for f, o in enumerate(outs):
            src[pl.ds(f, BATCH, stride=9), :] = mult * o


def return_kernel(ng, nt, nf, acc_ref, recv_ref, send_ref, tile_s, tile_r, local_sem):
    g, t = lax.axis_index("grp"), lax.axis_index("tile")
    sources, rows, _ = send_ref.shape
    takes = g < ng - 1

    @pl.when(takes)
    def _():
        for k in range(1, nt):
            p = lax.rem(t + k, nt)
            say_in((home(ng, nt, p)[0], p))

    origins = [source(ng, nt, k) for k in range(sources)]
    remote = [(to_g != g) | (to_d != t) for to_g, to_d in origins]
    for d in range(sources):
        for r in range(0, rows // SLOTS, 2):
            pair = [
                acc_ref[pl.ds(d * SLOTS * PITCH + q // nf * 8 + q % nf, SLOTS, stride=PITCH), :]
                for q in (r, r + 1)
            ]
            send_ref[d, r * SLOTS : (r + 2) * SLOTS, :] = jnp.concatenate(pair, axis=0).astype(BF16)
    def slab(k):
        return pltpu.make_async_remote_copy(
            src_ref=send_ref.at[k], dst_ref=recv_ref.at[t], send_sem=tile_s.at[k],
            recv_sem=tile_r.at[t], device_id=origins[k], device_id_type=MESH,
        )

    pl.semaphore_wait(pltpu.get_barrier_semaphore(), sources - jnp.where(takes, 1, 0))
    for k in range(sources):

        @pl.when(remote[k])
        def _():
            slab(k).start()

    kept = pltpu.make_async_copy(send_ref.at[home(ng, nt, t)[1]], recv_ref.at[t], local_sem)

    @pl.when(takes)
    def _():
        kept.start()
        kept.wait()
        for k in range(1, nt):
            p = lax.rem(t + k, nt)
            pltpu.make_async_remote_copy(
                src_ref=send_ref.at[0], dst_ref=recv_ref.at[p], send_sem=tile_s.at[0],
                recv_sem=tile_r.at[p], device_id=(home(ng, nt, p)[0], p), device_id_type=MESH,
            ).wait_recv()

    @pl.when(jnp.logical_not(takes))
    def _():
        recv_ref[...] = jnp.zeros_like(recv_ref)

    for k in range(sources):

        @pl.when(remote[k])
        def _():
            slab(k).wait_send()


def place_kernel(ng, nt, nf, recv_ref, placer_ref, part_ref, out_hbm, buf, sem):
    rows, planes, width = part_ref.shape
    gas_side = lax.axis_index("grp") < ng - 1
    placer = placer_ref[...]
    copies = []
    for r in range(0, rows, 2):
        inc = jnp.concatenate([recv_ref[d, r * SLOTS : (r + 2) * SLOTS, :] for d in range(nt)], axis=0)
        placed = jnp.dot(placer, inc, preferred_element_type=F32)
        for h in range(2):
            q = r + h
            buf[q] = part_ref[q] + jnp.where(gas_side, placed[h * planes : (h + 1) * planes], 0.0)
            c = pltpu.make_async_copy(buf.at[q], out_hbm.at[q % nf, :, q // nf, :], sem.at[q])
            c.start()
            copies.append(c)
    for c in copies:
        c.wait()


def local(
    flow_fields, turbulent_diffusivity, holder_unit, spray_volume_position, patch_pick_unreduced,
    droplet_motion, droplet_warmth, droplet_weightiness, droplet_multiplicity, living_spray_batches,
):
    ng, nt = lax.axis_size("grp"), lax.axis_size("tile")
    nf, planes, rows_y, width = flow_fields.shape
    rows = nf * rows_y
    dma = pltpu.SemaphoreType.DMA
    shape = jax.ShapeDtypeStruct
    blocks = spray_volume_position.shape[1]
    sources = nt * (SHARE - 1) // SHARE
    slots = sources * SLOTS
    prow = blocks // 128
    slab = (nt, rows * SLOTS, width)
    gas = (rows, planes, width)
    table, ints, part, placer, parcels = pl.pallas_call(
        functools.partial(gas_kernel, ng, nt, nf),
        out_shape=(
            shape(((slots + 1) * PITCH + 7, width), F32), shape((prow + 8, 128), I32), shape(gas, F32),
            shape((2 * planes, nt * 2 * SLOTS), BF16), shape((blocks * (ROW + 1), 128), F32),
        ),
        in_specs=[SMEM] + [HBM] * 9, out_specs=(VMEM,) * 5,
        scratch_shapes=[
            pltpu.VMEM((blocks, 128), I32), pltpu.VMEM((3, blocks, 128), F32),
            pltpu.VMEM((blocks, 128), F32), pltpu.VMEM((blocks, 128), F32), pltpu.VMEM((blocks, 128), F32),
            pltpu.VMEM((1, planes), I32), pltpu.VMEM((prow, 128), I32),
            pltpu.VMEM((rows_y, planes, width), F32), pltpu.VMEM(gas, F32),
            pltpu.VMEM((1, 1, 128), I32), pltpu.VMEM((1, 128), I32), pltpu.VMEM((ng, nt, 1, 128), I32),
            pltpu.VMEM(slab, BF16), pltpu.VMEM((sources,) + slab[1:], BF16),
            pltpu.VMEM((2, nf, planes, width), BF16),
            pltpu.VMEM((nf, planes, width), BF16), pltpu.VMEM((nf, planes, width), BF16),
            pltpu.VMEM((rows, width), BF16), pltpu.VMEM((rows, width), BF16),
            pltpu.VMEM((rows, width), BF16), pltpu.VMEM((rows, width), BF16),
            dma((2,)), dma((rows_y,)), dma((rows_y,)), dma((5,)),
            dma((nt,)), dma((sources,)), dma((nt - 1,)), dma((nt - 1,)),
            dma((ng - 1,)), dma((ng - 1,)), dma((4,)), dma((4,)), dma((2,)),
        ],
        compiler_params=pltpu.CompilerParams(
            collective_id=0, has_side_effects=True, vmem_limit_bytes=24 << 20
        ),
        name="gas",
    )(living_spray_batches, *(pltpu.with_memory_space_constraint(a, pltpu.MemorySpace.HBM) for a in (
        holder_unit.reshape(1, planes), flow_fields, turbulent_diffusivity,
        patch_pick_unreduced.reshape(prow, 128), spray_volume_position[0],
        droplet_motion[0].transpose(1, 0, 2), droplet_warmth[0], droplet_weightiness[0],
        droplet_multiplicity[0],
    )))
    acc = pl.pallas_call(
        parcel_kernel,
        out_shape=shape(((slots + 1) * PITCH + 7, width), F32),
        in_specs=[VMEM] * 3, out_specs=VMEM,
        scratch_shapes=[
            pltpu.VMEM((8 * (BATCH + 1), width), F32),
            pltpu.VMEM((8 * (BATCH + 1), width), F32),
            pltpu.VMEM((BATCH * 9, width), F32),
            pltpu.VMEM((BATCH * 32, width), F32),
            pltpu.SMEM((prow + 8, 128), I32),
            dma,
        ],
        compiler_params=pltpu.CompilerParams(vmem_limit_bytes=24 << 20),
        name="parcels",
    )(ints, table, parcels)
    recv = pl.pallas_call(
        functools.partial(return_kernel, ng, nt, nf),
        out_shape=shape(slab, BF16),
        in_specs=[VMEM], out_specs=VMEM,
        scratch_shapes=[
            pltpu.VMEM((sources,) + slab[1:], BF16), dma((sources,)), dma((nt,)), dma,
        ],
        compiler_params=pltpu.CompilerParams(
            collective_id=1, has_side_effects=True, vmem_limit_bytes=16 << 20
        ),
        name="return",
    )(acc)
    return pl.pallas_call(
        functools.partial(place_kernel, ng, nt, nf),
        out_shape=shape((nf, planes, rows_y, width), F32),
        in_specs=[VMEM] * 3, out_specs=HBM,
        scratch_shapes=[pltpu.VMEM(gas, F32), dma((rows,))],
        compiler_params=pltpu.CompilerParams(vmem_limit_bytes=12 << 20),
        name="place",
    )(recv, placer, part)


def solution(mesh):
    in_specs = (
        P(None, "tile", "grp", None),
        P("tile", "grp", None),
        P("grp", "tile", None),
        P("tile", None, None),
        P("tile", None),
        P("tile", None, None, None),
        P("tile", None, None),
        P("tile", None, None),
        P("tile", None, None),
        P("tile"),
    )
    out_specs = P(None, "tile", "grp", None)
    return jax.shard_map(local, mesh=mesh, in_specs=in_specs, out_specs=out_specs, check_vma=False)
```

```python
import functools

import jax
import jax.numpy as jnp
from jax import lax
from jax.experimental import pallas as pl
from jax.experimental.pallas import tpu as pltpu
from jax.sharding import PartitionSpec as P

MESH = pl.DeviceIdType.MESH
SLOTS = 8
BATCH = 64
HBM = pl.BlockSpec(memory_space=pltpu.MemorySpace.HBM)
VMEM = pl.BlockSpec(memory_space=pltpu.VMEM)
SMEM = pl.BlockSpec(memory_space=pltpu.SMEM)
F32, BF16, I32 = jnp.float32, jnp.bfloat16, jnp.int32


ROW = 8
PITCH = 25
SHARE = 4


def say_in(peer):
    pl.semaphore_signal(pltpu.get_barrier_semaphore(), inc=1, device_id=peer, device_id_type=MESH)


def wrap(x, n):
    return x - jnp.where(x >= n, n, 0)


def source(ng, nt, s):
    g, p = lax.axis_index("grp"), lax.axis_index("tile")
    spare = g == ng - 1
    e = jnp.where(spare, s // (ng - 1) * SHARE + SHARE - 1, s + s // (SHARE - 1))
    return jnp.where(spare, s % (ng - 1), g), wrap(e - p + nt, nt)


def home(ng, nt, p):
    g = lax.axis_index("grp")
    e = wrap(lax.axis_index("tile") + p, nt)
    quarter = lax.div(e, SHARE)
    shared = e - quarter * SHARE == SHARE - 1
    return jnp.where(shared, ng - 1, g), jnp.where(shared, quarter * (ng - 1) + g, e - quarter)


def send_to(src, dst, ss, rs, dev):
    c = pltpu.make_async_remote_copy(
        src_ref=src, dst_ref=dst, send_sem=ss, recv_sem=rs, device_id=dev, device_id_type=MESH
    )
    c.start()
    return c


def start_all(pairs, sems):
    loads = [pltpu.make_async_copy(a, b, sems.at[k]) for k, (a, b) in enumerate(pairs)]
    for c in loads:
        c.start()
    return loads


def block_list(ng, nt, owners, pick, live):
    p = lax.axis_index("tile")
    prow = pick.shape[0]
    sources = nt * (SHARE - 1) // SHARE
    slots = sources * SLOTS
    owned = jnp.where(owners == p, 1, 0)
    counts = jnp.sum(owned, axis=1, keepdims=True)
    which = lax.broadcasted_iota(I32, counts.shape, 0)
    counts = jnp.where(which < (ng - 1) * nt, counts, 0)
    total = jnp.maximum(jnp.sum(counts, axis=0, keepdims=True), 1)
    total_f = total.astype(F32)
    quotient = jnp.floor(pick.astype(F32) / total_f).astype(I32)
    left = pick - quotient * total
    left = jnp.where(left < 0, left + total, left)
    left = jnp.where(left >= total, left - total, left)
    slot = jnp.full(pick.shape, -1, I32)
    for k in range(sources):
        from_g, from_d = source(ng, nt, k)
        number = from_g * nt + from_d
        low = jnp.sum(jnp.where(which < number, counts, 0), axis=0, keepdims=True)
        size = jnp.sum(jnp.where(which == number, counts, 0), axis=0, keepdims=True)
        rank = left - low
        slot = jnp.where((rank >= 0) & (rank < size), rank + k * SLOTS, slot)
    row = lax.broadcasted_iota(I32, (prow, 128), 0)
    lane = lax.broadcasted_iota(I32, (prow, 128), 1)
    number = row * 128 + lane
    inside = (slot >= 0) & (number < live)
    flags = jnp.where(inside, 1, 0)
    square_a = lax.broadcasted_iota(I32, (128, 128), 0)
    square_b = lax.broadcasted_iota(I32, (128, 128), 1)
    before = jnp.where(square_a < square_b, 1.0, 0.0).astype(BF16)
    flags_low = flags.astype(F32).astype(BF16)
    place = jnp.dot(flags_low, before, preferred_element_type=F32).astype(I32)
    sums = jnp.sum(flags, axis=1, keepdims=True)
    start = jnp.zeros((1, 1), I32)
    listed = jnp.zeros((3 * prow, 128), F32)
    lane_f, slot_f = lane[0:1].astype(F32), slot.astype(F32)
    for i in range(prow):
        at = jnp.where(inside[i : i + 1], place[i : i + 1] + start, -1)
        goes = row == (at >> 7)
        parts = [
            jnp.where(goes, v, 0.0) for v in (slot_f[i : i + 1], jnp.full((1, 128), float(i), F32), lane_f)
        ]
        spot = jnp.where(square_a == (at & 127), 1.0, 0.0).astype(BF16)
        listed += lax.dot_general(
            jnp.concatenate(parts, axis=0).astype(BF16), spot, (((1,), (1,)), ((), ())),
            preferred_element_type=F32,
        )
        start = start + sums[i : i + 1]
    listed = listed.astype(I32)
    block = listed[prow : 2 * prow] * 128 + listed[2 * prow :]
    entry = ((listed[0:prow] * PITCH) << 16) + block * (ROW + 1)
    return jnp.where(number < start, entry, (slots * PITCH) << 16), start


def gas_kernel(
    ng, nt, nf, live_ref, holder_hbm, flow_hbm, nu_hbm, pick_hbm, pos_hbm, mot_hbm, warm_hbm, mass_hbm, mult_hbm,
    table_ref, ints_ref, part_ref, placer_ref, parcel_ref,
    pos_ref, mot_ref, warm_ref, mass_ref, mult_ref, holder_ref, pick_ref, nu_ref, gas_ref, own_ref, twice_ref, all_ref, send_ref, recv_ref,
    edge_ref, ylo_ref, yhi_ref, first_ref, last_ref, xlo_ref, xhi_ref,
    small_sem, gas_sem, nu_sem, bulk_sem, tile_s, tile_r, own_s, own_r, own2_s, own2_r, halo_s, halo_r, local_sem,
):
    g, t = lax.axis_index("grp"), lax.axis_index("tile")
    rows, planes, width = gas_ref.shape
    rows_y = rows // nf
    sources = recv_ref.shape[0]
    small = start_all([(holder_hbm, holder_ref), (pick_hbm, pick_ref)], small_sem)
    gas_loads = start_all(
        [(flow_hbm.at[:, :, y, :], gas_ref.at[pl.ds(y * nf, nf)]) for y in range(rows_y)], gas_sem
    )
    grp_peers = [(wrap(g + k, ng), t) for k in range(1, ng)]
    tile_peers = [(g, wrap(t + k, nt)) for k in range(1, nt)]
    for peer in grp_peers + tile_peers:
        say_in(peer)

    @pl.when(g == ng - 1)
    def _():
        for k in range(sources):
            say_in(source(ng, nt, k))

    targets = ng + nt - 2 + jnp.where(g < ng - 1, nt // SHARE, 0)
    pairs = [(pos_hbm, pos_ref), (warm_hbm, warm_ref), (mass_hbm, mass_ref), (mult_hbm, mult_ref)]
    pairs += [(mot_hbm, mot_ref)]
    bulk = start_all(pairs, bulk_sem)
    nu_loads = start_all([(nu_hbm.at[:, y, :], nu_ref.at[y]) for y in range(rows_y)], nu_sem)
    partners = [wrap(t + k, nt) for k in range(nt)]
    homes = [home(ng, nt, p) for p in partners]

    own_ref[0] = jnp.full((1, 128), -1, I32)
    twice_ref[...] = jnp.full((1, 128), -1, I32)
    for c in small:
        c.wait()
    own_ref[0, :, 0:planes] = holder_ref[...]
    own = own_ref[0]
    twice_ref[:, 0:planes] = holder_ref[...]
    twice_ref[:, planes : 2 * planes] = holder_ref[...]
    both = twice_ref[...]
    row = jnp.broadcast_to(both, (128, 128))
    col = row.T
    s = lax.broadcasted_iota(I32, (128, 128), 0)
    l = lax.broadcasted_iota(I32, (128, 128), 1)
    near = (col == row) & ((s >= planes) == (l >= planes))
    rank = jnp.sum(jnp.where(near & (s < l), 1, 0), axis=0, keepdims=True)
    rank_col = jnp.sum(jnp.where(near & (l < s), 1, 0), axis=1, keepdims=True)
    lanes = lax.broadcasted_iota(I32, (1, 128), 1)
    subs = lax.broadcasted_iota(I32, (128, 1), 0)
    goal = both * (2 * SLOTS) + rank + jnp.where(lanes >= planes, SLOTS, 0)
    goal_col = col[:, 0:1] * (2 * SLOTS) + rank_col + jnp.where(subs >= planes, SLOTS, 0)
    picker = jnp.where(
        goal[:, 0 : 2 * planes] == lax.broadcasted_iota(I32, (nt * 2 * SLOTS, 2 * planes), 0), 1.0, 0.0
    ).astype(BF16)
    placer_ref[...] = jnp.where(
        goal_col[0 : 2 * planes] == lax.broadcasted_iota(I32, (2 * planes, nt * 2 * SLOTS), 1), 1.0, 0.0
    ).astype(BF16)
    for c in gas_loads:
        c.wait()
    for r in range(0, rows, 2):
        low = jnp.concatenate([gas_ref[r], gas_ref[r + 1]], axis=0).astype(BF16)
        got = jnp.dot(picker, low, preferred_element_type=F32).astype(BF16)
        for o in range(nt):
            send_ref[o, r * SLOTS : (r + 2) * SLOTS, :] = got[o * 2 * SLOTS : (o + 1) * 2 * SLOTS]

    pl.semaphore_wait(pltpu.get_barrier_semaphore(), targets)
    own_copies = [
        send_to(own_ref.at[0], all_ref.at[g, t], own_s.at[k], own_r.at[k], peer)
        for k, peer in enumerate(tile_peers)
    ]
    mine = pltpu.make_async_copy(own_ref.at[0], all_ref.at[g, t], local_sem.at[0])
    mine.start()
    gives = g < ng - 1

    def slab(k):
        p, (to_g, at) = partners[k], homes[k]
        return pltpu.make_async_remote_copy(
            src_ref=send_ref.at[p], dst_ref=recv_ref.at[at], send_sem=tile_s.at[k],
            recv_sem=tile_r.at[at], device_id=(to_g, p), device_id_type=MESH,
        )

    kept = pltpu.make_async_copy(send_ref.at[t], recv_ref.at[homes[0][1]], local_sem.at[1])

    @pl.when(gives)
    def _():
        for k in range(1, nt):
            slab(k).start()
        kept.start()

    mine.wait()
    for c in own_copies:
        c.wait_recv()
    own2_copies = [
        send_to(all_ref.at[g], all_ref.at[g], own2_s.at[k], own2_r.at[k], peer)
        for k, peer in enumerate(grp_peers)
    ]
    gas_side = jnp.where(g < ng - 1, 1.0, 0.0).astype(F32)
    edge_ref[0] = (gas_ref[rows - nf : rows] * gas_side).astype(BF16)
    edge_ref[1] = (gas_ref[0:nf] * gas_side).astype(BF16)
    first_ref[...] = gas_ref[:, 0, :].astype(BF16)
    last_ref[...] = gas_ref[:, planes - 1, :].astype(BF16)
    halos = [
        send_to(edge_ref.at[0], ylo_ref, halo_s.at[0], halo_r.at[0], grp_peers[0]),
        send_to(edge_ref.at[1], yhi_ref, halo_s.at[1], halo_r.at[1], grp_peers[-1]),
        send_to(last_ref, xlo_ref, halo_s.at[2], halo_r.at[2], tile_peers[0]),
        send_to(first_ref, xhi_ref, halo_s.at[3], halo_r.at[3], tile_peers[-1]),
    ]
    table_ref[...] = jnp.zeros_like(table_ref)
    for c in bulk:
        c.wait()

    @pl.loop(0, pos_ref.shape[0] // 8)
    def _(k):
        at = pl.ds(pl.multiple_of(k * 8, 8), 8)
        cell = pos_ref[at, :]
        values = [mot_ref[f, at, :] for f in range(3)] + [warm_ref[at, :], mass_ref[at, :], mult_ref[at, :]]
        values += [(cell & 127).astype(F32), (cell >> 7).astype(F32)]
        for f, v in enumerate(values):
            parcel_ref[pl.ds(k * 8 * (ROW + 1) + f, 8, stride=ROW + 1), :] = v

    for c in own2_copies:
        c.wait_recv()
    owners = jnp.concatenate([all_ref[k].reshape(nt, 128) for k in range(ng)], axis=0)
    entries, number = block_list(ng, nt, owners, pick_ref[...], live_ref[0])
    prow, spans = entries.shape[0], 128 // BATCH
    for k in range(spans):
        here = entries if k == 0 else pltpu.roll(entries, 128 - k * BATCH, 1)
        ints_ref[pl.ds(k, prow, stride=spans), :] = here
    ints_ref[prow * spans : prow * spans + 8, :] = jnp.broadcast_to(number, (8, 128))

    for c in nu_loads:
        c.wait()
    for c in halos:
        c.wait_recv()
    sub = lax.broadcasted_iota(I32, (planes, width), 0)
    lane = lax.broadcasted_iota(I32, (planes, width), 1)
    has_low = jnp.where(t > 0, 1.0, 0.0).astype(F32)
    has_high = jnp.where(t < nt - 1, 1.0, 0.0).astype(F32)
    x_low = xlo_ref[...].astype(F32) * has_low
    x_high = xhi_ref[...].astype(F32) * has_high
    for r in range(rows):
        mid = gas_ref[r]
        below = gas_ref[r - nf] if r >= nf else ylo_ref[r].astype(F32)
        above = gas_ref[r + nf] if r < rows - nf else yhi_ref[r - (rows - nf)].astype(F32)
        total = below + above
        total += jnp.where(sub == 0, x_low[r : r + 1], pltpu.roll(mid, 1, 0))
        total += jnp.where(sub == planes - 1, x_high[r : r + 1], pltpu.roll(mid, planes - 1, 0))
        total += jnp.where(lane == 0, 0.0, pltpu.roll(mid, 1, 1))
        total += jnp.where(lane == width - 1, 0.0, pltpu.roll(mid, width - 1, 1))
        part_ref[r] = (mid + 0.5 * nu_ref[r // nf] * (total - 6.0 * mid)) * gas_side

    def unpack(d):
        for r in range(0, rows, 2):
            both = recv_ref[d, r * SLOTS : (r + 2) * SLOTS, :].astype(F32)
            for h in range(2):
                table_ref[pl.ds(d * SLOTS * PITCH + r + h, SLOTS, stride=PITCH), :] = both[h * SLOTS : (h + 1) * SLOTS]

    @pl.when(gives)
    def _():
        kept.wait()

    for k in range(sources):
        from_g, from_d = source(ng, nt, k)

        @pl.when((from_g != g) | (from_d != t))
        def _():
            pltpu.make_async_remote_copy(
                src_ref=send_ref.at[0], dst_ref=recv_ref.at[k], send_sem=tile_s.at[0],
                recv_sem=tile_r.at[k], device_id=(from_g, from_d), device_id_type=MESH,
            ).wait_recv()

        unpack(k)

    @pl.when(gives)
    def _():
        for k in range(1, nt):
            slab(k).wait_send()
    for c in own_copies + own2_copies + halos:
        c.wait_send()


def sources_of(field, own):
    v0, v1, v2, warm, mass, mult = own
    r0, r1, r2 = field[0] - v0, field[1] - v1, field[2] - v2
    speed_sq = r0 * r0 + r1 * r1 + r2 * r2
    inv_surface = jnp.exp(jnp.log(mass) * (-2.0 / 3.0))
    inverse_tau = 0.8 * (1.0 + 0.15 * jnp.exp(0.3435 * jnp.log(1.0 + speed_sq))) * inv_surface
    relax = 1.0 - jnp.exp(-0.5 * inverse_tau)
    heating = 1.0 / (1.0 + jnp.exp(field[4] - field[3]))
    remain = jnp.exp(-0.3 * heating * inv_surface)
    new_mass = mass * remain
    warming = 1.0 - jnp.exp(-0.25 * inverse_tau)
    new_warm = warm + warming * (field[3] - warm) - 0.5 * (1.0 - remain)
    outs = [mass * v - new_mass * (v + relax * r) for v, r in ((v0, r0), (v1, r1), (v2, r2))]
    outs += [mass * warm - new_mass * new_warm, mass - new_mass]
    return [mult * o for o in outs]


def parcel_kernel(nf, rows_y, ints_ref, table, parcels, acc, seen, par, src, cells, add, smem, sem):
    to_smem = pltpu.make_async_copy(ints_ref, smem, sem)
    to_smem.start()
    span = BATCH + 1
    acc[...] = jnp.zeros_like(acc)
    src[...] = jnp.zeros_like(src)
    to_smem.wait()

    n = smem[smem.shape[0] - 8, 0]
    sub = lax.broadcasted_iota(I32, (128, 128), 0).astype(F32).astype(BF16)
    yes, no = jnp.ones((128, 128), BF16), jnp.zeros((128, 128), BF16)
    spare = jnp.zeros((8, 128), F32)
    zero = jnp.zeros((32, 128), BF16)

    def batch(step, size):
        where_at = []
        for c in range(0, size, 8):
            for i in range(c, c + 8):
                v = smem[step, i]
                b, base = v & 65535, v >> 16
                where_at.append(base)
                z = jnp.broadcast_to(parcels[pl.ds(b + 6, 1), :], (8, 128)).astype(I32)
                for k in range(3):
                    seen[pl.ds(k * 8 * span + i, 8, stride=span), :] = jnp.take_along_axis(
                        table[pl.ds(base + k * 8, 8), :], z, axis=1, mode="promise_in_bounds",
                        wrap_negative_indices=False,
                    )
                par[pl.ds(i, 8, stride=span), :] = parcels[pl.ds(b, 8), :]
        for c in range(0, size, 8):
            own = [par[f * span + c : f * span + c + 8, :] for f in range(ROW)]
            y = own[7]
            cells[c : c + 8, :] = own[6]
            gas = []
            for f in range(nf):
                at = [seen[(k * nf + f) * span + c : (k * nf + f) * span + c + 8, :] for k in range(rows_y)]
                value = at[0]
                for k in range(1, rows_y):
                    value = jnp.where(y < k, value, at[k])
                gas.append(value)
            outs = sources_of(gas, own[0:6])
            for k in range(rows_y):
                here = y == k
                for f in range(nf):
                    src[pl.ds(c * PITCH + k * nf + f, 8, stride=PITCH), :] = jnp.where(here, outs[f], 0.0)
        for c in range(0, size, 8):
            for j in range(c, c + 8, 2):
                left, hot = [], []
                for i in (j, j + 1):
                    z = jnp.broadcast_to(cells[i : i + 1, :], (16, 128)).astype(BF16)
                    hot.append(jnp.where(sub == jnp.concatenate([z] * 8, axis=0), yes, no))
                    mine = jnp.concatenate([src[i * PITCH : i * PITCH + 24, :], spare], axis=0).astype(BF16)
                    left.append(jnp.concatenate([mine, zero] if i == j else [zero, mine], axis=1))
                added = lax.dot_general(
                    jnp.concatenate(left, axis=0), jnp.concatenate(hot, axis=1), (((1,), (1,)), ((), ())),
                    preferred_element_type=F32,
                )
                for i in (j, j + 1):
                    add[i * 24 : (i + 1) * 24, :] = added[(i - j) * 32 : (i - j) * 32 + 24]
        for i in range(size):
            at = pl.ds(where_at[i], 24)
            acc[at, :] = acc[at, :] + add[i * 24 : (i + 1) * 24, :]

    rest = lax.rem(n, BATCH)
    whole = n // BATCH + jnp.where(rest > BATCH // 2, 1, 0)

    @pl.loop(0, whole)
    def _(step):
        batch(step, BATCH)

    @pl.when((rest > 0) & (rest <= BATCH // 2))
    def _():
        batch(whole, BATCH // 2)


def return_kernel(ng, nt, acc_ref, recv_ref, send_ref, tile_s, tile_r, local_sem):
    g, t = lax.axis_index("grp"), lax.axis_index("tile")
    sources, rows, _ = send_ref.shape
    takes = g < ng - 1

    @pl.when(takes)
    def _():
        for k in range(1, nt):
            p = wrap(t + k, nt)
            say_in((home(ng, nt, p)[0], p))

    origins = [source(ng, nt, k) for k in range(sources)]
    remote = [(to_g != g) | (to_d != t) for to_g, to_d in origins]
    for d in range(sources):
        for r in range(0, rows // SLOTS, 2):
            pair = [
                acc_ref[pl.ds(d * SLOTS * PITCH + q, SLOTS, stride=PITCH), :]
                for q in (r, r + 1)
            ]
            send_ref[d, r * SLOTS : (r + 2) * SLOTS, :] = jnp.concatenate(pair, axis=0).astype(BF16)
    def slab(k):
        return pltpu.make_async_remote_copy(
            src_ref=send_ref.at[k], dst_ref=recv_ref.at[t], send_sem=tile_s.at[k],
            recv_sem=tile_r.at[t], device_id=origins[k], device_id_type=MESH,
        )

    pl.semaphore_wait(pltpu.get_barrier_semaphore(), sources - jnp.where(takes, 1, 0))
    for k in range(sources):

        @pl.when(remote[k])
        def _():
            slab(k).start()

    kept = pltpu.make_async_copy(send_ref.at[home(ng, nt, t)[1]], recv_ref.at[t], local_sem)

    @pl.when(takes)
    def _():
        kept.start()
        kept.wait()
        for k in range(1, nt):
            p = wrap(t + k, nt)
            pltpu.make_async_remote_copy(
                src_ref=send_ref.at[0], dst_ref=recv_ref.at[p], send_sem=tile_s.at[0],
                recv_sem=tile_r.at[p], device_id=(home(ng, nt, p)[0], p), device_id_type=MESH,
            ).wait_recv()

    @pl.when(jnp.logical_not(takes))
    def _():
        recv_ref[...] = jnp.zeros_like(recv_ref)

    for k in range(sources):

        @pl.when(remote[k])
        def _():
            slab(k).wait_send()


def place_kernel(ng, nt, nf, recv_ref, placer_ref, part_ref, out_hbm, buf, sem):
    rows, planes, width = part_ref.shape
    gas_side = lax.axis_index("grp") < ng - 1
    placer = placer_ref[...]
    copies = []
    for r in range(0, rows, 2):
        inc = jnp.concatenate([recv_ref[d, r * SLOTS : (r + 2) * SLOTS, :] for d in range(nt)], axis=0)
        placed = jnp.dot(placer, inc, preferred_element_type=F32)
        for h in range(2):
            q = r + h
            buf[q] = part_ref[q] + jnp.where(gas_side, placed[h * planes : (h + 1) * planes], 0.0)
            c = pltpu.make_async_copy(buf.at[q], out_hbm.at[q % nf, :, q // nf, :], sem.at[q])
            c.start()
            copies.append(c)
    for c in copies:
        c.wait()


def local(
    flow_fields, turbulent_diffusivity, holder_unit, spray_volume_position, patch_pick_unreduced,
    droplet_motion, droplet_warmth, droplet_weightiness, droplet_multiplicity, living_spray_batches,
):
    ng, nt = lax.axis_size("grp"), lax.axis_size("tile")
    nf, planes, rows_y, width = flow_fields.shape
    rows = nf * rows_y
    dma = pltpu.SemaphoreType.DMA
    shape = jax.ShapeDtypeStruct
    blocks = spray_volume_position.shape[1]
    sources = nt * (SHARE - 1) // SHARE
    slots = sources * SLOTS
    prow = blocks // 128
    lists = blocks // BATCH + 8
    slab = (nt, rows * SLOTS, width)
    gas = (rows, planes, width)
    table, ints, part, placer, parcels = pl.pallas_call(
        functools.partial(gas_kernel, ng, nt, nf),
        out_shape=(
            shape(((slots + 1) * PITCH + 7, width), F32), shape((lists, 128), I32), shape(gas, F32),
            shape((2 * planes, nt * 2 * SLOTS), BF16), shape((blocks * (ROW + 1), 128), F32),
        ),
        in_specs=[SMEM] + [HBM] * 9, out_specs=(VMEM,) * 5,
        scratch_shapes=[
            pltpu.VMEM((blocks, 128), I32), pltpu.VMEM((3, blocks, 128), F32),
            pltpu.VMEM((blocks, 128), F32), pltpu.VMEM((blocks, 128), F32), pltpu.VMEM((blocks, 128), F32),
            pltpu.VMEM((1, planes), I32), pltpu.VMEM((prow, 128), I32),
            pltpu.VMEM((rows_y, planes, width), F32), pltpu.VMEM(gas, F32),
            pltpu.VMEM((1, 1, 128), I32), pltpu.VMEM((1, 128), I32), pltpu.VMEM((ng, nt, 1, 128), I32),
            pltpu.VMEM(slab, BF16), pltpu.VMEM((sources,) + slab[1:], BF16),
            pltpu.VMEM((2, nf, planes, width), BF16),
            pltpu.VMEM((nf, planes, width), BF16), pltpu.VMEM((nf, planes, width), BF16),
            pltpu.VMEM((rows, width), BF16), pltpu.VMEM((rows, width), BF16),
            pltpu.VMEM((rows, width), BF16), pltpu.VMEM((rows, width), BF16),
            dma((2,)), dma((rows_y,)), dma((rows_y,)), dma((5,)),
            dma((nt,)), dma((sources,)), dma((nt - 1,)), dma((nt - 1,)),
            dma((ng - 1,)), dma((ng - 1,)), dma((4,)), dma((4,)), dma((2,)),
        ],
        compiler_params=pltpu.CompilerParams(
            collective_id=0, has_side_effects=True, vmem_limit_bytes=24 << 20
        ),
        name="gas",
    )(living_spray_batches, *(pltpu.with_memory_space_constraint(a, pltpu.MemorySpace.HBM) for a in (
        holder_unit.reshape(1, planes), flow_fields, turbulent_diffusivity,
        patch_pick_unreduced.reshape(prow, 128), spray_volume_position[0],
        droplet_motion[0].transpose(1, 0, 2), droplet_warmth[0], droplet_weightiness[0],
        droplet_multiplicity[0],
    )))
    acc = pl.pallas_call(
        functools.partial(parcel_kernel, nf, rows_y),
        out_shape=shape(((slots + 1) * PITCH + 7, width), F32),
        in_specs=[VMEM] * 3, out_specs=VMEM,
        scratch_shapes=[
            pltpu.VMEM((24 * (BATCH + 1), width), F32),
            pltpu.VMEM((ROW * (BATCH + 1), width), F32),
            pltpu.VMEM((BATCH * PITCH, width), F32),
            pltpu.VMEM((BATCH, width), F32),
            pltpu.VMEM((BATCH * 24, width), F32),
            pltpu.SMEM((lists, 128), I32),
            dma,
        ],
        compiler_params=pltpu.CompilerParams(vmem_limit_bytes=24 << 20),
        name="parcels",
    )(ints, table, parcels)
    recv = pl.pallas_call(
        functools.partial(return_kernel, ng, nt),
        out_shape=shape(slab, BF16),
        in_specs=[VMEM], out_specs=VMEM,
        scratch_shapes=[
            pltpu.VMEM((sources,) + slab[1:], BF16), dma((sources,)), dma((nt,)), dma,
        ],
        compiler_params=pltpu.CompilerParams(
            collective_id=1, has_side_effects=True, vmem_limit_bytes=16 << 20
        ),
        name="return",
    )(acc)
    return pl.pallas_call(
        functools.partial(place_kernel, ng, nt, nf),
        out_shape=shape((nf, planes, rows_y, width), F32),
        in_specs=[VMEM] * 3, out_specs=HBM,
        scratch_shapes=[pltpu.VMEM(gas, F32), dma((rows,))],
        compiler_params=pltpu.CompilerParams(vmem_limit_bytes=12 << 20),
        name="place",
    )(recv, placer, part)


def solution(mesh):
    in_specs = (
        P(None, "tile", "grp", None),
        P("tile", "grp", None),
        P("grp", "tile", None),
        P("tile", None, None),
        P("tile", None),
        P("tile", None, None, None),
        P("tile", None, None),
        P("tile", None, None),
        P("tile", None, None),
        P("tile"),
    )
    out_specs = P(None, "tile", "grp", None)
    return jax.shard_map(local, mesh=mesh, in_specs=in_specs, out_specs=out_specs, check_vma=False)
```

```python
import functools

import jax
import jax.numpy as jnp
from jax import lax
from jax.experimental import pallas as pl
from jax.experimental.pallas import tpu as pltpu
from jax.sharding import PartitionSpec as P

MESH = pl.DeviceIdType.MESH
SLOTS = 8
BATCH = 64
HBM = pl.BlockSpec(memory_space=pltpu.MemorySpace.HBM)
VMEM = pl.BlockSpec(memory_space=pltpu.VMEM)
SMEM = pl.BlockSpec(memory_space=pltpu.SMEM)
F32, BF16, I32 = jnp.float32, jnp.bfloat16, jnp.int32


ROW = 8
PITCH = 25
SHARE = 4


def say_in(peer):
    pl.semaphore_signal(pltpu.get_barrier_semaphore(), inc=1, device_id=peer, device_id_type=MESH)


def wrap(x, n):
    return x - jnp.where(x >= n, n, 0)


def source(ng, nt, s):
    g, p = lax.axis_index("grp"), lax.axis_index("tile")
    spare = g == ng - 1
    e = jnp.where(spare, s // (ng - 1) * SHARE + SHARE - 1, s + s // (SHARE - 1))
    return jnp.where(spare, s % (ng - 1), g), wrap(e - p + nt, nt)


def home(ng, nt, p):
    g = lax.axis_index("grp")
    e = wrap(lax.axis_index("tile") + p, nt)
    quarter = lax.div(e, SHARE)
    shared = e - quarter * SHARE == SHARE - 1
    return jnp.where(shared, ng - 1, g), jnp.where(shared, quarter * (ng - 1) + g, e - quarter)


def send_to(src, dst, ss, rs, dev):
    c = pltpu.make_async_remote_copy(
        src_ref=src, dst_ref=dst, send_sem=ss, recv_sem=rs, device_id=dev, device_id_type=MESH
    )
    c.start()
    return c


def start_all(pairs, sems):
    loads = [pltpu.make_async_copy(a, b, sems.at[k]) for k, (a, b) in enumerate(pairs)]
    for c in loads:
        c.start()
    return loads


def block_list(ng, nt, owners, pick, live):
    p = lax.axis_index("tile")
    prow = pick.shape[0]
    sources = nt * (SHARE - 1) // SHARE
    slots = sources * SLOTS
    owned = jnp.where(owners == p, 1, 0)
    counts = jnp.sum(owned, axis=1, keepdims=True)
    which = lax.broadcasted_iota(I32, counts.shape, 0)
    counts = jnp.where(which < (ng - 1) * nt, counts, 0)
    total = jnp.maximum(jnp.sum(counts, axis=0, keepdims=True), 1)
    total_f = total.astype(F32)
    quotient = jnp.floor(pick.astype(F32) / total_f).astype(I32)
    left = pick - quotient * total
    left = jnp.where(left < 0, left + total, left)
    left = jnp.where(left >= total, left - total, left)
    slot = jnp.full(pick.shape, -1, I32)
    for k in range(sources):
        from_g, from_d = source(ng, nt, k)
        number = from_g * nt + from_d
        low = jnp.sum(jnp.where(which < number, counts, 0), axis=0, keepdims=True)
        size = jnp.sum(jnp.where(which == number, counts, 0), axis=0, keepdims=True)
        rank = left - low
        slot = jnp.where((rank >= 0) & (rank < size), rank + k * SLOTS, slot)
    row = lax.broadcasted_iota(I32, (prow, 128), 0)
    lane = lax.broadcasted_iota(I32, (prow, 128), 1)
    number = row * 128 + lane
    inside = (slot >= 0) & (number < live)
    flags = jnp.where(inside, 1, 0)
    square_a = lax.broadcasted_iota(I32, (128, 128), 0)
    square_b = lax.broadcasted_iota(I32, (128, 128), 1)
    before = jnp.where(square_a < square_b, 1.0, 0.0).astype(BF16)
    flags_low = flags.astype(F32).astype(BF16)
    place = jnp.dot(flags_low, before, preferred_element_type=F32).astype(I32)
    sums = jnp.sum(flags, axis=1, keepdims=True)
    start = jnp.zeros((1, 1), I32)
    listed = jnp.zeros((3 * prow, 128), F32)
    lane_f, slot_f = lane[0:1].astype(F32), slot.astype(F32)
    for i in range(prow):
        at = jnp.where(inside[i : i + 1], place[i : i + 1] + start, -1)
        goes = row == (at >> 7)
        parts = [
            jnp.where(goes, v, 0.0) for v in (slot_f[i : i + 1], jnp.full((1, 128), float(i), F32), lane_f)
        ]
        spot = jnp.where(square_a == (at & 127), 1.0, 0.0).astype(BF16)
        listed += lax.dot_general(
            jnp.concatenate(parts, axis=0).astype(BF16), spot, (((1,), (1,)), ((), ())),
            preferred_element_type=F32,
        )
        start = start + sums[i : i + 1]
    listed = listed.astype(I32)
    block = listed[prow : 2 * prow] * 128 + listed[2 * prow :]
    entry = ((listed[0:prow] * PITCH) << 16) + block * (ROW + 1)
    return jnp.where(number < start, entry, (slots * PITCH) << 16), start


def gas_kernel(
    ng, nt, nf, live_ref, holder_hbm, flow_hbm, nu_hbm, pick_hbm, pos_hbm, mot_hbm, warm_hbm, mass_hbm, mult_hbm,
    table_ref, ints_ref, part_ref, placer_ref, parcel_ref,
    pos_ref, mot_ref, warm_ref, mass_ref, mult_ref, holder_ref, pick_ref, nu_ref, gas_ref, own_ref, twice_ref, all_ref, send_ref, recv_ref,
    edge_ref, ylo_ref, yhi_ref, first_ref, last_ref, xlo_ref, xhi_ref,
    small_sem, gas_sem, nu_sem, bulk_sem, tile_s, tile_r, own_s, own_r, own2_s, own2_r, halo_s, halo_r, local_sem,
):
    g, t = lax.axis_index("grp"), lax.axis_index("tile")
    rows, planes, width = gas_ref.shape
    rows_y = rows // nf
    sources = recv_ref.shape[0]
    small = start_all([(holder_hbm, holder_ref), (pick_hbm, pick_ref)], small_sem)
    gas_loads = start_all(
        [(flow_hbm.at[:, :, y, :], gas_ref.at[pl.ds(y * nf, nf)]) for y in range(rows_y)], gas_sem
    )
    grp_peers = [(wrap(g + k, ng), t) for k in range(1, ng)]
    tile_peers = [(g, wrap(t + k, nt)) for k in range(1, nt)]
    for peer in grp_peers + tile_peers:
        say_in(peer)

    @pl.when(g == ng - 1)
    def _():
        for k in range(sources):
            say_in(source(ng, nt, k))

    targets = ng + nt - 2 + jnp.where(g < ng - 1, nt // SHARE, 0)
    pairs = [(pos_hbm, pos_ref), (warm_hbm, warm_ref), (mass_hbm, mass_ref), (mult_hbm, mult_ref)]
    pairs += [(mot_hbm, mot_ref)]
    bulk = start_all(pairs, bulk_sem)
    nu_loads = start_all([(nu_hbm.at[:, y, :], nu_ref.at[y]) for y in range(rows_y)], nu_sem)
    partners = [wrap(t + k, nt) for k in range(nt)]
    homes = [home(ng, nt, p) for p in partners]

    own_ref[0] = jnp.full((1, 128), -1, I32)
    twice_ref[...] = jnp.full((1, 128), -1, I32)
    for c in small:
        c.wait()
    own_ref[0, :, 0:planes] = holder_ref[...]
    own = own_ref[0]
    twice_ref[:, 0:planes] = holder_ref[...]
    twice_ref[:, planes : 2 * planes] = holder_ref[...]
    both = twice_ref[...]
    row = jnp.broadcast_to(both, (128, 128))
    col = row.T
    s = lax.broadcasted_iota(I32, (128, 128), 0)
    l = lax.broadcasted_iota(I32, (128, 128), 1)
    near = (col == row) & ((s >= planes) == (l >= planes))
    rank = jnp.sum(jnp.where(near & (s < l), 1, 0), axis=0, keepdims=True)
    rank_col = jnp.sum(jnp.where(near & (l < s), 1, 0), axis=1, keepdims=True)
    lanes = lax.broadcasted_iota(I32, (1, 128), 1)
    subs = lax.broadcasted_iota(I32, (128, 1), 0)
    goal = both * (2 * SLOTS) + rank + jnp.where(lanes >= planes, SLOTS, 0)
    goal_col = col[:, 0:1] * (2 * SLOTS) + rank_col + jnp.where(subs >= planes, SLOTS, 0)
    picker = jnp.where(
        goal[:, 0 : 2 * planes] == lax.broadcasted_iota(I32, (nt * 2 * SLOTS, 2 * planes), 0), 1.0, 0.0
    ).astype(BF16)
    placer_ref[...] = jnp.where(
        goal_col[0 : 2 * planes] == lax.broadcasted_iota(I32, (2 * planes, nt * 2 * SLOTS), 1), 1.0, 0.0
    ).astype(BF16)
    for c in gas_loads:
        c.wait()
    for r in range(0, rows, 2):
        low = jnp.concatenate([gas_ref[r], gas_ref[r + 1]], axis=0).astype(BF16)
        got = jnp.dot(picker, low, preferred_element_type=F32).astype(BF16)
        for o in range(nt):
            send_ref[o, r * SLOTS : (r + 2) * SLOTS, :] = got[o * 2 * SLOTS : (o + 1) * 2 * SLOTS]

    pl.semaphore_wait(pltpu.get_barrier_semaphore(), targets)
    own_copies = [
        send_to(own_ref.at[0], all_ref.at[g, t], own_s.at[k], own_r.at[k], peer)
        for k, peer in enumerate(tile_peers)
    ]
    mine = pltpu.make_async_copy(own_ref.at[0], all_ref.at[g, t], local_sem.at[0])
    mine.start()
    gives = g < ng - 1

    def slab(k):
        p, (to_g, at) = partners[k], homes[k]
        return pltpu.make_async_remote_copy(
            src_ref=send_ref.at[p], dst_ref=recv_ref.at[at], send_sem=tile_s.at[k],
            recv_sem=tile_r.at[at], device_id=(to_g, p), device_id_type=MESH,
        )

    kept = pltpu.make_async_copy(send_ref.at[t], recv_ref.at[homes[0][1]], local_sem.at[1])

    @pl.when(gives)
    def _():
        for k in range(1, nt):
            slab(k).start()
        kept.start()

    mine.wait()
    for c in own_copies:
        c.wait_recv()
    own2_copies = [
        send_to(all_ref.at[g], all_ref.at[g], own2_s.at[k], own2_r.at[k], peer)
        for k, peer in enumerate(grp_peers)
    ]
    gas_side = jnp.where(g < ng - 1, 1.0, 0.0).astype(F32)
    edge_ref[0] = (gas_ref[rows - nf : rows] * gas_side).astype(BF16)
    edge_ref[1] = (gas_ref[0:nf] * gas_side).astype(BF16)
    first_ref[...] = gas_ref[:, 0, :].astype(BF16)
    last_ref[...] = gas_ref[:, planes - 1, :].astype(BF16)
    halos = [
        send_to(edge_ref.at[0], ylo_ref, halo_s.at[0], halo_r.at[0], grp_peers[0]),
        send_to(edge_ref.at[1], yhi_ref, halo_s.at[1], halo_r.at[1], grp_peers[-1]),
        send_to(last_ref, xlo_ref, halo_s.at[2], halo_r.at[2], tile_peers[0]),
        send_to(first_ref, xhi_ref, halo_s.at[3], halo_r.at[3], tile_peers[-1]),
    ]
    table_ref[...] = jnp.zeros_like(table_ref)
    for c in bulk:
        c.wait()

    @pl.loop(0, pos_ref.shape[0] // 8)
    def _(k):
        at = pl.ds(pl.multiple_of(k * 8, 8), 8)
        cell = pos_ref[at, :]
        values = [mot_ref[f, at, :] for f in range(3)] + [warm_ref[at, :], mass_ref[at, :], mult_ref[at, :]]
        values += [(cell & 127).astype(F32), (cell >> 7).astype(F32)]
        for f, v in enumerate(values):
            parcel_ref[pl.ds(k * 8 * (ROW + 1) + f, 8, stride=ROW + 1), :] = v

    for c in own2_copies:
        c.wait_recv()
    owners = jnp.concatenate([all_ref[k].reshape(nt, 128) for k in range(ng)], axis=0)
    entries, number = block_list(ng, nt, owners, pick_ref[...], live_ref[0])
    prow, spans = entries.shape[0], 128 // BATCH
    for k in range(spans):
        here = entries if k == 0 else pltpu.roll(entries, 128 - k * BATCH, 1)
        ints_ref[pl.ds(k, prow, stride=spans), :] = here
    ints_ref[prow * spans : prow * spans + 8, :] = jnp.broadcast_to(number, (8, 128))

    for c in nu_loads:
        c.wait()
    for c in halos:
        c.wait_recv()
    sub = lax.broadcasted_iota(I32, (planes, width), 0)
    lane = lax.broadcasted_iota(I32, (planes, width), 1)
    has_low = jnp.where(t > 0, 1.0, 0.0).astype(F32)
    has_high = jnp.where(t < nt - 1, 1.0, 0.0).astype(F32)
    x_low = xlo_ref[...].astype(F32) * has_low
    x_high = xhi_ref[...].astype(F32) * has_high
    for r in range(rows):
        mid = gas_ref[r]
        below = gas_ref[r - nf] if r >= nf else ylo_ref[r].astype(F32)
        above = gas_ref[r + nf] if r < rows - nf else yhi_ref[r - (rows - nf)].astype(F32)
        total = below + above
        total += jnp.where(sub == 0, x_low[r : r + 1], pltpu.roll(mid, 1, 0))
        total += jnp.where(sub == planes - 1, x_high[r : r + 1], pltpu.roll(mid, planes - 1, 0))
        total += jnp.where(lane == 0, 0.0, pltpu.roll(mid, 1, 1))
        total += jnp.where(lane == width - 1, 0.0, pltpu.roll(mid, width - 1, 1))
        part_ref[r] = (mid + 0.5 * nu_ref[r // nf] * (total - 6.0 * mid)) * gas_side

    def unpack(d):
        for r in range(0, rows, 2):
            both = recv_ref[d, r * SLOTS : (r + 2) * SLOTS, :].astype(F32)
            for h in range(2):
                table_ref[pl.ds(d * SLOTS * PITCH + r + h, SLOTS, stride=PITCH), :] = both[h * SLOTS : (h + 1) * SLOTS]

    @pl.when(gives)
    def _():
        kept.wait()

    for k in range(sources):
        from_g, from_d = source(ng, nt, k)

        @pl.when((from_g != g) | (from_d != t))
        def _():
            pltpu.make_async_remote_copy(
                src_ref=send_ref.at[0], dst_ref=recv_ref.at[k], send_sem=tile_s.at[0],
                recv_sem=tile_r.at[k], device_id=(from_g, from_d), device_id_type=MESH,
            ).wait_recv()

        unpack(k)

    @pl.when(gives)
    def _():
        for k in range(1, nt):
            slab(k).wait_send()
    for c in own_copies + own2_copies + halos:
        c.wait_send()


def sources_of(field, own):
    v0, v1, v2, warm, mass, mult = own
    r0, r1, r2 = field[0] - v0, field[1] - v1, field[2] - v2
    speed_sq = r0 * r0 + r1 * r1 + r2 * r2
    inv_surface = jnp.exp(jnp.log(mass) * (-2.0 / 3.0))
    inverse_tau = 0.8 * (1.0 + 0.15 * jnp.exp(0.3435 * jnp.log(1.0 + speed_sq))) * inv_surface
    relax = 1.0 - jnp.exp(-0.5 * inverse_tau)
    heating = 1.0 / (1.0 + jnp.exp(field[4] - field[3]))
    remain = jnp.exp(-0.3 * heating * inv_surface)
    new_mass = mass * remain
    warming = 1.0 - jnp.exp(-0.25 * inverse_tau)
    new_warm = warm + warming * (field[3] - warm) - 0.5 * (1.0 - remain)
    outs = [mass * v - new_mass * (v + relax * r) for v, r in ((v0, r0), (v1, r1), (v2, r2))]
    outs += [mass * warm - new_mass * new_warm, mass - new_mass]
    return [mult * o for o in outs]


def parcel_kernel(nf, rows_y, ints_ref, table, parcels, acc, seen, par, src, cells, add, smem, sem):
    to_smem = pltpu.make_async_copy(ints_ref, smem, sem)
    to_smem.start()
    span = BATCH + 1
    acc[...] = jnp.zeros_like(acc)
    src[...] = jnp.zeros_like(src)
    to_smem.wait()

    n = smem[smem.shape[0] - 8, 0]
    sub = lax.broadcasted_iota(I32, (128, 128), 0).astype(F32).astype(BF16)
    yes, no = jnp.ones((128, 128), BF16), jnp.zeros((128, 128), BF16)
    spare = jnp.zeros((8, 128), F32)
    zero = jnp.zeros((32, 128), BF16)

    def gather(step, c):
        for i in range(c, c + 8):
            v = smem[step, i]
            b, base = v & 65535, v >> 16
            z = jnp.broadcast_to(parcels[pl.ds(b + 6, 1), :], (8, 128)).astype(I32)
            for k in range(3):
                seen[pl.ds(k * 8 * span + i, 8, stride=span), :] = jnp.take_along_axis(
                    table[pl.ds(base + k * 8, 8), :], z, axis=1, mode="promise_in_bounds",
                    wrap_negative_indices=False,
                )
            par[pl.ds(i, 8, stride=span), :] = parcels[pl.ds(b, 8), :]

    def work(size):
        for c in range(0, size, 8):
            own = [par[f * span + c : f * span + c + 8, :] for f in range(ROW)]
            y = own[7]
            cells[c : c + 8, :] = own[6]
            gas = []
            for f in range(nf):
                at = [seen[(k * nf + f) * span + c : (k * nf + f) * span + c + 8, :] for k in range(rows_y)]
                value = at[0]
                for k in range(1, rows_y):
                    value = jnp.where(y < k, value, at[k])
                gas.append(value)
            outs = sources_of(gas, own[0:6])
            for k in range(rows_y):
                here = y == k
                for f in range(nf):
                    src[pl.ds(c * PITCH + k * nf + f, 8, stride=PITCH), :] = jnp.where(here, outs[f], 0.0)

    def deposit(c):
        for j in range(c, c + 8, 2):
            left, hot = [], []
            for i in (j, j + 1):
                z = jnp.broadcast_to(cells[i : i + 1, :], (16, 128)).astype(BF16)
                hot.append(jnp.where(sub == jnp.concatenate([z] * 8, axis=0), yes, no))
                mine = jnp.concatenate([src[i * PITCH : i * PITCH + 24, :], spare], axis=0).astype(BF16)
                left.append(jnp.concatenate([mine, zero] if i == j else [zero, mine], axis=1))
            added = lax.dot_general(
                jnp.concatenate(left, axis=0), jnp.concatenate(hot, axis=1), (((1,), (1,)), ((), ())),
                preferred_element_type=F32,
            )
            for i in (j, j + 1):
                add[i * 24 : (i + 1) * 24, :] = added[(i - j) * 32 : (i - j) * 32 + 24]

    def fold(step, size):
        for i in range(size):
            at = pl.ds(smem[step, i] >> 16, 24)
            acc[at, :] = acc[at, :] + add[i * 24 : (i + 1) * 24, :]

    rest = lax.rem(n, BATCH)
    whole = n // BATCH + jnp.where(rest > BATCH // 2, 1, 0)

    @pl.when(whole > 0)
    def _():
        for c in range(0, BATCH, 8):
            gather(0, c)
        work(BATCH)

        @pl.loop(1, whole)
        def _(step):
            for c in range(0, BATCH, 8):
                deposit(c)
                gather(step, c)
            fold(step - 1, BATCH)
            work(BATCH)

        for c in range(0, BATCH, 8):
            deposit(c)
        fold(whole - 1, BATCH)

    @pl.when((rest > 0) & (rest <= BATCH // 2))
    def _():
        for c in range(0, BATCH // 2, 8):
            gather(whole, c)
        work(BATCH // 2)
        for c in range(0, BATCH // 2, 8):
            deposit(c)
        fold(whole, BATCH // 2)


def return_kernel(ng, nt, acc_ref, recv_ref, send_ref, tile_s, tile_r, local_sem):
    g, t = lax.axis_index("grp"), lax.axis_index("tile")
    sources, rows, _ = send_ref.shape
    takes = g < ng - 1

    @pl.when(takes)
    def _():
        for k in range(1, nt):
            p = wrap(t + k, nt)
            say_in((home(ng, nt, p)[0], p))

    origins = [source(ng, nt, k) for k in range(sources)]
    remote = [(to_g != g) | (to_d != t) for to_g, to_d in origins]
    for d in range(sources):
        for r in range(0, rows // SLOTS, 2):
            pair = [
                acc_ref[pl.ds(d * SLOTS * PITCH + q, SLOTS, stride=PITCH), :]
                for q in (r, r + 1)
            ]
            send_ref[d, r * SLOTS : (r + 2) * SLOTS, :] = jnp.concatenate(pair, axis=0).astype(BF16)
    def slab(k):
        return pltpu.make_async_remote_copy(
            src_ref=send_ref.at[k], dst_ref=recv_ref.at[t], send_sem=tile_s.at[k],
            recv_sem=tile_r.at[t], device_id=origins[k], device_id_type=MESH,
        )

    pl.semaphore_wait(pltpu.get_barrier_semaphore(), sources - jnp.where(takes, 1, 0))
    for k in range(sources):

        @pl.when(remote[k])
        def _():
            slab(k).start()

    kept = pltpu.make_async_copy(send_ref.at[home(ng, nt, t)[1]], recv_ref.at[t], local_sem)

    @pl.when(takes)
    def _():
        kept.start()
        kept.wait()
        for k in range(1, nt):
            p = wrap(t + k, nt)
            pltpu.make_async_remote_copy(
                src_ref=send_ref.at[0], dst_ref=recv_ref.at[p], send_sem=tile_s.at[0],
                recv_sem=tile_r.at[p], device_id=(home(ng, nt, p)[0], p), device_id_type=MESH,
            ).wait_recv()

    @pl.when(jnp.logical_not(takes))
    def _():
        recv_ref[...] = jnp.zeros_like(recv_ref)

    for k in range(sources):

        @pl.when(remote[k])
        def _():
            slab(k).wait_send()


def place_kernel(ng, nt, nf, recv_ref, placer_ref, part_ref, out_hbm, buf, sem):
    rows, planes, width = part_ref.shape
    gas_side = lax.axis_index("grp") < ng - 1
    placer = placer_ref[...]
    copies = []
    for r in range(0, rows, 2):
        inc = jnp.concatenate([recv_ref[d, r * SLOTS : (r + 2) * SLOTS, :] for d in range(nt)], axis=0)
        placed = jnp.dot(placer, inc, preferred_element_type=F32)
        for h in range(2):
            q = r + h
            buf[q] = part_ref[q] + jnp.where(gas_side, placed[h * planes : (h + 1) * planes], 0.0)
            c = pltpu.make_async_copy(buf.at[q], out_hbm.at[q % nf, :, q // nf, :], sem.at[q])
            c.start()
            copies.append(c)
    for c in copies:
        c.wait()


def local(
    flow_fields, turbulent_diffusivity, holder_unit, spray_volume_position, patch_pick_unreduced,
    droplet_motion, droplet_warmth, droplet_weightiness, droplet_multiplicity, living_spray_batches,
):
    ng, nt = lax.axis_size("grp"), lax.axis_size("tile")
    nf, planes, rows_y, width = flow_fields.shape
    rows = nf * rows_y
    dma = pltpu.SemaphoreType.DMA
    shape = jax.ShapeDtypeStruct
    blocks = spray_volume_position.shape[1]
    sources = nt * (SHARE - 1) // SHARE
    slots = sources * SLOTS
    prow = blocks // 128
    lists = blocks // BATCH + 8
    slab = (nt, rows * SLOTS, width)
    gas = (rows, planes, width)
    table, ints, part, placer, parcels = pl.pallas_call(
        functools.partial(gas_kernel, ng, nt, nf),
        out_shape=(
            shape(((slots + 1) * PITCH + 7, width), F32), shape((lists, 128), I32), shape(gas, F32),
            shape((2 * planes, nt * 2 * SLOTS), BF16), shape((blocks * (ROW + 1), 128), F32),
        ),
        in_specs=[SMEM] + [HBM] * 9, out_specs=(VMEM,) * 5,
        scratch_shapes=[
            pltpu.VMEM((blocks, 128), I32), pltpu.VMEM((3, blocks, 128), F32),
            pltpu.VMEM((blocks, 128), F32), pltpu.VMEM((blocks, 128), F32), pltpu.VMEM((blocks, 128), F32),
            pltpu.VMEM((1, planes), I32), pltpu.VMEM((prow, 128), I32),
            pltpu.VMEM((rows_y, planes, width), F32), pltpu.VMEM(gas, F32),
            pltpu.VMEM((1, 1, 128), I32), pltpu.VMEM((1, 128), I32), pltpu.VMEM((ng, nt, 1, 128), I32),
            pltpu.VMEM(slab, BF16), pltpu.VMEM((sources,) + slab[1:], BF16),
            pltpu.VMEM((2, nf, planes, width), BF16),
            pltpu.VMEM((nf, planes, width), BF16), pltpu.VMEM((nf, planes, width), BF16),
            pltpu.VMEM((rows, width), BF16), pltpu.VMEM((rows, width), BF16),
            pltpu.VMEM((rows, width), BF16), pltpu.VMEM((rows, width), BF16),
            dma((2,)), dma((rows_y,)), dma((rows_y,)), dma((5,)),
            dma((nt,)), dma((sources,)), dma((nt - 1,)), dma((nt - 1,)),
            dma((ng - 1,)), dma((ng - 1,)), dma((4,)), dma((4,)), dma((2,)),
        ],
        compiler_params=pltpu.CompilerParams(
            collective_id=0, has_side_effects=True, vmem_limit_bytes=24 << 20
        ),
        name="gas",
    )(living_spray_batches, *(pltpu.with_memory_space_constraint(a, pltpu.MemorySpace.HBM) for a in (
        holder_unit.reshape(1, planes), flow_fields, turbulent_diffusivity,
        patch_pick_unreduced.reshape(prow, 128), spray_volume_position[0],
        droplet_motion[0].transpose(1, 0, 2), droplet_warmth[0], droplet_weightiness[0],
        droplet_multiplicity[0],
    )))
    acc = pl.pallas_call(
        functools.partial(parcel_kernel, nf, rows_y),
        out_shape=shape(((slots + 1) * PITCH + 7, width), F32),
        in_specs=[VMEM] * 3, out_specs=VMEM,
        scratch_shapes=[
            pltpu.VMEM((24 * (BATCH + 1), width), F32),
            pltpu.VMEM((ROW * (BATCH + 1), width), F32),
            pltpu.VMEM((BATCH * PITCH, width), F32),
            pltpu.VMEM((BATCH, width), F32),
            pltpu.VMEM((BATCH * 24, width), F32),
            pltpu.SMEM((lists, 128), I32),
            dma,
        ],
        compiler_params=pltpu.CompilerParams(vmem_limit_bytes=24 << 20),
        name="parcels",
    )(ints, table, parcels)
    recv = pl.pallas_call(
        functools.partial(return_kernel, ng, nt),
        out_shape=shape(slab, BF16),
        in_specs=[VMEM], out_specs=VMEM,
        scratch_shapes=[
            pltpu.VMEM((sources,) + slab[1:], BF16), dma((sources,)), dma((nt,)), dma,
        ],
        compiler_params=pltpu.CompilerParams(
            collective_id=1, has_side_effects=True, vmem_limit_bytes=16 << 20
        ),
        name="return",
    )(acc)
    return pl.pallas_call(
        functools.partial(place_kernel, ng, nt, nf),
        out_shape=shape((nf, planes, rows_y, width), F32),
        in_specs=[VMEM] * 3, out_specs=HBM,
        scratch_shapes=[pltpu.VMEM(gas, F32), dma((rows,))],
        compiler_params=pltpu.CompilerParams(vmem_limit_bytes=12 << 20),
        name="place",
    )(recv, placer, part)


def solution(mesh):
    in_specs = (
        P(None, "tile", "grp", None),
        P("tile", "grp", None),
        P("grp", "tile", None),
        P("tile", None, None),
        P("tile", None),
        P("tile", None, None, None),
        P("tile", None, None),
        P("tile", None, None),
        P("tile", None, None),
        P("tile"),
    )
    out_specs = P(None, "tile", "grp", None)
    return jax.shard_map(local, mesh=mesh, in_specs=in_specs, out_specs=out_specs, check_vma=False)
```

```python
import functools

import jax
import jax.numpy as jnp
from jax import lax
from jax.experimental import pallas as pl
from jax.experimental.pallas import tpu as pltpu
from jax.sharding import PartitionSpec as P

MESH = pl.DeviceIdType.MESH
SLOTS = 8
BATCH = 64
HBM = pl.BlockSpec(memory_space=pltpu.MemorySpace.HBM)
VMEM = pl.BlockSpec(memory_space=pltpu.VMEM)
SMEM = pl.BlockSpec(memory_space=pltpu.SMEM)
F32, BF16, I32 = jnp.float32, jnp.bfloat16, jnp.int32


ROW = 8
PITCH = 25
SHARE = 4


def say_in(peer):
    pl.semaphore_signal(pltpu.get_barrier_semaphore(), inc=1, device_id=peer, device_id_type=MESH)


def wrap(x, n):
    return x - jnp.where(x >= n, n, 0)


def source(ng, nt, s):
    g, p = lax.axis_index("grp"), lax.axis_index("tile")
    spare = g == ng - 1
    e = jnp.where(spare, s // (ng - 1) * SHARE + SHARE - 1, s + s // (SHARE - 1))
    return jnp.where(spare, s % (ng - 1), g), wrap(e - p + nt, nt)


def home(ng, nt, p):
    g = lax.axis_index("grp")
    e = wrap(lax.axis_index("tile") + p, nt)
    quarter = lax.div(e, SHARE)
    shared = e - quarter * SHARE == SHARE - 1
    return jnp.where(shared, ng - 1, g), jnp.where(shared, quarter * (ng - 1) + g, e - quarter)


def send_to(src, dst, ss, rs, dev):
    c = pltpu.make_async_remote_copy(
        src_ref=src, dst_ref=dst, send_sem=ss, recv_sem=rs, device_id=dev, device_id_type=MESH
    )
    c.start()
    return c


def start_all(pairs, sems):
    loads = [pltpu.make_async_copy(a, b, sems.at[k]) for k, (a, b) in enumerate(pairs)]
    for c in loads:
        c.start()
    return loads


def block_list(ng, nt, owners, pick, live):
    p = lax.axis_index("tile")
    prow = pick.shape[0]
    sources = nt * (SHARE - 1) // SHARE
    slots = sources * SLOTS
    owned = jnp.where(owners == p, 1, 0)
    counts = jnp.sum(owned, axis=1, keepdims=True)
    which = lax.broadcasted_iota(I32, counts.shape, 0)
    counts = jnp.where(which < (ng - 1) * nt, counts, 0)
    total = jnp.maximum(jnp.sum(counts, axis=0, keepdims=True), 1)
    total_f = total.astype(F32)
    quotient = jnp.floor(pick.astype(F32) / total_f).astype(I32)
    left = pick - quotient * total
    left = jnp.where(left < 0, left + total, left)
    left = jnp.where(left >= total, left - total, left)
    slot = jnp.full(pick.shape, -1, I32)
    for k in range(sources):
        from_g, from_d = source(ng, nt, k)
        number = from_g * nt + from_d
        low = jnp.sum(jnp.where(which < number, counts, 0), axis=0, keepdims=True)
        size = jnp.sum(jnp.where(which == number, counts, 0), axis=0, keepdims=True)
        rank = left - low
        slot = jnp.where((rank >= 0) & (rank < size), rank + k * SLOTS, slot)
    row = lax.broadcasted_iota(I32, (prow, 128), 0)
    lane = lax.broadcasted_iota(I32, (prow, 128), 1)
    number = row * 128 + lane
    inside = (slot >= 0) & (number < live)
    flags = jnp.where(inside, 1, 0)
    square_a = lax.broadcasted_iota(I32, (128, 128), 0)
    square_b = lax.broadcasted_iota(I32, (128, 128), 1)
    before = jnp.where(square_a < square_b, 1.0, 0.0).astype(BF16)
    flags_low = flags.astype(F32).astype(BF16)
    place = jnp.dot(flags_low, before, preferred_element_type=F32).astype(I32)
    sums = jnp.sum(flags, axis=1, keepdims=True)
    start = jnp.zeros((1, 1), I32)
    listed = jnp.zeros((3 * prow, 128), F32)
    lane_f, slot_f = lane[0:1].astype(F32), slot.astype(F32)
    for i in range(prow):
        at = jnp.where(inside[i : i + 1], place[i : i + 1] + start, -1)
        goes = row == (at >> 7)
        parts = [
            jnp.where(goes, v, 0.0) for v in (slot_f[i : i + 1], jnp.full((1, 128), float(i), F32), lane_f)
        ]
        spot = jnp.where(square_a == (at & 127), 1.0, 0.0).astype(BF16)
        listed += lax.dot_general(
            jnp.concatenate(parts, axis=0).astype(BF16), spot, (((1,), (1,)), ((), ())),
            preferred_element_type=F32,
        )
        start = start + sums[i : i + 1]
    listed = listed.astype(I32)
    block = listed[prow : 2 * prow] * 128 + listed[2 * prow :]
    entry = ((listed[0:prow] * PITCH) << 16) + block * (ROW + 1)
    return jnp.where(number < start, entry, (slots * PITCH) << 16), start


def gas_kernel(
    ng, nt, nf, live_ref, holder_hbm, flow_hbm, nu_hbm, pick_hbm, pos_hbm, mot_hbm, warm_hbm, mass_hbm, mult_hbm,
    table_ref, ints_ref, part_ref, placer_ref, parcel_ref,
    pos_ref, mot_ref, warm_ref, mass_ref, mult_ref, holder_ref, pick_ref, nu_ref, gas_ref, own_ref, twice_ref, all_ref, send_ref, recv_ref,
    edge_ref, ylo_ref, yhi_ref, first_ref, last_ref, xlo_ref, xhi_ref,
    small_sem, gas_sem, nu_sem, bulk_sem, tile_s, tile_r, own_s, own_r, own2_s, own2_r, halo_s, halo_r, local_sem,
):
    g, t = lax.axis_index("grp"), lax.axis_index("tile")
    rows, planes, width = gas_ref.shape
    rows_y = rows // nf
    sources = recv_ref.shape[0]
    small = start_all([(holder_hbm, holder_ref), (pick_hbm, pick_ref)], small_sem)
    gas_loads = start_all(
        [(flow_hbm.at[:, :, y, :], gas_ref.at[pl.ds(y * nf, nf)]) for y in range(rows_y)], gas_sem
    )
    grp_peers = [(wrap(g + k, ng), t) for k in range(1, ng)]
    tile_peers = [(g, wrap(t + k, nt)) for k in range(1, nt)]
    for peer in grp_peers + tile_peers:
        say_in(peer)

    @pl.when(g == ng - 1)
    def _():
        for k in range(sources):
            say_in(source(ng, nt, k))

    targets = ng + nt - 2 + jnp.where(g < ng - 1, nt // SHARE, 0)
    pairs = [(pos_hbm, pos_ref), (warm_hbm, warm_ref), (mass_hbm, mass_ref), (mult_hbm, mult_ref)]
    pairs += [(mot_hbm, mot_ref)]
    bulk = start_all(pairs, bulk_sem)
    nu_loads = start_all([(nu_hbm.at[:, y, :], nu_ref.at[y]) for y in range(rows_y)], nu_sem)
    partners = [wrap(t + k, nt) for k in range(nt)]
    homes = [home(ng, nt, p) for p in partners]

    own_ref[0] = jnp.full((1, 128), -1, I32)
    twice_ref[...] = jnp.full((1, 128), -1, I32)
    for c in small:
        c.wait()
    own_ref[0, :, 0:planes] = holder_ref[...]
    own = own_ref[0]
    twice_ref[:, 0:planes] = holder_ref[...]
    twice_ref[:, planes : 2 * planes] = holder_ref[...]
    both = twice_ref[...]
    row = jnp.broadcast_to(both, (128, 128))
    col = row.T
    s = lax.broadcasted_iota(I32, (128, 128), 0)
    l = lax.broadcasted_iota(I32, (128, 128), 1)
    near = (col == row) & ((s >= planes) == (l >= planes))
    rank = jnp.sum(jnp.where(near & (s < l), 1, 0), axis=0, keepdims=True)
    rank_col = jnp.sum(jnp.where(near & (l < s), 1, 0), axis=1, keepdims=True)
    lanes = lax.broadcasted_iota(I32, (1, 128), 1)
    subs = lax.broadcasted_iota(I32, (128, 1), 0)
    goal = both * (2 * SLOTS) + rank + jnp.where(lanes >= planes, SLOTS, 0)
    goal_col = col[:, 0:1] * (2 * SLOTS) + rank_col + jnp.where(subs >= planes, SLOTS, 0)
    picker = jnp.where(
        goal[:, 0 : 2 * planes] == lax.broadcasted_iota(I32, (nt * 2 * SLOTS, 2 * planes), 0), 1.0, 0.0
    ).astype(BF16)
    placer_ref[...] = jnp.where(
        goal_col[0 : 2 * planes] == lax.broadcasted_iota(I32, (2 * planes, nt * 2 * SLOTS), 1), 1.0, 0.0
    ).astype(BF16)
    for c in gas_loads:
        c.wait()
    for r in range(0, rows, 2):
        low = jnp.concatenate([gas_ref[r], gas_ref[r + 1]], axis=0).astype(BF16)
        got = jnp.dot(picker, low, preferred_element_type=F32).astype(BF16)
        for o in range(nt):
            send_ref[o, r * SLOTS : (r + 2) * SLOTS, :] = got[o * 2 * SLOTS : (o + 1) * 2 * SLOTS]

    pl.semaphore_wait(pltpu.get_barrier_semaphore(), targets)
    own_copies = [
        send_to(own_ref.at[0], all_ref.at[g, t], own_s.at[k], own_r.at[k], peer)
        for k, peer in enumerate(tile_peers)
    ]
    mine = pltpu.make_async_copy(own_ref.at[0], all_ref.at[g, t], local_sem.at[0])
    mine.start()
    gives = g < ng - 1

    def slab(k):
        p, (to_g, at) = partners[k], homes[k]
        return pltpu.make_async_remote_copy(
            src_ref=send_ref.at[p], dst_ref=recv_ref.at[at], send_sem=tile_s.at[k],
            recv_sem=tile_r.at[at], device_id=(to_g, p), device_id_type=MESH,
        )

    kept = pltpu.make_async_copy(send_ref.at[t], recv_ref.at[homes[0][1]], local_sem.at[1])

    @pl.when(gives)
    def _():
        for k in range(1, nt):
            slab(k).start()
        kept.start()

    mine.wait()
    for c in own_copies:
        c.wait_recv()
    own2_copies = [
        send_to(all_ref.at[g], all_ref.at[g], own2_s.at[k], own2_r.at[k], peer)
        for k, peer in enumerate(grp_peers)
    ]
    gas_side = jnp.where(g < ng - 1, 1.0, 0.0).astype(F32)
    edge_ref[0] = (gas_ref[rows - nf : rows] * gas_side).astype(BF16)
    edge_ref[1] = (gas_ref[0:nf] * gas_side).astype(BF16)
    first_ref[...] = gas_ref[:, 0, :].astype(BF16)
    last_ref[...] = gas_ref[:, planes - 1, :].astype(BF16)
    halos = [
        send_to(edge_ref.at[0], ylo_ref, halo_s.at[0], halo_r.at[0], grp_peers[0]),
        send_to(edge_ref.at[1], yhi_ref, halo_s.at[1], halo_r.at[1], grp_peers[-1]),
        send_to(last_ref, xlo_ref, halo_s.at[2], halo_r.at[2], tile_peers[0]),
        send_to(first_ref, xhi_ref, halo_s.at[3], halo_r.at[3], tile_peers[-1]),
    ]
    table_ref[...] = jnp.zeros_like(table_ref)
    for c in bulk:
        c.wait()

    @pl.loop(0, pos_ref.shape[0] // 8)
    def _(k):
        at = pl.ds(pl.multiple_of(k * 8, 8), 8)
        cell = pos_ref[at, :]
        values = [mot_ref[f, at, :] for f in range(3)] + [warm_ref[at, :], mass_ref[at, :], mult_ref[at, :]]
        values += [(cell & 127).astype(F32), (cell >> 7).astype(F32)]
        for f, v in enumerate(values):
            parcel_ref[pl.ds(k * 8 * (ROW + 1) + f, 8, stride=ROW + 1), :] = v

    for c in own2_copies:
        c.wait_recv()
    owners = jnp.concatenate([all_ref[k].reshape(nt, 128) for k in range(ng)], axis=0)
    entries, number = block_list(ng, nt, owners, pick_ref[...], live_ref[0])
    prow, spans = entries.shape[0], 128 // BATCH
    for k in range(spans):
        here = entries if k == 0 else pltpu.roll(entries, 128 - k * BATCH, 1)
        ints_ref[pl.ds(k, prow, stride=spans), :] = here
    ints_ref[prow * spans : prow * spans + 8, :] = jnp.broadcast_to(number, (8, 128))

    for c in nu_loads:
        c.wait()
    for c in halos:
        c.wait_recv()
    sub = lax.broadcasted_iota(I32, (planes, width), 0)
    lane = lax.broadcasted_iota(I32, (planes, width), 1)
    has_low = jnp.where(t > 0, 1.0, 0.0).astype(F32)
    has_high = jnp.where(t < nt - 1, 1.0, 0.0).astype(F32)
    x_low = xlo_ref[...].astype(F32) * has_low
    x_high = xhi_ref[...].astype(F32) * has_high
    for r in range(rows):
        mid = gas_ref[r]
        below = gas_ref[r - nf] if r >= nf else ylo_ref[r].astype(F32)
        above = gas_ref[r + nf] if r < rows - nf else yhi_ref[r - (rows - nf)].astype(F32)
        total = below + above
        total += jnp.where(sub == 0, x_low[r : r + 1], pltpu.roll(mid, 1, 0))
        total += jnp.where(sub == planes - 1, x_high[r : r + 1], pltpu.roll(mid, planes - 1, 0))
        total += jnp.where(lane == 0, 0.0, pltpu.roll(mid, 1, 1))
        total += jnp.where(lane == width - 1, 0.0, pltpu.roll(mid, width - 1, 1))
        part_ref[r] = (mid + 0.5 * nu_ref[r // nf] * (total - 6.0 * mid)) * gas_side

    def unpack(d):
        for r in range(0, rows, 2):
            both = recv_ref[d, r * SLOTS : (r + 2) * SLOTS, :].astype(F32)
            for h in range(2):
                table_ref[pl.ds(d * SLOTS * PITCH + r + h, SLOTS, stride=PITCH), :] = both[h * SLOTS : (h + 1) * SLOTS]

    @pl.when(gives)
    def _():
        kept.wait()

    for k in range(sources):
        from_g, from_d = source(ng, nt, k)

        @pl.when((from_g != g) | (from_d != t))
        def _():
            pltpu.make_async_remote_copy(
                src_ref=send_ref.at[0], dst_ref=recv_ref.at[k], send_sem=tile_s.at[0],
                recv_sem=tile_r.at[k], device_id=(from_g, from_d), device_id_type=MESH,
            ).wait_recv()

        unpack(k)

    @pl.when(gives)
    def _():
        for k in range(1, nt):
            slab(k).wait_send()
    for c in own_copies + own2_copies + halos:
        c.wait_send()


def sources_of(field, own):
    v0, v1, v2, warm, mass, mult = own
    r0, r1, r2 = field[0] - v0, field[1] - v1, field[2] - v2
    speed_sq = r0 * r0 + r1 * r1 + r2 * r2
    inv_surface = jnp.exp(jnp.log(mass) * (-2.0 / 3.0))
    inverse_tau = 0.8 * (1.0 + 0.15 * jnp.exp(0.3435 * jnp.log(1.0 + speed_sq))) * inv_surface
    relax = 1.0 - jnp.exp(-0.5 * inverse_tau)
    heating = 1.0 / (1.0 + jnp.exp(field[4] - field[3]))
    remain = jnp.exp(-0.3 * heating * inv_surface)
    new_mass = mass * remain
    warming = 1.0 - jnp.exp(-0.25 * inverse_tau)
    new_warm = warm + warming * (field[3] - warm) - 0.5 * (1.0 - remain)
    outs = [mass * v - new_mass * (v + relax * r) for v, r in ((v0, r0), (v1, r1), (v2, r2))]
    outs += [mass * warm - new_mass * new_warm, mass - new_mass]
    return [mult * o for o in outs]


def parcel_kernel(nf, rows_y, ints_ref, table, parcels, acc, seen, par, src, cells, add, smem, sem):
    to_smem = pltpu.make_async_copy(ints_ref, smem, sem)
    to_smem.start()
    span = BATCH + 1
    acc[...] = jnp.zeros_like(acc)
    src[...] = jnp.zeros_like(src)
    to_smem.wait()

    n = smem[smem.shape[0] - 8, 0]
    sub = lax.broadcasted_iota(I32, (128, 128), 0).astype(F32).astype(BF16)
    yes, no = jnp.ones((128, 128), BF16), jnp.zeros((128, 128), BF16)
    spare = jnp.zeros((8, 128), F32)
    zero = jnp.zeros((32, 128), BF16)

    def gather(step, c):
        for i in range(c, c + 8):
            v = smem[step, i]
            b, base = v & 65535, v >> 16
            z = jnp.broadcast_to(parcels[pl.ds(b + 6, 1), :], (8, 128)).astype(I32)
            for k in range(3):
                seen[pl.ds(k * 8 * span + i, 8, stride=span), :] = jnp.take_along_axis(
                    table[pl.ds(base + k * 8, 8), :], z, axis=1, mode="promise_in_bounds",
                    wrap_negative_indices=False,
                )
            par[pl.ds(i, 8, stride=span), :] = parcels[pl.ds(b, 8), :]

    def work(size):
        for c in range(0, size, 8):
            own = [par[f * span + c : f * span + c + 8, :] for f in range(ROW)]
            y = own[7]
            cells[c : c + 8, :] = own[6]
            gas = []
            for f in range(nf):
                at = [seen[(k * nf + f) * span + c : (k * nf + f) * span + c + 8, :] for k in range(rows_y)]
                value = at[0]
                for k in range(1, rows_y):
                    value = jnp.where(y < k, value, at[k])
                gas.append(value)
            outs = sources_of(gas, own[0:6])
            for k in range(rows_y):
                here = y == k
                for f in range(nf):
                    src[pl.ds(c * PITCH + k * nf + f, 8, stride=PITCH), :] = jnp.where(here, outs[f], 0.0)

    def deposit(c):
        for j in range(c, c + 8, 2):
            left, hot = [], []
            for i in (j, j + 1):
                z = jnp.broadcast_to(cells[i : i + 1, :], (16, 128)).astype(BF16)
                hot.append(jnp.where(sub == jnp.concatenate([z] * 8, axis=0), yes, no))
                mine = jnp.concatenate([src[i * PITCH : i * PITCH + 24, :], spare], axis=0).astype(BF16)
                left.append(jnp.concatenate([mine, zero] if i == j else [zero, mine], axis=1))
            added = lax.dot_general(
                jnp.concatenate(left, axis=0), jnp.concatenate(hot, axis=1), (((1,), (1,)), ((), ())),
                preferred_element_type=F32,
            )
            for i in (j, j + 1):
                add[i * 24 : (i + 1) * 24, :] = added[(i - j) * 32 : (i - j) * 32 + 24]

    def fold(step, size):
        for i in range(size):
            at = pl.ds(smem[step, i] >> 16, 24)
            acc[at, :] = acc[at, :] + add[i * 24 : (i + 1) * 24, :]

    rest = lax.rem(n, BATCH)
    whole = n // BATCH + jnp.where(rest > BATCH // 2, 1, 0)

    @pl.when(whole > 0)
    def _():
        for c in range(0, BATCH, 8):
            gather(0, c)
        work(BATCH)

        @pl.loop(1, whole)
        def _(step):
            for c in range(0, BATCH, 8):
                deposit(c)
                gather(step, c)
            fold(step - 1, BATCH)
            work(BATCH)

        for c in range(0, BATCH, 8):
            deposit(c)
        fold(whole - 1, BATCH)

    @pl.when((rest > 0) & (rest <= BATCH // 2))
    def _():
        for c in range(0, BATCH // 2, 8):
            gather(whole, c)
        work(BATCH // 2)
        for c in range(0, BATCH // 2, 8):
            deposit(c)
        fold(whole, BATCH // 2)


def return_kernel(ng, nt, acc_ref, recv_ref, send_ref, tile_s, tile_r, local_sem):
    g, t = lax.axis_index("grp"), lax.axis_index("tile")
    sources, rows, _ = send_ref.shape
    takes = g < ng - 1

    @pl.when(takes)
    def _():
        for k in range(1, nt):
            p = wrap(t + k, nt)
            say_in((home(ng, nt, p)[0], p))

    origins = [source(ng, nt, k) for k in range(sources)]
    remote = [(to_g != g) | (to_d != t) for to_g, to_d in origins]
    for d in range(sources):
        for r in range(0, rows // SLOTS, 2):
            pair = [
                acc_ref[pl.ds(d * SLOTS * PITCH + q, SLOTS, stride=PITCH), :]
                for q in (r, r + 1)
            ]
            send_ref[d, r * SLOTS : (r + 2) * SLOTS, :] = jnp.concatenate(pair, axis=0).astype(BF16)
    def slab(k):
        return pltpu.make_async_remote_copy(
            src_ref=send_ref.at[k], dst_ref=recv_ref.at[t], send_sem=tile_s.at[k],
            recv_sem=tile_r.at[t], device_id=origins[k], device_id_type=MESH,
        )

    pl.semaphore_wait(pltpu.get_barrier_semaphore(), sources - jnp.where(takes, 1, 0))
    for k in range(sources):

        @pl.when(remote[k])
        def _():
            slab(k).start()

    kept = pltpu.make_async_copy(send_ref.at[home(ng, nt, t)[1]], recv_ref.at[t], local_sem)

    @pl.when(takes)
    def _():
        kept.start()
        kept.wait()
        for k in range(1, nt):
            p = wrap(t + k, nt)
            pltpu.make_async_remote_copy(
                src_ref=send_ref.at[0], dst_ref=recv_ref.at[p], send_sem=tile_s.at[0],
                recv_sem=tile_r.at[p], device_id=(home(ng, nt, p)[0], p), device_id_type=MESH,
            ).wait_recv()

    @pl.when(jnp.logical_not(takes))
    def _():
        recv_ref[...] = jnp.zeros_like(recv_ref)

    for k in range(sources):

        @pl.when(remote[k])
        def _():
            slab(k).wait_send()


def place_kernel(ng, nt, nf, recv_ref, placer_ref, part_ref, out_hbm, buf, sem):
    rows, planes, width = part_ref.shape
    gas_side = lax.axis_index("grp") < ng - 1
    placer = placer_ref[...]
    copies = []
    for r in range(0, rows, 2):
        inc = jnp.concatenate([recv_ref[d, r * SLOTS : (r + 2) * SLOTS, :] for d in range(nt)], axis=0)
        placed = jnp.dot(placer, inc, preferred_element_type=F32)
        for h in range(2):
            q = r + h
            buf[q] = part_ref[q] + jnp.where(gas_side, placed[h * planes : (h + 1) * planes], 0.0)
            if (q + 1) % nf == 0:
                y = q // nf
                c = pltpu.make_async_copy(buf.at[pl.ds(y * nf, nf)], out_hbm.at[:, :, y, :], sem.at[y])
                c.start()
                copies.append(c)
    for c in copies:
        c.wait()


def local(
    flow_fields, turbulent_diffusivity, holder_unit, spray_volume_position, patch_pick_unreduced,
    droplet_motion, droplet_warmth, droplet_weightiness, droplet_multiplicity, living_spray_batches,
):
    ng, nt = lax.axis_size("grp"), lax.axis_size("tile")
    nf, planes, rows_y, width = flow_fields.shape
    rows = nf * rows_y
    dma = pltpu.SemaphoreType.DMA
    shape = jax.ShapeDtypeStruct
    blocks = spray_volume_position.shape[1]
    sources = nt * (SHARE - 1) // SHARE
    slots = sources * SLOTS
    prow = blocks // 128
    lists = blocks // BATCH + 8
    slab = (nt, rows * SLOTS, width)
    gas = (rows, planes, width)
    table, ints, part, placer, parcels = pl.pallas_call(
        functools.partial(gas_kernel, ng, nt, nf),
        out_shape=(
            shape(((slots + 1) * PITCH + 7, width), F32), shape((lists, 128), I32), shape(gas, F32),
            shape((2 * planes, nt * 2 * SLOTS), BF16), shape((blocks * (ROW + 1), 128), F32),
        ),
        in_specs=[SMEM] + [HBM] * 9, out_specs=(VMEM,) * 5,
        scratch_shapes=[
            pltpu.VMEM((blocks, 128), I32), pltpu.VMEM((3, blocks, 128), F32),
            pltpu.VMEM((blocks, 128), F32), pltpu.VMEM((blocks, 128), F32), pltpu.VMEM((blocks, 128), F32),
            pltpu.VMEM((1, planes), I32), pltpu.VMEM((prow, 128), I32),
            pltpu.VMEM((rows_y, planes, width), F32), pltpu.VMEM(gas, F32),
            pltpu.VMEM((1, 1, 128), I32), pltpu.VMEM((1, 128), I32), pltpu.VMEM((ng, nt, 1, 128), I32),
            pltpu.VMEM(slab, BF16), pltpu.VMEM((sources,) + slab[1:], BF16),
            pltpu.VMEM((2, nf, planes, width), BF16),
            pltpu.VMEM((nf, planes, width), BF16), pltpu.VMEM((nf, planes, width), BF16),
            pltpu.VMEM((rows, width), BF16), pltpu.VMEM((rows, width), BF16),
            pltpu.VMEM((rows, width), BF16), pltpu.VMEM((rows, width), BF16),
            dma((2,)), dma((rows_y,)), dma((rows_y,)), dma((5,)),
            dma((nt,)), dma((sources,)), dma((nt - 1,)), dma((nt - 1,)),
            dma((ng - 1,)), dma((ng - 1,)), dma((4,)), dma((4,)), dma((2,)),
        ],
        compiler_params=pltpu.CompilerParams(
            collective_id=0, has_side_effects=True, vmem_limit_bytes=24 << 20
        ),
        name="gas",
    )(living_spray_batches, *(pltpu.with_memory_space_constraint(a, pltpu.MemorySpace.HBM) for a in (
        holder_unit.reshape(1, planes), flow_fields, turbulent_diffusivity,
        patch_pick_unreduced.reshape(prow, 128), spray_volume_position[0],
        droplet_motion[0].transpose(1, 0, 2), droplet_warmth[0], droplet_weightiness[0],
        droplet_multiplicity[0],
    )))
    acc = pl.pallas_call(
        functools.partial(parcel_kernel, nf, rows_y),
        out_shape=shape(((slots + 1) * PITCH + 7, width), F32),
        in_specs=[VMEM] * 3, out_specs=VMEM,
        scratch_shapes=[
            pltpu.VMEM((24 * (BATCH + 1), width), F32),
            pltpu.VMEM((ROW * (BATCH + 1), width), F32),
            pltpu.VMEM((BATCH * PITCH, width), F32),
            pltpu.VMEM((BATCH, width), F32),
            pltpu.VMEM((BATCH * 24, width), F32),
            pltpu.SMEM((lists, 128), I32),
            dma,
        ],
        compiler_params=pltpu.CompilerParams(vmem_limit_bytes=24 << 20),
        name="parcels",
    )(ints, table, parcels)
    recv = pl.pallas_call(
        functools.partial(return_kernel, ng, nt),
        out_shape=shape(slab, BF16),
        in_specs=[VMEM], out_specs=VMEM,
        scratch_shapes=[
            pltpu.VMEM((sources,) + slab[1:], BF16), dma((sources,)), dma((nt,)), dma,
        ],
        compiler_params=pltpu.CompilerParams(
            collective_id=1, has_side_effects=True, vmem_limit_bytes=16 << 20
        ),
        name="return",
    )(acc)
    return pl.pallas_call(
        functools.partial(place_kernel, ng, nt, nf),
        out_shape=shape((nf, planes, rows_y, width), F32),
        in_specs=[VMEM] * 3, out_specs=HBM,
        scratch_shapes=[pltpu.VMEM(gas, F32), dma((rows_y,))],
        compiler_params=pltpu.CompilerParams(vmem_limit_bytes=12 << 20),
        name="place",
    )(recv, placer, part)


def solution(mesh):
    in_specs = (
        P(None, "tile", "grp", None),
        P("tile", "grp", None),
        P("grp", "tile", None),
        P("tile", None, None),
        P("tile", None),
        P("tile", None, None, None),
        P("tile", None, None),
        P("tile", None, None),
        P("tile", None, None),
        P("tile"),
    )
    out_specs = P(None, "tile", "grp", None)
    return jax.shard_map(local, mesh=mesh, in_specs=in_specs, out_specs=out_specs, check_vma=False)
```

```python
import functools

import jax
import jax.numpy as jnp
from jax import lax
from jax.experimental import pallas as pl
from jax.experimental.pallas import tpu as pltpu
from jax.sharding import PartitionSpec as P

MESH = pl.DeviceIdType.MESH
SLOTS = 8
BATCH = 64
HBM = pl.BlockSpec(memory_space=pltpu.MemorySpace.HBM)
VMEM = pl.BlockSpec(memory_space=pltpu.VMEM)
SMEM = pl.BlockSpec(memory_space=pltpu.SMEM)
F32, BF16, I32 = jnp.float32, jnp.bfloat16, jnp.int32


ROW = 8
PITCH = 25
SHARE = 4


def say_in(peer):
    pl.semaphore_signal(pltpu.get_barrier_semaphore(), inc=1, device_id=peer, device_id_type=MESH)


def wrap(x, n):
    return x - jnp.where(x >= n, n, 0)


def source(ng, nt, s):
    g, p = lax.axis_index("grp"), lax.axis_index("tile")
    spare = g == ng - 1
    e = jnp.where(spare, s // (ng - 1) * SHARE + SHARE - 1, s + s // (SHARE - 1))
    return jnp.where(spare, s % (ng - 1), g), wrap(e - p + nt, nt)


def home(ng, nt, p):
    g = lax.axis_index("grp")
    e = wrap(lax.axis_index("tile") + p, nt)
    quarter = lax.div(e, SHARE)
    shared = e - quarter * SHARE == SHARE - 1
    return jnp.where(shared, ng - 1, g), jnp.where(shared, quarter * (ng - 1) + g, e - quarter)


def send_to(src, dst, ss, rs, dev):
    c = pltpu.make_async_remote_copy(
        src_ref=src, dst_ref=dst, send_sem=ss, recv_sem=rs, device_id=dev, device_id_type=MESH
    )
    c.start()
    return c


def start_all(pairs, sems):
    loads = [pltpu.make_async_copy(a, b, sems.at[k]) for k, (a, b) in enumerate(pairs)]
    for c in loads:
        c.start()
    return loads


def block_list(ng, nt, owners, pick, live):
    p = lax.axis_index("tile")
    prow = pick.shape[0]
    sources = nt * (SHARE - 1) // SHARE
    slots = sources * SLOTS
    owned = jnp.where(owners == p, 1, 0)
    counts = jnp.sum(owned, axis=1, keepdims=True)
    which = lax.broadcasted_iota(I32, counts.shape, 0)
    counts = jnp.where(which < (ng - 1) * nt, counts, 0)
    total = jnp.maximum(jnp.sum(counts, axis=0, keepdims=True), 1)
    total_f = total.astype(F32)
    quotient = jnp.floor(pick.astype(F32) / total_f).astype(I32)
    left = pick - quotient * total
    left = jnp.where(left < 0, left + total, left)
    left = jnp.where(left >= total, left - total, left)
    slot = jnp.full(pick.shape, -1, I32)
    for k in range(sources):
        from_g, from_d = source(ng, nt, k)
        number = from_g * nt + from_d
        low = jnp.sum(jnp.where(which < number, counts, 0), axis=0, keepdims=True)
        size = jnp.sum(jnp.where(which == number, counts, 0), axis=0, keepdims=True)
        rank = left - low
        slot = jnp.where((rank >= 0) & (rank < size), rank + k * SLOTS, slot)
    row = lax.broadcasted_iota(I32, (prow, 128), 0)
    lane = lax.broadcasted_iota(I32, (prow, 128), 1)
    number = row * 128 + lane
    inside = (slot >= 0) & (number < live)
    flags = jnp.where(inside, 1, 0)
    square_a = lax.broadcasted_iota(I32, (128, 128), 0)
    square_b = lax.broadcasted_iota(I32, (128, 128), 1)
    before = jnp.where(square_a < square_b, 1.0, 0.0).astype(BF16)
    flags_low = flags.astype(F32).astype(BF16)
    place = jnp.dot(flags_low, before, preferred_element_type=F32).astype(I32)
    sums = jnp.sum(flags, axis=1, keepdims=True)
    start = jnp.zeros((1, 1), I32)
    listed = jnp.zeros((3 * prow, 128), F32)
    lane_f, slot_f = lane[0:1].astype(F32), slot.astype(F32)
    for i in range(prow):
        at = jnp.where(inside[i : i + 1], place[i : i + 1] + start, -1)
        goes = row == (at >> 7)
        parts = [
            jnp.where(goes, v, 0.0) for v in (slot_f[i : i + 1], jnp.full((1, 128), float(i), F32), lane_f)
        ]
        spot = jnp.where(square_a == (at & 127), 1.0, 0.0).astype(BF16)
        listed += lax.dot_general(
            jnp.concatenate(parts, axis=0).astype(BF16), spot, (((1,), (1,)), ((), ())),
            preferred_element_type=F32,
        )
        start = start + sums[i : i + 1]
    listed = listed.astype(I32)
    block = listed[prow : 2 * prow] * 128 + listed[2 * prow :]
    entry = ((listed[0:prow] * PITCH) << 16) + block * (ROW + 1)
    return jnp.where(number < start, entry, (slots * PITCH) << 16), start


def gas_kernel(
    ng, nt, nf, live_ref, holder_hbm, flow_hbm, nu_hbm, pick_hbm, pos_hbm, mot_hbm, warm_hbm, mass_hbm, mult_hbm,
    table_ref, ints_ref, part_ref, placer_ref, parcel_ref,
    pos_ref, mot_ref, warm_ref, mass_ref, mult_ref, holder_ref, pick_ref, nu_ref, gas_ref, own_ref, twice_ref, all_ref, send_ref, recv_ref,
    edge_ref, ylo_ref, yhi_ref, first_ref, last_ref, xlo_ref, xhi_ref,
    small_sem, gas_sem, nu_sem, bulk_sem, tile_s, tile_r, own_s, own_r, own2_s, own2_r, halo_s, halo_r, local_sem,
):
    g, t = lax.axis_index("grp"), lax.axis_index("tile")
    rows, planes, width = gas_ref.shape
    rows_y = rows // nf
    sources = recv_ref.shape[0]
    small = start_all([(holder_hbm, holder_ref), (pick_hbm, pick_ref)], small_sem)
    gas_loads = start_all(
        [(flow_hbm.at[:, :, y, :], gas_ref.at[pl.ds(y * nf, nf)]) for y in range(rows_y)], gas_sem
    )
    grp_peers = [(wrap(g + k, ng), t) for k in range(1, ng)]
    tile_peers = [(g, wrap(t + k, nt)) for k in range(1, nt)]
    for peer in grp_peers + tile_peers:
        say_in(peer)

    @pl.when(g == ng - 1)
    def _():
        for k in range(sources):
            say_in(source(ng, nt, k))

    targets = ng + nt - 2 + jnp.where(g < ng - 1, nt // SHARE, 0)
    pairs = [(pos_hbm, pos_ref), (warm_hbm, warm_ref), (mass_hbm, mass_ref), (mult_hbm, mult_ref)]
    pairs += [(mot_hbm, mot_ref)]
    bulk = start_all(pairs, bulk_sem)
    nu_loads = start_all([(nu_hbm.at[:, y, :], nu_ref.at[y]) for y in range(rows_y)], nu_sem)
    partners = [wrap(t + k, nt) for k in range(nt)]
    homes = [home(ng, nt, p) for p in partners]

    own_ref[0] = jnp.full((1, 128), -1, I32)
    twice_ref[...] = jnp.full((1, 128), -1, I32)
    for c in small:
        c.wait()
    own_ref[0, :, 0:planes] = holder_ref[...]
    own = own_ref[0]
    twice_ref[:, 0:planes] = holder_ref[...]
    twice_ref[:, planes : 2 * planes] = holder_ref[...]
    both = twice_ref[...]
    used = 2 * planes
    col = jnp.broadcast_to(both, (128, 128)).T[0:used]
    s = lax.broadcasted_iota(I32, (used, 128), 0)
    l = lax.broadcasted_iota(I32, (used, 128), 1)
    near = (col == both) & ((s >= planes) == (l >= planes))
    rank = jnp.sum(jnp.where(near & (s < l), 1, 0), axis=0, keepdims=True)
    rank_col = jnp.sum(jnp.where(near & (l < s), 1, 0), axis=1, keepdims=True)
    lanes = lax.broadcasted_iota(I32, (1, 128), 1)
    subs = lax.broadcasted_iota(I32, (used, 1), 0)
    goal = both * (2 * SLOTS) + rank + jnp.where(lanes >= planes, SLOTS, 0)
    goal_col = col[:, 0:1] * (2 * SLOTS) + rank_col + jnp.where(subs >= planes, SLOTS, 0)
    picker = jnp.where(
        goal[:, 0 : 2 * planes] == lax.broadcasted_iota(I32, (nt * 2 * SLOTS, 2 * planes), 0), 1.0, 0.0
    ).astype(BF16)
    placer_ref[...] = jnp.where(
        goal_col == lax.broadcasted_iota(I32, (2 * planes, nt * 2 * SLOTS), 1), 1.0, 0.0
    ).astype(BF16)
    for c in gas_loads:
        c.wait()
    for r in range(0, rows, 2):
        low = jnp.concatenate([gas_ref[r], gas_ref[r + 1]], axis=0).astype(BF16)
        got = jnp.dot(picker, low, preferred_element_type=F32).astype(BF16)
        for o in range(nt):
            send_ref[o, r * SLOTS : (r + 2) * SLOTS, :] = got[o * 2 * SLOTS : (o + 1) * 2 * SLOTS]

    pl.semaphore_wait(pltpu.get_barrier_semaphore(), targets)
    own_copies = [
        send_to(own_ref.at[0], all_ref.at[g, t], own_s.at[k], own_r.at[k], peer)
        for k, peer in enumerate(tile_peers)
    ]
    mine = pltpu.make_async_copy(own_ref.at[0], all_ref.at[g, t], local_sem.at[0])
    mine.start()
    gives = g < ng - 1

    def slab(k):
        p, (to_g, at) = partners[k], homes[k]
        return pltpu.make_async_remote_copy(
            src_ref=send_ref.at[p], dst_ref=recv_ref.at[at], send_sem=tile_s.at[k],
            recv_sem=tile_r.at[at], device_id=(to_g, p), device_id_type=MESH,
        )

    kept = pltpu.make_async_copy(send_ref.at[t], recv_ref.at[homes[0][1]], local_sem.at[1])

    @pl.when(gives)
    def _():
        for k in range(1, nt):
            slab(k).start()
        kept.start()

    mine.wait()
    for c in own_copies:
        c.wait_recv()
    own2_copies = [
        send_to(all_ref.at[g], all_ref.at[g], own2_s.at[k], own2_r.at[k], peer)
        for k, peer in enumerate(grp_peers)
    ]
    gas_side = jnp.where(g < ng - 1, 1.0, 0.0).astype(F32)
    edge_ref[0] = (gas_ref[rows - nf : rows] * gas_side).astype(BF16)
    edge_ref[1] = (gas_ref[0:nf] * gas_side).astype(BF16)
    first_ref[...] = gas_ref[:, 0, :].astype(BF16)
    last_ref[...] = gas_ref[:, planes - 1, :].astype(BF16)
    halos = [
        send_to(edge_ref.at[0], ylo_ref, halo_s.at[0], halo_r.at[0], grp_peers[0]),
        send_to(edge_ref.at[1], yhi_ref, halo_s.at[1], halo_r.at[1], grp_peers[-1]),
        send_to(last_ref, xlo_ref, halo_s.at[2], halo_r.at[2], tile_peers[0]),
        send_to(first_ref, xhi_ref, halo_s.at[3], halo_r.at[3], tile_peers[-1]),
    ]
    table_ref[...] = jnp.zeros_like(table_ref)
    for c in bulk:
        c.wait()

    @pl.loop(0, pos_ref.shape[0] // 8)
    def _(k):
        at = pl.ds(pl.multiple_of(k * 8, 8), 8)
        cell = pos_ref[at, :]
        values = [mot_ref[f, at, :] for f in range(3)] + [warm_ref[at, :], mass_ref[at, :], mult_ref[at, :]]
        values += [(cell & 127).astype(F32), (cell >> 7).astype(F32)]
        for f, v in enumerate(values):
            parcel_ref[pl.ds(k * 8 * (ROW + 1) + f, 8, stride=ROW + 1), :] = v

    for c in own2_copies:
        c.wait_recv()
    owners = jnp.concatenate([all_ref[k].reshape(nt, 128) for k in range(ng)], axis=0)
    entries, number = block_list(ng, nt, owners, pick_ref[...], live_ref[0])
    prow, spans = entries.shape[0], 128 // BATCH
    for k in range(spans):
        here = entries if k == 0 else pltpu.roll(entries, 128 - k * BATCH, 1)
        ints_ref[pl.ds(k, prow, stride=spans), :] = here
    ints_ref[prow * spans : prow * spans + 8, :] = jnp.broadcast_to(number, (8, 128))

    for c in nu_loads:
        c.wait()
    for c in halos:
        c.wait_recv()
    sub = lax.broadcasted_iota(I32, (planes, width), 0)
    lane = lax.broadcasted_iota(I32, (planes, width), 1)
    has_low = jnp.where(t > 0, 1.0, 0.0).astype(F32)
    has_high = jnp.where(t < nt - 1, 1.0, 0.0).astype(F32)
    x_low = xlo_ref[...].astype(F32) * has_low
    x_high = xhi_ref[...].astype(F32) * has_high
    for r in range(rows):
        mid = gas_ref[r]
        below = gas_ref[r - nf] if r >= nf else ylo_ref[r].astype(F32)
        above = gas_ref[r + nf] if r < rows - nf else yhi_ref[r - (rows - nf)].astype(F32)
        total = below + above
        total += jnp.where(sub == 0, x_low[r : r + 1], pltpu.roll(mid, 1, 0))
        total += jnp.where(sub == planes - 1, x_high[r : r + 1], pltpu.roll(mid, planes - 1, 0))
        total += jnp.where(lane == 0, 0.0, pltpu.roll(mid, 1, 1))
        total += jnp.where(lane == width - 1, 0.0, pltpu.roll(mid, width - 1, 1))
        part_ref[r] = (mid + 0.5 * nu_ref[r // nf] * (total - 6.0 * mid)) * gas_side

    def unpack(d):
        for r in range(0, rows, 2):
            both = recv_ref[d, r * SLOTS : (r + 2) * SLOTS, :].astype(F32)
            for h in range(2):
                table_ref[pl.ds(d * SLOTS * PITCH + r + h, SLOTS, stride=PITCH), :] = both[h * SLOTS : (h + 1) * SLOTS]

    @pl.when(gives)
    def _():
        kept.wait()

    for k in range(sources):
        from_g, from_d = source(ng, nt, k)

        @pl.when((from_g != g) | (from_d != t))
        def _():
            pltpu.make_async_remote_copy(
                src_ref=send_ref.at[0], dst_ref=recv_ref.at[k], send_sem=tile_s.at[0],
                recv_sem=tile_r.at[k], device_id=(from_g, from_d), device_id_type=MESH,
            ).wait_recv()

        unpack(k)

    @pl.when(gives)
    def _():
        for k in range(1, nt):
            slab(k).wait_send()
    for c in own_copies + own2_copies + halos:
        c.wait_send()


def sources_of(field, own):
    v0, v1, v2, warm, mass, mult = own
    r0, r1, r2 = field[0] - v0, field[1] - v1, field[2] - v2
    speed_sq = r0 * r0 + r1 * r1 + r2 * r2
    inv_surface = jnp.exp(jnp.log(mass) * (-2.0 / 3.0))
    inverse_tau = 0.8 * (1.0 + 0.15 * jnp.exp(0.3435 * jnp.log(1.0 + speed_sq))) * inv_surface
    relax = 1.0 - jnp.exp(-0.5 * inverse_tau)
    heating = 1.0 / (1.0 + jnp.exp(field[4] - field[3]))
    remain = jnp.exp(-0.3 * heating * inv_surface)
    new_mass = mass * remain
    warming = 1.0 - jnp.exp(-0.25 * inverse_tau)
    new_warm = warm + warming * (field[3] - warm) - 0.5 * (1.0 - remain)
    outs = [mass * v - new_mass * (v + relax * r) for v, r in ((v0, r0), (v1, r1), (v2, r2))]
    outs += [mass * warm - new_mass * new_warm, mass - new_mass]
    return [mult * o for o in outs]


def parcel_kernel(nf, rows_y, ints_ref, table, parcels, acc, seen, par, src, cells, add, smem, sem):
    to_smem = pltpu.make_async_copy(ints_ref, smem, sem)
    to_smem.start()
    span = BATCH + 1
    acc[...] = jnp.zeros_like(acc)
    src[...] = jnp.zeros_like(src)
    to_smem.wait()

    n = smem[smem.shape[0] - 8, 0]
    sub = lax.broadcasted_iota(I32, (128, 128), 0).astype(F32).astype(BF16)
    yes, no = jnp.ones((128, 128), BF16), jnp.zeros((128, 128), BF16)
    spare = jnp.zeros((8, 128), F32)
    zero = jnp.zeros((32, 128), BF16)

    def gather(step, c):
        for i in range(c, c + 8):
            v = smem[step, i]
            b, base = v & 65535, v >> 16
            z = jnp.broadcast_to(parcels[pl.ds(b + 6, 1), :], (8, 128)).astype(I32)
            for k in range(3):
                seen[pl.ds(k * 8 * span + i, 8, stride=span), :] = jnp.take_along_axis(
                    table[pl.ds(base + k * 8, 8), :], z, axis=1, mode="promise_in_bounds",
                    wrap_negative_indices=False,
                )
            par[pl.ds(i, 8, stride=span), :] = parcels[pl.ds(b, 8), :]

    def work(size):
        for c in range(0, size, 8):
            own = [par[f * span + c : f * span + c + 8, :] for f in range(ROW)]
            y = own[7]
            cells[c : c + 8, :] = own[6]
            gas = []
            for f in range(nf):
                at = [seen[(k * nf + f) * span + c : (k * nf + f) * span + c + 8, :] for k in range(rows_y)]
                value = at[0]
                for k in range(1, rows_y):
                    value = jnp.where(y < k, value, at[k])
                gas.append(value)
            outs = sources_of(gas, own[0:6])
            for k in range(rows_y):
                here = y == k
                for f in range(nf):
                    src[pl.ds(c * PITCH + k * nf + f, 8, stride=PITCH), :] = jnp.where(here, outs[f], 0.0)

    def deposit(c):
        for j in range(c, c + 8, 2):
            left, hot = [], []
            for i in (j, j + 1):
                z = jnp.broadcast_to(cells[i : i + 1, :], (16, 128)).astype(BF16)
                hot.append(jnp.where(sub == jnp.concatenate([z] * 8, axis=0), yes, no))
                mine = jnp.concatenate([src[i * PITCH : i * PITCH + 24, :], spare], axis=0).astype(BF16)
                left.append(jnp.concatenate([mine, zero] if i == j else [zero, mine], axis=1))
            added = lax.dot_general(
                jnp.concatenate(left, axis=0), jnp.concatenate(hot, axis=1), (((1,), (1,)), ((), ())),
                preferred_element_type=F32,
            )
            for i in (j, j + 1):
                add[i * 24 : (i + 1) * 24, :] = added[(i - j) * 32 : (i - j) * 32 + 24]

    def fold(step, size):
        for i in range(size):
            at = pl.ds(smem[step, i] >> 16, 24)
            acc[at, :] = acc[at, :] + add[i * 24 : (i + 1) * 24, :]

    rest = lax.rem(n, BATCH)
    whole = n // BATCH + jnp.where(rest > BATCH // 2, 1, 0)

    @pl.when(whole > 0)
    def _():
        for c in range(0, BATCH, 8):
            gather(0, c)
        work(BATCH)

        @pl.loop(1, whole)
        def _(step):
            for c in range(0, BATCH, 8):
                deposit(c)
                gather(step, c)
            fold(step - 1, BATCH)
            work(BATCH)

        for c in range(0, BATCH, 8):
            deposit(c)
        fold(whole - 1, BATCH)

    @pl.when((rest > 0) & (rest <= BATCH // 2))
    def _():
        for c in range(0, BATCH // 2, 8):
            gather(whole, c)
        work(BATCH // 2)
        for c in range(0, BATCH // 2, 8):
            deposit(c)
        fold(whole, BATCH // 2)


def return_kernel(ng, nt, acc_ref, recv_ref, send_ref, tile_s, tile_r, local_sem):
    g, t = lax.axis_index("grp"), lax.axis_index("tile")
    sources, rows, _ = send_ref.shape
    takes = g < ng - 1

    @pl.when(takes)
    def _():
        for k in range(1, nt):
            p = wrap(t + k, nt)
            say_in((home(ng, nt, p)[0], p))

    origins = [source(ng, nt, k) for k in range(sources)]
    remote = [(to_g != g) | (to_d != t) for to_g, to_d in origins]
    for d in range(sources):
        for r in range(0, rows // SLOTS, 2):
            pair = [
                acc_ref[pl.ds(d * SLOTS * PITCH + q, SLOTS, stride=PITCH), :]
                for q in (r, r + 1)
            ]
            send_ref[d, r * SLOTS : (r + 2) * SLOTS, :] = jnp.concatenate(pair, axis=0).astype(BF16)
    def slab(k):
        return pltpu.make_async_remote_copy(
            src_ref=send_ref.at[k], dst_ref=recv_ref.at[t], send_sem=tile_s.at[k],
            recv_sem=tile_r.at[t], device_id=origins[k], device_id_type=MESH,
        )

    pl.semaphore_wait(pltpu.get_barrier_semaphore(), sources - jnp.where(takes, 1, 0))
    for k in range(sources):

        @pl.when(remote[k])
        def _():
            slab(k).start()

    kept = pltpu.make_async_copy(send_ref.at[home(ng, nt, t)[1]], recv_ref.at[t], local_sem)

    @pl.when(takes)
    def _():
        kept.start()
        kept.wait()
        for k in range(1, nt):
            p = wrap(t + k, nt)
            pltpu.make_async_remote_copy(
                src_ref=send_ref.at[0], dst_ref=recv_ref.at[p], send_sem=tile_s.at[0],
                recv_sem=tile_r.at[p], device_id=(home(ng, nt, p)[0], p), device_id_type=MESH,
            ).wait_recv()

    @pl.when(jnp.logical_not(takes))
    def _():
        recv_ref[...] = jnp.zeros_like(recv_ref)

    for k in range(sources):

        @pl.when(remote[k])
        def _():
            slab(k).wait_send()


def place_kernel(ng, nt, nf, recv_ref, placer_ref, part_ref, out_hbm, buf, sem):
    rows, planes, width = part_ref.shape
    gas_side = lax.axis_index("grp") < ng - 1
    placer = placer_ref[...]
    copies = []
    for r in range(0, rows, 2):
        inc = jnp.concatenate([recv_ref[d, r * SLOTS : (r + 2) * SLOTS, :] for d in range(nt)], axis=0)
        placed = jnp.dot(placer, inc, preferred_element_type=F32)
        for h in range(2):
            q = r + h
            buf[q] = part_ref[q] + jnp.where(gas_side, placed[h * planes : (h + 1) * planes], 0.0)
            if (q + 1) % nf == 0:
                y = q // nf
                c = pltpu.make_async_copy(buf.at[pl.ds(y * nf, nf)], out_hbm.at[:, :, y, :], sem.at[y])
                c.start()
                copies.append(c)
    for c in copies:
        c.wait()


def local(
    flow_fields, turbulent_diffusivity, holder_unit, spray_volume_position, patch_pick_unreduced,
    droplet_motion, droplet_warmth, droplet_weightiness, droplet_multiplicity, living_spray_batches,
):
    ng, nt = lax.axis_size("grp"), lax.axis_size("tile")
    nf, planes, rows_y, width = flow_fields.shape
    rows = nf * rows_y
    dma = pltpu.SemaphoreType.DMA
    shape = jax.ShapeDtypeStruct
    blocks = spray_volume_position.shape[1]
    sources = nt * (SHARE - 1) // SHARE
    slots = sources * SLOTS
    prow = blocks // 128
    lists = blocks // BATCH + 8
    slab = (nt, rows * SLOTS, width)
    gas = (rows, planes, width)
    table, ints, part, placer, parcels = pl.pallas_call(
        functools.partial(gas_kernel, ng, nt, nf),
        out_shape=(
            shape(((slots + 1) * PITCH + 7, width), F32), shape((lists, 128), I32), shape(gas, F32),
            shape((2 * planes, nt * 2 * SLOTS), BF16), shape((blocks * (ROW + 1), 128), F32),
        ),
        in_specs=[SMEM] + [HBM] * 9, out_specs=(VMEM,) * 5,
        scratch_shapes=[
            pltpu.VMEM((blocks, 128), I32), pltpu.VMEM((3, blocks, 128), F32),
            pltpu.VMEM((blocks, 128), F32), pltpu.VMEM((blocks, 128), F32), pltpu.VMEM((blocks, 128), F32),
            pltpu.VMEM((1, planes), I32), pltpu.VMEM((prow, 128), I32),
            pltpu.VMEM((rows_y, planes, width), F32), pltpu.VMEM(gas, F32),
            pltpu.VMEM((1, 1, 128), I32), pltpu.VMEM((1, 128), I32), pltpu.VMEM((ng, nt, 1, 128), I32),
            pltpu.VMEM(slab, BF16), pltpu.VMEM((sources,) + slab[1:], BF16),
            pltpu.VMEM((2, nf, planes, width), BF16),
            pltpu.VMEM((nf, planes, width), BF16), pltpu.VMEM((nf, planes, width), BF16),
            pltpu.VMEM((rows, width), BF16), pltpu.VMEM((rows, width), BF16),
            pltpu.VMEM((rows, width), BF16), pltpu.VMEM((rows, width), BF16),
            dma((2,)), dma((rows_y,)), dma((rows_y,)), dma((5,)),
            dma((nt,)), dma((sources,)), dma((nt - 1,)), dma((nt - 1,)),
            dma((ng - 1,)), dma((ng - 1,)), dma((4,)), dma((4,)), dma((2,)),
        ],
        compiler_params=pltpu.CompilerParams(
            collective_id=0, has_side_effects=True, vmem_limit_bytes=24 << 20
        ),
        name="gas",
    )(living_spray_batches, *(pltpu.with_memory_space_constraint(a, pltpu.MemorySpace.HBM) for a in (
        holder_unit.reshape(1, planes), flow_fields, turbulent_diffusivity,
        patch_pick_unreduced.reshape(prow, 128), spray_volume_position[0],
        droplet_motion[0].transpose(1, 0, 2), droplet_warmth[0], droplet_weightiness[0],
        droplet_multiplicity[0],
    )))
    acc = pl.pallas_call(
        functools.partial(parcel_kernel, nf, rows_y),
        out_shape=shape(((slots + 1) * PITCH + 7, width), F32),
        in_specs=[VMEM] * 3, out_specs=VMEM,
        scratch_shapes=[
            pltpu.VMEM((24 * (BATCH + 1), width), F32),
            pltpu.VMEM((ROW * (BATCH + 1), width), F32),
            pltpu.VMEM((BATCH * PITCH, width), F32),
            pltpu.VMEM((BATCH, width), F32),
            pltpu.VMEM((BATCH * 24, width), F32),
            pltpu.SMEM((lists, 128), I32),
            dma,
        ],
        compiler_params=pltpu.CompilerParams(vmem_limit_bytes=24 << 20),
        name="parcels",
    )(ints, table, parcels)
    recv = pl.pallas_call(
        functools.partial(return_kernel, ng, nt),
        out_shape=shape(slab, BF16),
        in_specs=[VMEM], out_specs=VMEM,
        scratch_shapes=[
            pltpu.VMEM((sources,) + slab[1:], BF16), dma((sources,)), dma((nt,)), dma,
        ],
        compiler_params=pltpu.CompilerParams(
            collective_id=1, has_side_effects=True, vmem_limit_bytes=16 << 20
        ),
        name="return",
    )(acc)
    return pl.pallas_call(
        functools.partial(place_kernel, ng, nt, nf),
        out_shape=shape((nf, planes, rows_y, width), F32),
        in_specs=[VMEM] * 3, out_specs=HBM,
        scratch_shapes=[pltpu.VMEM(gas, F32), dma((rows_y,))],
        compiler_params=pltpu.CompilerParams(vmem_limit_bytes=12 << 20),
        name="place",
    )(recv, placer, part)


def solution(mesh):
    in_specs = (
        P(None, "tile", "grp", None),
        P("tile", "grp", None),
        P("grp", "tile", None),
        P("tile", None, None),
        P("tile", None),
        P("tile", None, None, None),
        P("tile", None, None),
        P("tile", None, None),
        P("tile", None, None),
        P("tile"),
    )
    out_specs = P(None, "tile", "grp", None)
    return jax.shard_map(local, mesh=mesh, in_specs=in_specs, out_specs=out_specs, check_vma=False)
```
